32 devices in a mesh: dp: 8 (over y, x, core), tensor: 4 (over z).
Axes of the slice: x: 2, y: 2, z: 4, core: 2. Of those that a mesh axis runs over, the one named last changes fastest.
Arguments:
- tokens: bfloat16 [8192, 2048], P(('dp', 'tensor')), may hold values from -6 to 6
- seq_start: int32 [8192], P('dp'), may hold values from 0 to 8191, as said below
- proj_weight: bfloat16 [2048, 3, 2048], P('dp', None, 'tensor'), may hold values from -0.125 to 0.125
- proj_bias: bfloat16 [3, 8, 256], P(None, 'tensor', 'dp'), may hold values from -3 to 3
- out_weight: bfloat16 [2048, 2048], P('tensor', 'dp'), may hold values from -1.5 to 1.5
- up_weight: bfloat16 [2048, 8192], P('dp', 'tensor'), may hold values from -0.125 to 0.125
- up_bias: bfloat16 [4, 2048], P('tensor', 'dp'), may hold values from -3 to 3
- down_weight: bfloat16 [8192, 2048], P('tensor', 'dp'), may hold values from -0.0625 to 0.0625
- norm_gains: bfloat16 [2, 2048], P(None, ('dp', 'tensor')), may hold values from 0.099609375 to 1.8984375
- biases: bfloat16 [4, 2048], P(None, ('dp', 'tensor')), may hold values from -3 to 3
- cotangent: bfloat16 [8192, 2048], P(('dp', 'tensor')), may hold values from -6 to 6
Outputs:
- output: bfloat16 [8192, 2048], P(('dp', 'tensor'))
- input_grad: float32 [8192, 2048], P(('dp', 'tensor'))
- proj_grad: float32 [2048, 3, 2048], P('dp', None, 'tensor')
- proj_bias_grad: float32 [3, 8, 256], P(None, 'tensor', 'dp')
- out_grad: float32 [2048, 2048], P('tensor', 'dp')
- up_grad: float32 [2048, 8192], P('dp', 'tensor')
- up_bias_grad: float32 [4, 2048], P('tensor', 'dp')
- down_grad: float32 [8192, 2048], P('tensor', 'dp')
- gains_grad: float32 [2, 2048], P(None, ('dp', 'tensor'))
- biases_grad: float32 [4, 2048], P(None, ('dp', 'tensor'))
The draws below stay inside these ranges and needn't reach their ends.
Inputs may be any that keep to these rules, and one draw needn't show every extreme that they name: seq_start never falls along the tokens, is at most the token's own index, and every sequence lies inside one aligned block of 1024 tokens (the tokens of one index of dp); some block other than the last holds a single sequence of 1024 tokens, the others hold sequences of uneven lengths, and the last token begins a sequence of its own.
All inputs are finite; a program needn't handle non-finite values.
Results may differ from the reference program's by a relative error of at most 0.012.
Values may be sent and summed in bfloat16 or wider, within the bound.
No kernel may reach another device: no remote copies, remote signals or barrier semaphores. Data moves between devices by JAX's collectives and lax.ppermute only.
A program may use at most 192 MiB of HBM per device.

```python
import jax
import jax.numpy as jnp
from jax import lax

D = 2048
HEADS = 8
HD = 256
ROT = 64
FF = 8192
GROUP_ROWS = 1024
TOKENS = 8192
N_TENSOR = 4


def draw_seq_start(key, part):
    cut_key, whole_key = jax.random.split(key)
    token_index = jnp.arange(TOKENS, dtype=jnp.int32)
    cutting = jax.random.randint(cut_key, (TOKENS,), 0, GROUP_ROWS) < 4
    single = jax.random.randint(whole_key, (), 0, TOKENS // GROUP_ROWS - 1)
    cutting = jnp.logical_and(cutting, token_index // GROUP_ROWS != single)
    cutting = jnp.logical_or(cutting, token_index % GROUP_ROWS == 0)
    cutting = jnp.logical_or(cutting, token_index == TOKENS - 1)
    return lax.cummax(jnp.where(cutting, token_index, 0), axis=0)


def block_scale(stream_key, extent, cuts, least, top_value):
    gain = 1.0
    for position, shards_of in cuts:
        draws = jax.random.uniform(jax.random.fold_in(jax.random.fold_in(stream_key, 6), position), (shards_of,), jnp.float32, least / len(cuts), top_value / len(cuts))
        gain = gain * jnp.repeat(jnp.exp(draws), extent[position] // shards_of).reshape((-1,) + (1,) * (len(extent) - 1 - position))
    return gain


def centred(key, shape, scale, reach, cuts=(), kind=jnp.bfloat16):
    entries = jax.random.normal(key, shape, jnp.float32) * scale
    if len(cuts) > 0:
        entries = block_scale(key, shape, cuts, -0.22, 0.18) * entries
    return jnp.clip(entries, min=-reach, max=reach).astype(kind)


def setup_inputs(seed: int = 0) -> dict:
    arg_keys = jax.random.split(jax.random.key(seed), 12)
    return {
        "tokens": centred(arg_keys[0], (TOKENS, D), 1.0, 6.0, ((0, 32),)),
        "seq_start": draw_seq_start(jax.random.fold_in(arg_keys[11], 71), 0),
        "proj_weight": centred(arg_keys[2], (D, 3, D), D ** -0.5, 0.125, ((0, 8), (2, 4))),
        "proj_bias": centred(arg_keys[3], (3, HEADS, HD), 0.5, 3.0, ((1, 4), (2, 8))),
        "out_weight": centred(arg_keys[4], (D, D), 16 ** -0.5, 1.5, ((0, 4), (1, 8))),
        "up_weight": centred(arg_keys[5], (D, FF), D ** -0.5, 0.125, ((0, 8), (1, 4))),
        "up_bias": centred(arg_keys[6], (N_TENSOR, FF // N_TENSOR), 0.5, 3.0, ((0, 4), (1, 8))),
        "down_weight": centred(arg_keys[7], (FF, D), FF ** -0.5, 0.0625, ((0, 4), (1, 8))),
        "norm_gains": jnp.clip(1.0 + 0.18 * jax.random.normal(arg_keys[8], (2, D), jnp.float32), 0.099609375, 1.8984375).astype(jnp.bfloat16),
        "biases": centred(arg_keys[9], (4, D), 0.5, 3.0, ((1, 32),)),
        "cotangent": centred(arg_keys[10], (TOKENS, D), 1.0, 6.0, ((0, 32),)),
    }


EPSILON = 1e-05
ROTARY_BASE = 10000.0
PRECISE = lax.Precision.HIGHEST

@jax.custom_vjp
def low(v):
    return lax.optimization_barrier(v.astype(jnp.bfloat16)).astype(jnp.float32)

@jax.custom_vjp
def low_back(v):
    return v

def low_keep(v):
    return (low(v), None)

def low_pass(kept, grad):
    return (grad,)

def back_keep(v):
    return (v, None)

def back_low(kept, grad):
    return (low(grad),)
low.defvjp(low_keep, low_pass)
low_back.defvjp(back_keep, back_low)

def layer_norm(values, gain_row, shift_row):
    centered = values - lax.optimization_barrier(jnp.mean(values, axis=-1, keepdims=True))
    spread = lax.optimization_barrier(jnp.mean(centered * centered, axis=-1, keepdims=True))
    return centered * lax.rsqrt(spread + EPSILON) * gain_row + shift_row

def rotate(values, positions, turn_sign):
    half_rot = ROT // 2
    frequency = ROTARY_BASE ** (-(jnp.arange(half_rot, dtype=jnp.float32) * 2.0) / ROT)
    angles = positions.astype(jnp.float32)[:, None] * frequency[None, :]
    cosine = jnp.cos(angles)[:, None, :]
    sine_term = turn_sign * jnp.sin(angles)[:, None, :]
    first_half = values[..., :half_rot]
    second_half = values[..., half_rot:ROT]
    return jnp.concatenate([first_half * cosine - second_half * sine_term, second_half * cosine + first_half * sine_term, values[..., ROT:]], axis=-1)

def attend(queries, key_rows, value_rows, starts, block_rows):
    row_count = queries.shape[0]
    score_scale = HD ** (-0.5)
    key_index = jnp.arange(row_count, dtype=jnp.int32)

    @jax.checkpoint
    def one_block(block_start):
        query_block = lax.dynamic_slice_in_dim(queries, block_start, block_rows, 0)
        query_begin = lax.dynamic_slice_in_dim(starts, block_start, block_rows, 0)
        query_index = block_start + jnp.arange(block_rows, dtype=jnp.int32)
        scores = low_back(jnp.einsum('qhe,khe->hqk', query_block, key_rows, precision=PRECISE) * score_scale)
        allowed = (query_begin[:, None] == starts[None, :]) & (key_index[None, :] <= query_index[:, None])
        scores = jnp.where(allowed[None], scores, -1e+30)
        row_max = lax.optimization_barrier(jnp.max(scores, axis=-1, keepdims=True))
        powers = jnp.exp(scores - row_max)
        row_total = lax.optimization_barrier(jnp.sum(powers, axis=-1, keepdims=True))
        weights = low(powers / row_total)
        return jnp.einsum('hqk,khe->qhe', weights, value_rows, precision=PRECISE)
    block_starts = jnp.arange(row_count // block_rows, dtype=jnp.int32) * block_rows
    attended = lax.map(one_block, block_starts)
    return attended.reshape(row_count, HEADS, HD)

def group_forward(group_in, starts, base, proj_weight, proj_bias, out_weight, up_weight, up_bias, down_weight, norm_gains, biases):
    row_count = group_in.shape[0]
    block_rows = min(512, row_count)
    first_norm = low(layer_norm(group_in, norm_gains[0], biases[0]))
    second_norm = low(layer_norm(group_in, norm_gains[1], biases[1]))
    projected = low_back(jnp.einsum('nd,dch->nch', first_norm, proj_weight, precision=PRECISE) + proj_bias.reshape(3, D))
    positions = base + jnp.arange(row_count, dtype=jnp.int32) - starts
    queries = low(rotate(projected[:, 0].reshape(row_count, HEADS, HD), positions, 1.0))
    key_rows = low(rotate(projected[:, 1].reshape(row_count, HEADS, HD), positions, 1.0))
    value_rows = low(projected[:, 2].reshape(row_count, HEADS, HD))
    attended = low(low_back(attend(queries, key_rows, value_rows, starts, block_rows))).reshape(row_count, D)
    attn_branch = jnp.dot(attended, out_weight, precision=PRECISE) + biases[2]
    hidden = low_back(jnp.dot(second_norm, up_weight, precision=PRECISE) + up_bias.reshape(FF))
    activated = low(jax.nn.gelu(hidden, approximate=False))
    mlp_branch = jnp.dot(activated, down_weight, precision=PRECISE) + biases[3]
    return group_in + attn_branch + mlp_branch

def reference(tokens, seq_start, proj_weight, proj_bias, out_weight, up_weight, up_bias, down_weight, norm_gains, biases, cotangent):
    group_count = TOKENS // GROUP_ROWS
    params = tuple((p.astype(jnp.float32) for p in (proj_weight, proj_bias, out_weight, up_weight, up_bias, down_weight, norm_gains, biases)))
    tokens_f = tokens.astype(jnp.float32)

    def forward(inputs_f, *weights):

        def step(state, pieces):
            group_in, starts, base = pieces
            return (state, group_forward(group_in, starts, base, *weights))
        bases = jnp.arange(group_count, dtype=jnp.int32) * GROUP_ROWS
        _, result = lax.scan(step, jnp.zeros((), jnp.float32), (inputs_f.reshape(group_count, GROUP_ROWS, D), seq_start.reshape(group_count, GROUP_ROWS), bases))
        return result.reshape(TOKENS, D)
    output, pullback = jax.vjp(forward, tokens_f, *params)
    grads = pullback(cotangent.astype(jnp.float32))
    return (output.astype(jnp.bfloat16), grads[0], grads[1], grads[2], grads[3], grads[4], grads[5], grads[6], grads[7], grads[8])
```

```python
import jax
import jax.numpy as jnp
from jax import lax
from jax.sharding import PartitionSpec as P

ROT = 64
EPSILON = 1e-05
ROTARY_BASE = 10000.0
F32 = jnp.float32
BF16 = jnp.bfloat16


def xor_shift(values, axis, bit):
    size = lax.axis_size(axis)
    return lax.ppermute(values, axis, [(i, i ^ bit) for i in range(size)])


def is_power(n):
    return n & (n - 1) == 0


def butterfly(values, axis):
    size = lax.axis_size(axis)
    if not is_power(size):
        return lax.psum(values, axis)
    bit = 1
    while bit < size:
        values = values + xor_shift(values, axis, bit)
        bit *= 2
    return values


def dp_gather(shard):
    size = lax.axis_size("dp")
    if size != 8:
        return lax.all_gather(shard, "dp", axis=0, tiled=True)
    me = lax.axis_index("dp")
    rows = shard.shape[0]
    half = rows // 2
    from_x = xor_shift(shard, "dp", 2)
    from_y = xor_shift(shard, "dp", 4)
    far_a = xor_shift(from_x[:half], "dp", 4)
    far_b = xor_shift(from_y[half:], "dp", 2)
    mine = [(0, 0, shard), (2, 0, from_x), (4, 0, from_y), (6, 0, far_a), (6, half, far_b)]
    pieces = mine + [(p ^ 1, off, xor_shift(v, "dp", 1)) for p, off, v in mine]
    whole = jnp.zeros((size * rows,) + shard.shape[1:], shard.dtype)
    for p, off, v in pieces:
        start = (me ^ p) * rows + off
        whole = lax.dynamic_update_slice_in_dim(whole, v, start, 0)
    return whole


def dp_scatter(terms):
    size = lax.axis_size("dp")
    if size != 8:
        return lax.psum_scatter(terms, "dp", scatter_dimension=0, tiled=True).astype(F32)
    me = lax.axis_index("dp")
    core = me % 2
    chip = me // 2
    rows = terms.shape[0] // size
    half = rows // 2
    blocks = terms.reshape((4, 2, rows) + terms.shape[1:])
    away = lax.dynamic_index_in_dim(blocks, 1 - core, 1, keepdims=False)
    came = xor_shift(away, "dp", 1)

    def block(p):
        at = chip ^ p
        kept = lax.dynamic_index_in_dim(blocks, at, 0, keepdims=False)
        kept = lax.dynamic_index_in_dim(kept, core, 0, keepdims=False)
        return kept.astype(F32) + lax.dynamic_index_in_dim(came, at, 0, keepdims=False).astype(F32)

    far = block(3).astype(BF16)
    to_x = block(1)
    to_y = block(2)
    far_a = xor_shift(far[:half], "dp", 4)
    far_b = xor_shift(far[half:], "dp", 2)
    x_b = xor_shift(to_x[half:].astype(BF16), "dp", 2)
    y_a = xor_shift(to_y[:half].astype(BF16), "dp", 4)
    x_a = xor_shift((to_x[:half] + far_a.astype(F32)).astype(BF16), "dp", 2)
    y_b = xor_shift((to_y[half:] + far_b.astype(F32)).astype(BF16), "dp", 4)
    total = block(0)
    top = total[:half] + x_a.astype(F32) + y_a.astype(F32)
    low = total[half:] + x_b.astype(F32) + y_b.astype(F32)
    return jnp.concatenate([top, low], axis=0)


def standardize(values):
    values = values.astype(F32)
    centered = values - jnp.mean(values, axis=-1, keepdims=True)
    spread = jnp.mean(centered * centered, axis=-1, keepdims=True)
    scale = lax.rsqrt(spread + EPSILON)
    return centered * scale, scale


def rotate(values, positions, turn_sign):
    half_rot = ROT // 2
    frequency = ROTARY_BASE ** (-(jnp.arange(half_rot, dtype=F32) * 2.0) / ROT)
    angles = positions.astype(F32)[:, None] * frequency[None, :]
    cosine = jnp.cos(angles)[:, None, :]
    sine_term = turn_sign * jnp.sin(angles)[:, None, :]
    first_half = values[..., :half_rot]
    second_half = values[..., half_rot:ROT]
    return jnp.concatenate(
        [
            first_half * cosine - second_half * sine_term,
            second_half * cosine + first_half * sine_term,
            values[..., ROT:],
        ],
        axis=-1,
    )


def masked_scores(query_block, key_rows, starts, block_start, block_rows):
    row_count = key_rows.shape[0]
    score_scale = key_rows.shape[-1] ** (-0.5)
    key_index = jnp.arange(row_count, dtype=jnp.int32)
    query_begin = lax.dynamic_slice_in_dim(starts, block_start, block_rows, 0)
    query_index = block_start + jnp.arange(block_rows, dtype=jnp.int32)
    scores = (
        jnp.einsum("qhe,khe->hqk", query_block, key_rows, preferred_element_type=F32)
        * score_scale
    )
    allowed = (query_begin[:, None] == starts[None, :]) & (
        key_index[None, :] <= query_index[:, None]
    )
    return jnp.where(allowed[None], scores, -1e30)


def attention_forward(queries, key_rows, value_rows, starts, block_rows):
    row_count = queries.shape[0]

    def one_block(block_start):
        query_block = lax.dynamic_slice_in_dim(queries, block_start, block_rows, 0)
        scores = masked_scores(query_block, key_rows, starts, block_start, block_rows)
        row_max = jnp.max(scores, axis=-1, keepdims=True)
        powers = jnp.exp(scores - row_max)
        row_total = jnp.sum(powers, axis=-1, keepdims=True)
        weights = (powers / row_total).astype(BF16)
        attended = jnp.einsum("hqk,khe->qhe", weights, value_rows, preferred_element_type=F32)
        return (attended, (row_max + jnp.log(row_total))[..., 0])

    block_starts = jnp.arange(row_count // block_rows, dtype=jnp.int32) * block_rows
    attended, log_total = lax.map(one_block, block_starts)
    return (attended.reshape(queries.shape), log_total)


def attention_backward(queries, key_rows, value_rows, starts, log_total, grad_attended, block_rows):
    row_count = queries.shape[0]
    score_scale = queries.shape[-1] ** (-0.5)

    def one_block(accumulated, pieces):
        block_start, block_total = pieces
        grad_keys, grad_values = accumulated
        query_block = lax.dynamic_slice_in_dim(queries, block_start, block_rows, 0)
        grad_block = lax.dynamic_slice_in_dim(grad_attended, block_start, block_rows, 0)
        scores = masked_scores(query_block, key_rows, starts, block_start, block_rows)
        probs = jnp.exp(scores - block_total[..., None])
        grad_values = grad_values + jnp.einsum(
            "hqk,qhe->khe", probs.astype(BF16), grad_block, preferred_element_type=F32
        )
        grad_probs = jnp.einsum("qhe,khe->hqk", grad_block, value_rows, preferred_element_type=F32)
        inner_sum = jnp.sum(probs * grad_probs, axis=-1, keepdims=True)
        grad_scores = (probs * (grad_probs - inner_sum)).astype(BF16)
        grad_query = (
            jnp.einsum("hqk,khe->qhe", grad_scores, key_rows, preferred_element_type=F32)
            * score_scale
        )
        grad_keys = (
            grad_keys
            + jnp.einsum("hqk,qhe->khe", grad_scores, query_block, preferred_element_type=F32)
            * score_scale
        )
        return ((grad_keys, grad_values), grad_query)

    block_starts = jnp.arange(row_count // block_rows, dtype=jnp.int32) * block_rows
    zeros_like_keys = jnp.zeros(queries.shape, F32)
    (grad_keys, grad_values), grad_queries = lax.scan(
        one_block, (zeros_like_keys, zeros_like_keys), (block_starts, log_total)
    )
    return (grad_queries.reshape(queries.shape), grad_keys, grad_values)


def shards(
    tokens,
    seq_start,
    proj_weight,
    proj_bias,
    out_weight,
    up_weight,
    up_bias,
    down_weight,
    norm_gains,
    biases,
    cotangent,
):
    local_rows, width = tokens.shape
    n_dp, n_tensor = lax.axis_size("dp"), lax.axis_size("tensor")
    dp_index, tensor_index = lax.axis_index("dp"), lax.axis_index("tensor")
    row_count = local_rows * n_tensor
    block_rows = min(512, row_count)
    hidden_width = up_weight.shape[1]
    heads_here = proj_bias.shape[1]
    head_size = proj_bias.shape[2] * n_dp
    local_width = heads_here * head_size

    up_rows = dp_gather(up_weight)
    down_rows = dp_gather(down_weight.T)
    joined_rows = dp_gather(proj_weight.reshape(proj_weight.shape[0], 3 * local_width))
    mix_rows = dp_gather(out_weight.T)

    token_rows = lax.all_gather(tokens, "tensor", axis=0, tiled=True)
    grad_rows = lax.all_gather(cotangent, "tensor", axis=0, tiled=True)

    vectors = jnp.concatenate([norm_gains, biases], axis=0).reshape(1, -1)
    table = jnp.zeros((n_dp * n_tensor, vectors.shape[1]), BF16)
    table = lax.dynamic_update_slice(table, vectors, (dp_index * n_tensor + tensor_index, 0))
    shifts = jnp.concatenate([proj_bias.reshape(1, -1), up_bias.reshape(1, -1)], axis=1)
    shift_table = jnp.zeros((n_dp, shifts.shape[1]), BF16)
    shift_table = lax.dynamic_update_slice(shift_table, shifts, (dp_index, 0))
    table = butterfly(butterfly(table, "dp"), "tensor")
    shift_table = butterfly(shift_table, "dp")
    six_rows = (
        table.reshape(n_dp * n_tensor, 6, -1).transpose(1, 0, 2).reshape(6, width).astype(F32)
    )
    gain_rows, shift_rows = six_rows[:2], six_rows[2:]
    proj_part = proj_bias.size
    joined_bias = (
        shift_table[:, :proj_part]
        .reshape(n_dp, 3, heads_here, -1)
        .transpose(1, 2, 0, 3)
        .reshape(3 * local_width)
        .astype(F32)
    )
    hidden_bias = shift_table[:, proj_part:].reshape(hidden_width).astype(F32)

    xhat, _ = standardize(token_rows)
    first_rows = (xhat * gain_rows[0] + shift_rows[0]).astype(BF16)
    second_rows = (xhat * gain_rows[1] + shift_rows[1]).astype(BF16)

    hidden = jnp.dot(second_rows, up_rows, preferred_element_type=F32) + hidden_bias
    bell = lax.erf(hidden * (0.5**0.5))
    activated = (0.5 * hidden * (1.0 + bell)).astype(BF16)
    gelu_slope = 0.5 * (1.0 + bell) + hidden * jnp.exp(-0.5 * hidden * hidden) * 0.3989422804014327

    projected = jnp.dot(first_rows, joined_rows, preferred_element_type=F32) + joined_bias
    projected = projected.reshape(row_count, 3, local_width)
    positions = dp_index * row_count + jnp.arange(row_count, dtype=jnp.int32) - seq_start
    queries = rotate(
        projected[:, 0].reshape(row_count, heads_here, head_size), positions, 1.0
    ).astype(BF16)
    key_rows = rotate(
        projected[:, 1].reshape(row_count, heads_here, head_size), positions, 1.0
    ).astype(BF16)
    value_rows = projected[:, 2].reshape(row_count, heads_here, head_size).astype(BF16)
    attended, log_total = attention_forward(queries, key_rows, value_rows, seq_start, block_rows)
    attended = attended.reshape(row_count, local_width).astype(BF16)

    branch_terms = jnp.einsum(
        "ne,de->nd", attended, mix_rows, preferred_element_type=F32
    ) + jnp.einsum("nf,df->nd", activated, down_rows, preferred_element_type=F32)
    branches = lax.psum_scatter(
        branch_terms.astype(BF16), "tensor", scatter_dimension=0, tiled=True
    ).astype(F32)
    local_f = tokens.astype(F32)
    output = (local_f + branches + shift_rows[2] + shift_rows[3]).astype(BF16)

    grad_active = jnp.einsum("nd,df->nf", grad_rows, down_rows, preferred_element_type=F32)
    grad_hidden = (grad_active * gelu_slope).astype(BF16)
    down_term = jnp.einsum(
        "nd,nf->df", grad_rows, activated, preferred_element_type=F32
    ).astype(BF16)
    down_sum = dp_scatter(down_term)
    up_term = jnp.einsum(
        "nd,nf->df", second_rows, grad_hidden, preferred_element_type=F32
    ).astype(BF16)
    up_sum = dp_scatter(up_term)
    up_bias_term = jnp.sum(grad_hidden, axis=0, dtype=F32)
    grad_second = jnp.einsum("nf,df->nd", grad_hidden, up_rows, preferred_element_type=F32)
    grad_attended = jnp.einsum(
        "nd,de->ne", grad_rows, mix_rows, preferred_element_type=F32
    ).astype(BF16)
    mix_term = jnp.einsum(
        "nd,ne->de", grad_rows, attended, preferred_element_type=F32
    ).astype(BF16)
    mix_sum = dp_scatter(mix_term)
    query_back, key_back, value_back = attention_backward(
        queries,
        key_rows,
        value_rows,
        seq_start,
        log_total,
        grad_attended.reshape(row_count, heads_here, head_size),
        block_rows,
    )
    query_back = rotate(query_back, positions, -1.0).reshape(row_count, local_width)
    key_back = rotate(key_back, positions, -1.0).reshape(row_count, local_width)
    grad_projected = jnp.concatenate(
        [query_back, key_back, value_back.reshape(row_count, local_width)], axis=1
    ).astype(BF16)
    joined_term = jnp.einsum(
        "nd,nc->dc", first_rows, grad_projected, preferred_element_type=F32
    ).astype(BF16)
    joined_sum = dp_scatter(joined_term)
    joined_bias_term = jnp.sum(grad_projected, axis=0, dtype=F32)
    grad_first = jnp.einsum("nc,dc->nd", grad_projected, joined_rows, preferred_element_type=F32)

    back = grad_first * gain_rows[0] + grad_second * gain_rows[1]
    back = lax.psum_scatter(
        back.astype(BF16), "tensor", scatter_dimension=0, tiled=True
    ).astype(F32)
    xhat_local, scale_local = standardize(tokens)
    grad_norm_in = (
        back
        - jnp.mean(back, axis=-1, keepdims=True)
        - xhat_local * jnp.mean(back * xhat_local, axis=-1, keepdims=True)
    ) * scale_local
    grad_local = cotangent.astype(F32)
    input_grad = grad_local + grad_norm_in

    five = jnp.stack(
        [
            jnp.sum(grad_first * xhat, axis=0),
            jnp.sum(grad_second * xhat, axis=0),
            jnp.sum(grad_first, axis=0),
            jnp.sum(grad_second, axis=0),
            jnp.sum(grad_local, axis=0),
        ],
        axis=0,
    )
    shift_terms = jnp.concatenate([joined_bias_term, up_bias_term])[None]
    five, shift_terms = butterfly(butterfly(five, "dp"), "tensor"), butterfly(shift_terms, "dp")
    columns = norm_gains.shape[1]
    mine = lax.dynamic_slice_in_dim(five, (dp_index * n_tensor + tensor_index) * columns, columns, 1)
    gains_grad = mine[:2]
    biases_grad = jnp.concatenate([mine[2:], mine[4:]], axis=0)
    joined_bias_sum = lax.dynamic_slice_in_dim(
        shift_terms[0, : 3 * local_width].reshape(3, heads_here, head_size),
        dp_index * proj_bias.shape[2],
        proj_bias.shape[2],
        2,
    )
    up_bias_sum = lax.dynamic_slice_in_dim(
        shift_terms[:, 3 * local_width :], dp_index * up_bias.shape[1], up_bias.shape[1], 1
    )
    return (
        output,
        input_grad,
        joined_sum.reshape(proj_weight.shape),
        joined_bias_sum,
        mix_sum.T,
        up_sum,
        up_bias_sum,
        down_sum.T,
        gains_grad,
        biases_grad,
    )


def solution(mesh):
    in_specs = (
        P(("dp", "tensor"), None),
        P("dp"),
        P("dp", None, "tensor"),
        P(None, "tensor", "dp"),
        P("tensor", "dp"),
        P("dp", "tensor"),
        P("tensor", "dp"),
        P("tensor", "dp"),
        P(None, ("dp", "tensor")),
        P(None, ("dp", "tensor")),
        P(("dp", "tensor"), None),
    )
    out_specs = (
        P(("dp", "tensor"), None),
        P(("dp", "tensor"), None),
        P("dp", None, "tensor"),
        P(None, "tensor", "dp"),
        P("tensor", "dp"),
        P("dp", "tensor"),
        P("tensor", "dp"),
        P("tensor", "dp"),
        P(None, ("dp", "tensor")),
        P(None, ("dp", "tensor")),
    )
    return jax.shard_map(shards, mesh=mesh, in_specs=in_specs, out_specs=out_specs, check_vma=False)
```

```python
import functools

import jax
import jax.numpy as jnp
from jax import lax
from jax.experimental import pallas as pl
from jax.experimental.pallas import tpu as pltpu
from jax.sharding import PartitionSpec as P

ROT = 64
EPSILON = 1e-05
ROTARY_BASE = 10000.0
F32 = jnp.float32
BF16 = jnp.bfloat16
HALVES = [(0, 0), (0, 1), (2, 1), (2, 0), (6, 0), (6, 1), (4, 1), (4, 0)]
ORDER = HALVES + [(p ^ 1, h) for p, h in HALVES]


def cut(*values):
    return lax.optimization_barrier(values)


def is_power(n):
    return n & (n - 1) == 0


def fast_dp():
    return lax.axis_size("dp") == 8


def xor_shift(values, axis, bit):
    size = lax.axis_size(axis)
    return lax.ppermute(values, axis, [(i, i ^ bit) for i in range(size)])


def butterfly(values, axis):
    size = lax.axis_size(axis)
    if not is_power(size):
        return lax.psum(values, axis)
    bit = 1
    while bit < size:
        values = values + xor_shift(values, axis, bit)
        bit *= 2
    return values


def columns_kernel(index_ref, x_ref, o_ref, *, count, step):
    for j in range(count):
        at = pl.multiple_of(index_ref[j] * step, step)
        o_ref[:, j * step : (j + 1) * step] = x_ref[:, pl.ds(at, step)]


def take_columns(values, index):
    rows, width = values.shape
    count = index.shape[0]
    return pl.pallas_call(
        functools.partial(columns_kernel, count=count, step=width // count),
        out_shape=jax.ShapeDtypeStruct(values.shape, values.dtype),
        grid_spec=pltpu.PrefetchScalarGridSpec(
            num_scalar_prefetch=1,
            grid=(1,),
            in_specs=[pl.BlockSpec((rows, width), lambda i, s: (0, 0))],
            out_specs=pl.BlockSpec((rows, width), lambda i, s: (0, 0)),
        ),
        name="columns",
    )(index, values)


def frame_index():
    me = lax.axis_index("dp")
    return jnp.stack([(me ^ p) * 2 + h for p, h in ORDER]).astype(jnp.int32)


def plain_index():
    me = lax.axis_index("dp")
    spot = jnp.array([ORDER.index((k // 2, k % 2)) for k in range(16)], jnp.int32)
    return jnp.stack([jnp.take(spot, (me ^ (k // 2)) * 2 + k % 2) for k in range(16)])


def to_frame(values):
    return take_columns(values, frame_index()) if fast_dp() else values


def from_frame(values):
    return take_columns(values, plain_index()) if fast_dp() else values


def dp_gather(shard):
    if not fast_dp():
        return [lax.all_gather(shard, "dp", axis=0, tiled=True)]
    half = shard.shape[0] // 2
    from_x = xor_shift(shard, "dp", 2)
    from_y = xor_shift(shard, "dp", 4)
    far_1 = xor_shift(from_y[:half], "dp", 2)
    far_2 = xor_shift(from_x[half:], "dp", 4)
    far = jnp.concatenate([far_1, far_2], axis=0)
    near = xor_shift(shard, "dp", 1)
    near_x = xor_shift(from_x, "dp", 1)
    near_y = xor_shift(from_y, "dp", 1)
    near_far = xor_shift(far, "dp", 1)
    out = []
    for own, x, f, y in ((shard, from_x, far, from_y), (near, near_x, near_far, near_y)):
        out += [own, x[half:], x[:half], f, y[half:], y[:half]]
    return out


def join(pieces, start, stop):
    return jnp.concatenate([p[:, start:stop] for p in pieces], axis=0)


def dp_scatter(make):
    away = make(1)
    came = xor_shift(away, "dp", 1)
    kept = make(0)
    rows = kept.shape[0] // 4
    half = rows // 2

    def summed(start, stop):
        return kept[start:stop].astype(F32) + came[start:stop].astype(F32)

    first_x = xor_shift(summed(rows + half, 2 * rows + half).astype(BF16), "dp", 2)
    first_y = xor_shift(summed(2 * rows + half, 3 * rows + half).astype(BF16), "dp", 4)
    last_x = summed(rows, rows + half) + first_y[:half].astype(F32)
    last_y = summed(3 * rows + half, 4 * rows) + first_x[half:].astype(F32)
    last_x = xor_shift(last_x.astype(BF16), "dp", 2)
    last_y = xor_shift(last_y.astype(BF16), "dp", 4)
    top = summed(0, half) + first_x[:half].astype(F32) + last_y.astype(F32)
    low = summed(half, rows) + first_y[half:].astype(F32) + last_x.astype(F32)
    return jnp.concatenate([top, low], axis=0)


def weight_grad(rows, columns):
    def make(part):
        width = rows.shape[1] // 2
        chosen = rows[:, part * width : (part + 1) * width]
        return jnp.einsum("nd,nf->df", chosen, columns, preferred_element_type=F32).astype(BF16)

    if fast_dp():
        return dp_scatter(make)
    whole = jnp.einsum("nd,nf->df", rows, columns, preferred_element_type=F32).astype(BF16)
    return lax.psum_scatter(whole, "dp", scatter_dimension=0, tiled=True).astype(F32)


def line_gather(block):
    size = lax.axis_size("tensor")
    me = lax.axis_index("tensor")
    up = down = block
    ups, downs = [block], [block]
    for s in range(size - 1):
        up = lax.ppermute(up, "tensor", [(i, i + 1) for i in range(s, size - 1)])
        down = lax.ppermute(down, "tensor", [(i + 1, i) for i in range(size - 1 - s)])
        ups.append(up)
        downs.append(down)
    blocks = [block]
    for r in range(1, size):
        blocks.append(jnp.where(me + r < size, downs[r], ups[size - r]))
    return jnp.concatenate(blocks, axis=0)


def line_scatter(terms):
    size = lax.axis_size("tensor")
    rows = terms.shape[0] // size

    def block(r):
        return terms[r * rows : (r + 1) * rows]

    up = down = None
    for s in range(1, size):
        to_up, to_down = block(size - s), block(s)
        if s > 1:
            to_up = (to_up.astype(F32) + up.astype(F32)).astype(BF16)
            to_down = (to_down.astype(F32) + down.astype(F32)).astype(BF16)
        up = lax.ppermute(to_up, "tensor", [(i, i + 1) for i in range(s)])
        down = lax.ppermute(to_down, "tensor", [(i, i - 1) for i in range(size - s, size)])
    return block(0).astype(F32) + up.astype(F32) + down.astype(F32)


def turn(values, cosine, low_sine, high_sine, sign):
    half = ROT // 2
    lanes = cosine.shape[-1]
    head = values[:, :lanes]
    turned = (
        head * cosine
        - sign * pltpu.roll(head, lanes - half, 1) * low_sine
        + sign * pltpu.roll(head, half, 1) * high_sine
    )
    return jnp.concatenate([turned, values[:, lanes:]], axis=1)


def contract(a, b, dims):
    return lax.dot_general(a, b, (dims, ((), ())), preferred_element_type=F32)


def masked(scores, column_starts, row_starts, query_block, block):
    keys = scores.shape[1]
    query = lax.broadcasted_iota(jnp.int32, scores.shape, 0) + query_block * block
    key = lax.broadcasted_iota(jnp.int32, scores.shape, 1)
    allowed = (column_starts == row_starts[:, :keys]) & (key <= query)
    return allowed, jnp.where(allowed, scores, -1e30)


def forward_kernel(
    me_ref, q_ref, k_ref, v_ref, cos_ref, low_ref, high_ref, col_ref, row_ref,
    q_out, k_out, v_out, att_ref, log_ref, *, size, block,
):
    def spot(b):
        return pl.ds(pl.multiple_of(lax.rem(b - me_ref[0] + size, size) * block, block), block)

    scale = q_ref.shape[-1] ** (-0.5)
    for b in range(size):
        here = slice(b * block, (b + 1) * block)
        at = spot(b)
        tables = cos_ref[here, :], low_ref[here, :], high_ref[here, :]
        q_out[at, :] = turn(q_ref[at, :], *tables, 1.0).astype(BF16)
        k_out[at, :] = turn(k_ref[at, :], *tables, 1.0).astype(BF16)
        v_out[at, :] = v_ref[at, :].astype(BF16)
    for b in range(size):
        here = slice(b * block, (b + 1) * block)
        query = q_out[spot(b), :]
        scores = jnp.concatenate(
            [contract(query, k_out[spot(c), :], ((1,), (1,))) for c in range(b + 1)], axis=1
        ) * scale
        _, scores = masked(scores, col_ref[here, :1], row_ref[:1, :], b, block)
        top = jnp.max(scores, axis=1, keepdims=True)
        powers = jnp.exp(scores - top)
        total = jnp.sum(powers, axis=1, keepdims=True)
        weights = (powers / total).astype(BF16)
        attended = contract(weights[:, :block], v_out[spot(0), :], ((1,), (0,)))
        for c in range(1, b + 1):
            attended = attended + contract(
                weights[:, c * block : (c + 1) * block], v_out[spot(c), :], ((1,), (0,))
            )
        att_ref[spot(b), :] = attended.astype(BF16)
        log_ref[0, here, :] = jnp.broadcast_to(top + jnp.log(total), (block, log_ref.shape[2]))


def backward_kernel(
    me_ref, q_ref, k_ref, v_ref, g_ref, log_ref, cos_ref, low_ref, high_ref, col_ref, row_ref,
    dq_ref, dk_ref, dv_ref, k_acc, v_acc, *, size, block,
):
    def spot(b):
        return pl.ds(pl.multiple_of(lax.rem(b - me_ref[0] + size, size) * block, block), block)

    scale = q_ref.shape[-1] ** (-0.5)
    for b in range(size):
        here = slice(b * block, (b + 1) * block)
        query, grad = q_ref[spot(b), :], g_ref[spot(b), :]
        scores = jnp.concatenate(
            [contract(query, k_ref[spot(c), :], ((1,), (1,))) for c in range(b + 1)], axis=1
        ) * scale
        allowed, scores = masked(scores, col_ref[here, :1], row_ref[:1, :], b, block)
        probs = jnp.where(allowed, jnp.exp(scores - log_ref[0, here, :1]), 0.0)
        grad_probs = jnp.concatenate(
            [contract(grad, v_ref[spot(c), :], ((1,), (1,))) for c in range(b + 1)], axis=1
        )
        inner = jnp.sum(probs * grad_probs, axis=1, keepdims=True)
        weights = probs.astype(BF16)
        grad_scores = (probs * (grad_probs - inner)).astype(BF16)
        back = None
        for c in range(b + 1):
            part = slice(c * block, (c + 1) * block)
            key_term = contract(grad_scores[:, part], query, ((0,), (0,)))
            value_term = contract(weights[:, part], grad, ((0,), (0,)))
            query_term = contract(grad_scores[:, part], k_ref[spot(c), :], ((1,), (0,)))
            back = query_term if c == 0 else back + query_term
            if c == b:
                k_acc[part, :] = key_term
                v_acc[part, :] = value_term
            else:
                k_acc[part, :] += key_term
                v_acc[part, :] += value_term
        tables = cos_ref[here, :], low_ref[here, :], high_ref[here, :]
        dq_ref[spot(b), :] = turn(back * scale, *tables, -1.0).astype(BF16)
    for b in range(size):
        here = slice(b * block, (b + 1) * block)
        tables = cos_ref[here, :], low_ref[here, :], high_ref[here, :]
        dk_ref[spot(b), :] = turn(k_acc[here, :] * scale, *tables, -1.0).astype(BF16)
        dv_ref[spot(b), :] = v_acc[here, :].astype(BF16)


def attention_tables(positions, starts):
    half = ROT // 2
    frequency = ROTARY_BASE ** (-(jnp.arange(half, dtype=F32) * 2.0) / ROT)
    angles = positions.astype(F32)[:, None] * frequency[None, :]
    cosine, sine = jnp.cos(angles), jnp.sin(angles)
    rows = positions.shape[0]
    cosines = jnp.concatenate([cosine, cosine, jnp.ones((rows, 128 - ROT), F32)], axis=1)
    low = jnp.concatenate([sine, jnp.zeros((rows, 128 - half), F32)], axis=1)
    high = jnp.concatenate([jnp.zeros((rows, half), F32), sine, jnp.zeros((rows, 128 - ROT), F32)], axis=1)
    columns = jnp.broadcast_to(starts[:, None], (rows, 128))
    across = jnp.broadcast_to(starts[None, :], (8, rows))
    return cosines, low, high, columns, across


def attention_forward(projected, tables, me, heads, size):
    rows = projected.shape[0]
    head = projected.shape[1] // (3 * heads)
    block = rows // size
    whole = lambda h, s: (0, 0)
    table_specs = [pl.BlockSpec((rows, 128), whole)] * 4 + [pl.BlockSpec((8, rows), whole)]
    by_head = pl.BlockSpec((rows, head), lambda h, s: (0, h))
    wide = jax.ShapeDtypeStruct((rows, heads * head), BF16)
    return pl.pallas_call(
        functools.partial(forward_kernel, size=size, block=block),
        out_shape=(wide, wide, wide, wide, jax.ShapeDtypeStruct((heads, rows, 128), F32)),
        grid_spec=pltpu.PrefetchScalarGridSpec(
            num_scalar_prefetch=1,
            grid=(heads,),
            in_specs=[
                pl.BlockSpec((rows, head), lambda h, s, k=k: (0, k * heads + h)) for k in range(3)
            ]
            + table_specs,
            out_specs=(by_head,) * 4 + (pl.BlockSpec((1, rows, 128), lambda h, s: (h, 0, 0)),),
        ),
        cost_estimate=pl.CostEstimate(
            flops=heads * rows * rows * head * 40, bytes_accessed=rows * head * heads * 24,
            transcendentals=heads * rows * rows // 2,
        ),
        name="attention_forward",
    )(me, projected, projected, projected, *tables)


def attention_backward(queries, keys, values, grads, log_total, tables, me, heads, size):
    rows = queries.shape[0]
    head = queries.shape[1] // heads
    block = rows // size
    whole = lambda h, s: (0, 0)
    table_specs = [pl.BlockSpec((rows, 128), whole)] * 4 + [pl.BlockSpec((8, rows), whole)]
    by_head = pl.BlockSpec((rows, head), lambda h, s: (0, h))
    wide = jax.ShapeDtypeStruct((rows, heads * head), BF16)
    return pl.pallas_call(
        functools.partial(backward_kernel, size=size, block=block),
        out_shape=(wide, wide, wide),
        grid_spec=pltpu.PrefetchScalarGridSpec(
            num_scalar_prefetch=1,
            grid=(heads,),
            in_specs=[by_head] * 4
            + [pl.BlockSpec((1, rows, 128), lambda h, s: (h, 0, 0))]
            + table_specs,
            out_specs=(by_head,) * 3,
            scratch_shapes=[pltpu.VMEM((rows, head), F32)] * 2,
        ),
        cost_estimate=pl.CostEstimate(
            flops=heads * rows * rows * head * 60, bytes_accessed=rows * head * heads * 24,
            transcendentals=heads * rows * rows // 2,
        ),
        name="attention_backward",
    )(me, queries, keys, values, grads, log_total, *tables)


def standardize(values):
    values = values.astype(F32)
    centered = values - jnp.mean(values, axis=-1, keepdims=True)
    spread = jnp.mean(centered * centered, axis=-1, keepdims=True)
    scale = lax.rsqrt(spread + EPSILON)
    return centered * scale, scale


def norm_rows(token_rows, gain_rows, shift_rows):
    xhat, _ = standardize(token_rows)
    first_rows = (xhat * gain_rows[0] + shift_rows[0]).astype(BF16)
    second_rows = (xhat * gain_rows[1] + shift_rows[1]).astype(BF16)
    return first_rows, second_rows


def hidden_units(second_rows, up_rows, hidden_bias):
    hidden = jnp.dot(second_rows, up_rows, preferred_element_type=F32) + hidden_bias
    bell = lax.erf(hidden * (0.5**0.5))
    activated = (0.5 * hidden * (1.0 + bell)).astype(BF16)
    slope = 0.5 * (1.0 + bell) + hidden * jnp.exp(-0.5 * hidden * hidden) * 0.3989422804014327
    return activated, slope.astype(BF16)


def branch_rows(attended, mix_rows, activated, down_rows):
    return (
        jnp.einsum("ne,de->nd", attended, mix_rows, preferred_element_type=F32)
        + jnp.einsum("nf,df->nd", activated, down_rows, preferred_element_type=F32)
    ).astype(BF16)


def hidden_grads(grad_rows, down_rows, slope):
    grad_active = jnp.einsum("nd,df->nf", grad_rows, down_rows, preferred_element_type=F32)
    return (grad_active * slope.astype(F32)).astype(BF16)


def attended_grads(grad_rows, mix_rows):
    return jnp.einsum("nd,de->ne", grad_rows, mix_rows, preferred_element_type=F32).astype(BF16)


def back_rows(grads, weight_rows):
    return jnp.einsum("nf,df->nd", grads, weight_rows, preferred_element_type=F32)


def grad_half(rows, columns, part):
    width = rows.shape[1] // 2
    chosen = rows[:, part * width : (part + 1) * width]
    return jnp.einsum("nd,nf->df", chosen, columns, preferred_element_type=F32).astype(BF16)


def plus(*terms):
    return functools.reduce(lambda a, b: a + b, [t.astype(F32) for t in terms])


def width_sums(grad_first, grad_second, xhat, grad_local):
    return jnp.stack(
        [
            jnp.sum(grad_first * xhat, axis=0),
            jnp.sum(grad_second * xhat, axis=0),
            jnp.sum(grad_first, axis=0),
            jnp.sum(grad_second, axis=0),
            jnp.sum(grad_local.astype(F32), axis=0),
        ],
        axis=0,
    )


def shards(
    tokens,
    seq_start,
    proj_weight,
    proj_bias,
    out_weight,
    up_weight,
    up_bias,
    down_weight,
    norm_gains,
    biases,
    cotangent,
):
    local_rows, width = tokens.shape
    n_dp, n_tensor = lax.axis_size("dp"), lax.axis_size("tensor")
    dp_index, tensor_index = lax.axis_index("dp"), lax.axis_index("tensor")
    row_count = local_rows * n_tensor
    hidden_width = up_weight.shape[1]
    heads_here = proj_bias.shape[1]
    head_size = proj_bias.shape[2] * n_dp
    local_width = heads_here * head_size
    joined_width = 3 * local_width
    columns = norm_gains.shape[1]

    vectors = jnp.concatenate(
        [norm_gains.reshape(1, -1), biases.reshape(1, -1), proj_bias.reshape(1, -1), up_bias.reshape(1, -1)],
        axis=1,
    )
    table = jnp.zeros((n_dp * n_tensor, vectors.shape[1]), BF16)
    table = lax.dynamic_update_slice(table, vectors, (dp_index * n_tensor + tensor_index, 0))
    table = butterfly(butterfly(table, "dp"), "tensor")
    local_tokens, local_grads = to_frame(tokens), to_frame(cotangent)
    positions = dp_index * row_count + jnp.arange(row_count, dtype=jnp.int32) - seq_start
    tables = attention_tables(positions, seq_start)
    me = tensor_index.astype(jnp.int32).reshape(1)
    flat_proj = proj_weight.reshape(-1, joined_width)

    def small_parameters(table):
        six_rows = table[:, : 6 * columns].reshape(n_dp * n_tensor, 6, columns).transpose(1, 0, 2)
        six_rows = to_frame(six_rows.reshape(6, width).astype(F32))
        of_tensor = lax.dynamic_index_in_dim(
            table[:, 6 * columns :].reshape(n_dp, n_tensor, -1), tensor_index, 1, keepdims=False
        ).astype(F32)
        joined_bias = (
            of_tensor[:, : proj_bias.size]
            .reshape(n_dp, 3, heads_here, -1)
            .transpose(1, 2, 0, 3)
            .reshape(joined_width)
        )
        hidden_bias = of_tensor[:, proj_bias.size :].reshape(hidden_width)
        return six_rows[:2], six_rows[2:], joined_bias, hidden_bias

    def attend(first_rows, joined_rows, joined_bias):
        projected = jnp.dot(first_rows, joined_rows, preferred_element_type=F32) + joined_bias
        return attention_forward(projected, tables, me, heads_here, n_tensor)

    def attend_back(kept, grad_attended):
        queries, keys, values, log_total = kept
        backs = attention_backward(
            queries, keys, values, grad_attended, log_total, tables, me, heads_here, n_tensor
        )
        return jnp.concatenate(backs, axis=1)

    def finish_output(branches, shift_rows):
        output = local_tokens.astype(F32) + branches + shift_rows[2] + shift_rows[3]
        return from_frame(output.astype(BF16))

    def finish_input_grad(back):
        xhat_local, scale_local = standardize(local_tokens)
        grad_norm_in = (
            back
            - jnp.mean(back, axis=-1, keepdims=True)
            - xhat_local * jnp.mean(back * xhat_local, axis=-1, keepdims=True)
        ) * scale_local
        return from_frame(local_grads.astype(F32) + grad_norm_in)

    def small_grads(five, joined_bias_term, up_bias_term):
        five = from_frame(five).reshape(1, -1)
        terms = jnp.concatenate([five, joined_bias_term[None], up_bias_term[None]], axis=1)
        terms = butterfly(terms, "dp")
        five = butterfly(terms[:, : 5 * width], "tensor").reshape(5, width)
        mine = lax.dynamic_slice_in_dim(
            five, (dp_index * n_tensor + tensor_index) * columns, columns, 1
        )
        biases_grad = jnp.concatenate([mine[2:], mine[4:]], axis=0)
        joined_bias_sum = lax.dynamic_slice_in_dim(
            terms[0, 5 * width : 5 * width + joined_width].reshape(3, heads_here, head_size),
            dp_index * proj_bias.shape[2],
            proj_bias.shape[2],
            2,
        )
        up_bias_sum = lax.dynamic_slice_in_dim(
            terms[:, 5 * width + joined_width :], dp_index * up_bias.shape[1], up_bias.shape[1], 1
        )
        return mine[:2], biases_grad, joined_bias_sum, up_bias_sum

    def plain():
        token_rows, grad_rows = line_gather(local_tokens), line_gather(local_grads)
        up_rows, down_rows = dp_gather(up_weight), dp_gather(down_weight.T)
        joined_rows, mix_rows = dp_gather(flat_proj), dp_gather(out_weight.T)
        up_rows, down_rows, joined_rows, mix_rows = (
            join(w, 0, None) for w in (up_rows, down_rows, joined_rows, mix_rows)
        )
        gain_rows, shift_rows, joined_bias, hidden_bias = small_parameters(table)
        first_rows, second_rows = norm_rows(token_rows, gain_rows, shift_rows)
        activated, slope = cut(*hidden_units(second_rows, up_rows, hidden_bias))
        *kept, attended, log_total = attend(first_rows, joined_rows, joined_bias)
        branches = line_scatter(branch_rows(attended, mix_rows, activated, down_rows))
        output = finish_output(branches, shift_rows)
        grad_hidden = hidden_grads(grad_rows, down_rows, slope)
        down_sum = weight_grad(grad_rows, activated)
        up_sum = weight_grad(second_rows, grad_hidden)
        grad_second = back_rows(grad_hidden, up_rows)
        grad_attended = attended_grads(grad_rows, mix_rows)
        mix_sum = weight_grad(grad_rows, attended)
        grad_projected = attend_back((*kept, log_total), grad_attended)
        joined_sum = weight_grad(first_rows, grad_projected)
        grad_first = back_rows(grad_projected, joined_rows)
        back = grad_first * gain_rows[0] + grad_second * gain_rows[1]
        input_grad = finish_input_grad(line_scatter(back.astype(BF16)))
        five = width_sums(grad_first, grad_second, standardize(token_rows)[0], local_grads)
        small = small_grads(
            five, jnp.sum(grad_projected, axis=0, dtype=F32), jnp.sum(grad_hidden, axis=0, dtype=F32)
        )
        return output, input_grad, joined_sum, mix_sum, up_sum, down_sum, small

    def staged():
        half = local_rows // 2
        first, second = slice(0, half), slice(half, 2 * half)

        def x(values):
            return xor_shift(values, "dp", 2)

        def y(values):
            return xor_shift(values, "dp", 4)

        def core(values):
            return xor_shift(values, "dp", 1)

        def gather_step(up, down, s):
            up = lax.ppermute(up, "tensor", [(i, i + 1) for i in range(s, 3)])
            down = lax.ppermute(down, "tensor", [(i + 1, i) for i in range(3 - s)])
            return up, down

        def scatter_step(terms, up, down, s):
            to_up = terms[(4 - s) * local_rows : (5 - s) * local_rows]
            to_down = terms[s * local_rows : (s + 1) * local_rows]
            if s > 1:
                to_up, to_down = plus(to_up, up).astype(BF16), plus(to_down, down).astype(BF16)
            up = lax.ppermute(to_up, "tensor", [(i, i + 1) for i in range(s)])
            down = lax.ppermute(to_down, "tensor", [(i, i - 1) for i in range(4 - s, 4)])
            return up, down

        def in_turn(block, ups, downs):
            blocks = [block] + [
                jnp.where(tensor_index + r < 4, downs[r - 1], ups[3 - r]) for r in range(1, 4)
            ]
            return jnp.concatenate(blocks, axis=0)

        def pair(top, low):
            return jnp.concatenate([top, low], axis=0)

        wa = up_weight
        wb = jnp.concatenate([flat_proj, out_weight.T], axis=1)
        wc = down_weight.T

        tu1, td1 = gather_step(local_tokens, local_tokens, 0)
        ax, ay, na = x(wa), y(wa), core(wa)
        tu1, td1, ax, ay, na, table1, wb, wc = cut(tu1, td1, ax, ay, na, table, wb, wc)
        tu2, td2 = gather_step(tu1, td1, 1)
        p2x, p2y = x(pair(ay[first], wb[second])), y(pair(ax[second], wb[first]))
        nax, nay = core(ax), core(ay)
        gain_rows, shift_rows, joined_bias, hidden_bias = small_parameters(table1)
        tu2, td2, p2x, p2y, nax, nay = cut(tu2, td2, p2x, p2y, nax, nay)
        tu3, td3 = gather_step(tu2, td2, 2)
        p3x, p3y = x(pair(p2y[second], wb[first])), y(pair(p2x[second], wb[second]))
        n2x, n2y, nb = core(p2x), core(p2y), core(wb)
        tu3, td3, p3x, p3y, n2x, n2y, nb, local_grads1 = cut(
            tu3, td3, p3x, p3y, n2x, n2y, nb, local_grads
        )
        cu1, cd1 = gather_step(local_grads1, local_grads1, 0)
        cx, cy = x(wc), y(wc)
        n3x, n3y, nc = core(p3x), core(p3y), core(wc)
        token_rows = in_turn(local_tokens, (tu1, tu2, tu3), (td1, td2, td3))
        first_rows, second_rows = norm_rows(token_rows, gain_rows, shift_rows)
        up_rows = jnp.concatenate(
            [wa, ax[second], ax[first], p2x[first], p2y[first], ay[second], ay[first]]
            + [na, nax[second], nax[first], n2x[first], n2y[first], nay[second], nay[first]],
            axis=0,
        )
        activated, slope = hidden_units(second_rows, up_rows, hidden_bias)
        cu1, cd1, cx, cy, n3x, n3y, nc, first_rows, activated, slope = cut(
            cu1, cd1, cx, cy, n3x, n3y, nc, first_rows, activated, slope
        )
        cu2, cd2 = gather_step(cu1, cd1, 1)
        fcx, fcy = x(cy[first]), y(cx[second])
        ncx, ncy = core(cx), core(cy)
        second_pieces = [wb, p2x[second], p3x[second], p3x[first], p3y[first], p3y[second], p2y[second]] + [
            nb, n2x[second], n3x[second], n3x[first], n3y[first], n3y[second], n2y[second]
        ]
        joined_rows = join(second_pieces, 0, joined_width)
        mix_rows = join(second_pieces, joined_width, None)
        *kept, attended, log_total = attend(first_rows, joined_rows, joined_bias)
        kept = (*kept, log_total)
        cu2, cd2, fcx, fcy, ncx, ncy, attended = cut(cu2, cd2, fcx, fcy, ncx, ncy, attended)
        cu3, cd3 = gather_step(cu2, cd2, 2)
        nfx, nfy = core(fcx), core(fcy)
        down_rows = jnp.concatenate(
            [wc, cx[second], cx[first], fcx, fcy, cy[second], cy[first]]
            + [nc, ncx[second], ncx[first], nfx, nfy, ncy[second], ncy[first]],
            axis=0,
        )
        branch_terms = branch_rows(attended, mix_rows, activated, down_rows)
        cu3, cd3, branch_terms, activated = cut(cu3, cd3, branch_terms, activated)
        bu, bd = scatter_step(branch_terms, None, None, 1)
        grad_rows = in_turn(local_grads1, (cu1, cu2, cu3), (cd1, cd2, cd3))
        away = grad_half(grad_rows, activated, 1)
        came = core(away)
        keep_d = grad_half(grad_rows, activated, 0)
        grad_hidden = hidden_grads(grad_rows, down_rows, slope)
        bu, bd, came_d, keep_d, grad_hidden, grad_rows = cut(
            bu, bd, came, keep_d, grad_hidden, grad_rows
        )

        def at(keep, came, start, stop):
            return plus(keep[start * half : stop * half], came[start * half : stop * half])

        bu, bd = scatter_step(branch_terms, bu, bd, 2)
        d1x = x(at(keep_d, came_d, 3, 5).astype(BF16))
        d1y = y(at(keep_d, came_d, 5, 7).astype(BF16))
        came_u = core(grad_half(second_rows, grad_hidden, 1))
        keep_u = grad_half(second_rows, grad_hidden, 0)
        grad_projected = attend_back(kept, attended_grads(grad_rows, mix_rows))
        bu, bd, d1x, d1y, came_u, keep_u, grad_projected, grad_hidden = cut(
            bu, bd, d1x, d1y, came_u, keep_u, grad_projected, grad_hidden
        )
        bu, bd = scatter_step(branch_terms, bu, bd, 3)
        d2x = plus(at(keep_d, came_d, 2, 3), d1y[first]).astype(BF16)
        d2y = plus(at(keep_d, came_d, 7, 8), d1x[second]).astype(BF16)
        s9x = x(pair(d2x, at(keep_u, came_u, 4, 5).astype(BF16)))
        s9y = y(pair(d2y, at(keep_u, came_u, 5, 6).astype(BF16)))
        grad_second = back_rows(grad_hidden, up_rows)
        grad_first = back_rows(grad_projected, joined_rows)
        back = (grad_first * gain_rows[0] + grad_second * gain_rows[1]).astype(BF16)
        bu, bd, s9x, s9y, back, grad_projected, attended = cut(
            bu, bd, s9x, s9y, back, grad_projected, attended
        )
        eu, ed = scatter_step(back, None, None, 1)
        s10x = x(pair(plus(at(keep_u, came_u, 2, 3), s9y[second]), at(keep_u, came_u, 3, 4)).astype(BF16))
        s10y = y(pair(at(keep_u, came_u, 6, 7), plus(at(keep_u, came_u, 7, 8), s9x[second])).astype(BF16))

        def joined_half(part):
            return jnp.concatenate(
                [grad_half(first_rows, grad_projected, part), grad_half(grad_rows, attended, part)], axis=1
            )

        came_j = core(joined_half(1))
        keep_j = joined_half(0)
        output = finish_output(plus(branch_terms[:local_rows], bu, bd), shift_rows)
        down_sum = pair(
            plus(at(keep_d, came_d, 0, 1), d1x[first], s9y[first]),
            plus(at(keep_d, came_d, 1, 2), d1y[second], s9x[first]),
        )
        eu, ed, s10x, s10y, came_j, keep_j = cut(eu, ed, s10x, s10y, came_j, keep_j)
        eu, ed = scatter_step(back, eu, ed, 2)
        j1x = x(at(keep_j, came_j, 3, 5).astype(BF16))
        j1y = y(at(keep_j, came_j, 5, 7).astype(BF16))
        up_sum = pair(
            plus(at(keep_u, came_u, 0, 1), s10x[second], s10y[second]),
            plus(at(keep_u, came_u, 1, 2), s10x[first], s10y[first]),
        )
        five = width_sums(grad_first, grad_second, standardize(token_rows)[0], local_grads)
        small = small_grads(
            five, jnp.sum(grad_projected, axis=0, dtype=F32), jnp.sum(grad_hidden, axis=0, dtype=F32)
        )
        eu, ed, j1x, j1y = cut(eu, ed, j1x, j1y)
        eu, ed = scatter_step(back, eu, ed, 3)
        j2x = x(plus(at(keep_j, came_j, 2, 3), j1y[first]).astype(BF16))
        j2y = y(plus(at(keep_j, came_j, 7, 8), j1x[second]).astype(BF16))
        joined_mix = pair(
            plus(at(keep_j, came_j, 0, 1), j1x[first], j2y),
            plus(at(keep_j, came_j, 1, 2), j1y[second], j2x),
        )
        input_grad = finish_input_grad(plus(back[:local_rows], eu, ed))
        return (
            output, input_grad, joined_mix[:, :joined_width], joined_mix[:, joined_width:], up_sum, down_sum, small
        )

    parts = staged() if fast_dp() and n_tensor == 4 else plain()
    output, input_grad, joined_sum, mix_sum, up_sum, down_sum, small = parts
    gains_grad, biases_grad, joined_bias_sum, up_bias_sum = small
    return (
        output,
        input_grad,
        joined_sum.reshape(proj_weight.shape),
        joined_bias_sum,
        mix_sum.T,
        up_sum,
        up_bias_sum,
        down_sum.T,
        gains_grad,
        biases_grad,
    )


def solution(mesh):
    in_specs = (
        P(("dp", "tensor"), None),
        P("dp"),
        P("dp", None, "tensor"),
        P(None, "tensor", "dp"),
        P("tensor", "dp"),
        P("dp", "tensor"),
        P("tensor", "dp"),
        P("tensor", "dp"),
        P(None, ("dp", "tensor")),
        P(None, ("dp", "tensor")),
        P(("dp", "tensor"), None),
    )
    out_specs = (
        P(("dp", "tensor"), None),
        P(("dp", "tensor"), None),
        P("dp", None, "tensor"),
        P(None, "tensor", "dp"),
        P("tensor", "dp"),
        P("dp", "tensor"),
        P("tensor", "dp"),
        P("tensor", "dp"),
        P(None, ("dp", "tensor")),
        P(None, ("dp", "tensor")),
    )
    return jax.shard_map(shards, mesh=mesh, in_specs=in_specs, out_specs=out_specs, check_vma=False)
```

```python
import functools

import jax
import jax.numpy as jnp
from jax import lax
from jax.experimental import pallas as pl
from jax.experimental.pallas import tpu as pltpu
from jax.sharding import PartitionSpec as P

ROT = 64
EPSILON = 1e-05
ROTARY_BASE = 10000.0
F32 = jnp.float32
BF16 = jnp.bfloat16
HALVES = [(0, 0), (0, 1), (2, 1), (2, 0), (6, 0), (6, 1), (4, 1), (4, 0)]
ORDER = HALVES + [(p ^ 1, h) for p, h in HALVES]


def cut(*values):
    return lax.optimization_barrier(values)


def is_power(n):
    return n & (n - 1) == 0


def fast_dp():
    return lax.axis_size("dp") == 8


def xor_shift(values, axis, bit):
    size = lax.axis_size(axis)
    return lax.ppermute(values, axis, [(i, i ^ bit) for i in range(size)])


def butterfly(values, axis):
    size = lax.axis_size(axis)
    if not is_power(size):
        return lax.psum(values, axis)
    bit = 1
    while bit < size:
        values = values + xor_shift(values, axis, bit)
        bit *= 2
    return values


def columns_kernel(index_ref, x_ref, o_ref, *, count, step):
    for j in range(count):
        at = pl.multiple_of(index_ref[j] * step, step)
        o_ref[:, j * step : (j + 1) * step] = x_ref[:, pl.ds(at, step)]


def take_columns(values, index):
    rows, width = values.shape
    count = index.shape[0]
    return pl.pallas_call(
        functools.partial(columns_kernel, count=count, step=width // count),
        out_shape=jax.ShapeDtypeStruct(values.shape, values.dtype),
        grid_spec=pltpu.PrefetchScalarGridSpec(
            num_scalar_prefetch=1,
            grid=(1,),
            in_specs=[pl.BlockSpec((rows, width), lambda i, s: (0, 0))],
            out_specs=pl.BlockSpec((rows, width), lambda i, s: (0, 0)),
        ),
        name="columns",
    )(index, values)


def frame_index():
    me = lax.axis_index("dp")
    return jnp.stack([(me ^ p) * 2 + h for p, h in ORDER]).astype(jnp.int32)


def plain_index():
    me = lax.axis_index("dp")
    spot = jnp.array([ORDER.index((k // 2, k % 2)) for k in range(16)], jnp.int32)
    return jnp.stack([jnp.take(spot, (me ^ (k // 2)) * 2 + k % 2) for k in range(16)])


def to_frame(values):
    return take_columns(values, frame_index()) if fast_dp() else values


def from_frame(values):
    return take_columns(values, plain_index()) if fast_dp() else values


def dp_gather(shard):
    if not fast_dp():
        return [lax.all_gather(shard, "dp", axis=0, tiled=True)]
    half = shard.shape[0] // 2
    from_x = xor_shift(shard, "dp", 2)
    from_y = xor_shift(shard, "dp", 4)
    far_1 = xor_shift(from_y[:half], "dp", 2)
    far_2 = xor_shift(from_x[half:], "dp", 4)
    far = jnp.concatenate([far_1, far_2], axis=0)
    near = xor_shift(shard, "dp", 1)
    near_x = xor_shift(from_x, "dp", 1)
    near_y = xor_shift(from_y, "dp", 1)
    near_far = xor_shift(far, "dp", 1)
    out = []
    for own, x, f, y in ((shard, from_x, far, from_y), (near, near_x, near_far, near_y)):
        out += [own, x[half:], x[:half], f, y[half:], y[:half]]
    return out


def join(pieces, start, stop):
    return jnp.concatenate([p[:, start:stop] for p in pieces], axis=0)


def dp_scatter(make):
    away = make(1)
    came = xor_shift(away, "dp", 1)
    kept = make(0)
    rows = kept.shape[0] // 4
    half = rows // 2

    def summed(start, stop):
        return kept[start:stop].astype(F32) + came[start:stop].astype(F32)

    first_x = xor_shift(summed(rows + half, 2 * rows + half).astype(BF16), "dp", 2)
    first_y = xor_shift(summed(2 * rows + half, 3 * rows + half).astype(BF16), "dp", 4)
    last_x = summed(rows, rows + half) + first_y[:half].astype(F32)
    last_y = summed(3 * rows + half, 4 * rows) + first_x[half:].astype(F32)
    last_x = xor_shift(last_x.astype(BF16), "dp", 2)
    last_y = xor_shift(last_y.astype(BF16), "dp", 4)
    top = summed(0, half) + first_x[:half].astype(F32) + last_y.astype(F32)
    low = summed(half, rows) + first_y[half:].astype(F32) + last_x.astype(F32)
    return jnp.concatenate([top, low], axis=0)


def weight_grad(rows, columns):
    def make(part):
        width = rows.shape[1] // 2
        chosen = rows[:, part * width : (part + 1) * width]
        return jnp.einsum("nd,nf->df", chosen, columns, preferred_element_type=F32).astype(BF16)

    if fast_dp():
        return dp_scatter(make)
    whole = jnp.einsum("nd,nf->df", rows, columns, preferred_element_type=F32).astype(BF16)
    return lax.psum_scatter(whole, "dp", scatter_dimension=0, tiled=True).astype(F32)


def line_gather(block):
    size = lax.axis_size("tensor")
    me = lax.axis_index("tensor")
    up = down = block
    ups, downs = [block], [block]
    for s in range(size - 1):
        up = lax.ppermute(up, "tensor", [(i, i + 1) for i in range(s, size - 1)])
        down = lax.ppermute(down, "tensor", [(i + 1, i) for i in range(size - 1 - s)])
        ups.append(up)
        downs.append(down)
    blocks = [block]
    for r in range(1, size):
        blocks.append(jnp.where(me + r < size, downs[r], ups[size - r]))
    return jnp.concatenate(blocks, axis=0)


def line_scatter(terms):
    size = lax.axis_size("tensor")
    rows = terms.shape[0] // size

    def block(r):
        return terms[r * rows : (r + 1) * rows]

    up = down = None
    for s in range(1, size):
        to_up, to_down = block(size - s), block(s)
        if s > 1:
            to_up = (to_up.astype(F32) + up.astype(F32)).astype(BF16)
            to_down = (to_down.astype(F32) + down.astype(F32)).astype(BF16)
        up = lax.ppermute(to_up, "tensor", [(i, i + 1) for i in range(s)])
        down = lax.ppermute(to_down, "tensor", [(i, i - 1) for i in range(size - s, size)])
    return block(0).astype(F32) + up.astype(F32) + down.astype(F32)


def turn(values, cosine, low_sine, high_sine, sign):
    half = ROT // 2
    lanes = cosine.shape[-1]
    head = values[:, :lanes]
    turned = (
        head * cosine
        - sign * pltpu.roll(head, lanes - half, 1) * low_sine
        + sign * pltpu.roll(head, half, 1) * high_sine
    )
    return jnp.concatenate([turned, values[:, lanes:]], axis=1)


def contract(a, b, dims):
    return lax.dot_general(a, b, (dims, ((), ())), preferred_element_type=F32)


def masked(scores, column_starts, row_starts, query_block, block):
    keys = scores.shape[1]
    query = lax.broadcasted_iota(jnp.int32, scores.shape, 0) + query_block * block
    key = lax.broadcasted_iota(jnp.int32, scores.shape, 1)
    allowed = (column_starts == row_starts[:, :keys]) & (key <= query)
    return allowed, jnp.where(allowed, scores, -1e30)


SMALL = pl.CostEstimate(flops=1000, bytes_accessed=1000, transcendentals=0)


def spots(me_ref, size, block):
    def spot(b):
        return pl.ds(pl.multiple_of(lax.rem(b - me_ref[0] + size, size) * block, block), block)

    return spot


def forward_block(q_out, k_out, v_out, att_ref, log_ref, col_ref, row_ref, spot, b, block):
    scale = q_out.shape[-1] ** (-0.5)
    here = slice(b * block, (b + 1) * block)
    query = q_out[spot(b), :]
    scores = jnp.concatenate(
        [contract(query, k_out[spot(c), :], ((1,), (1,))) for c in range(b + 1)], axis=1
    ) * scale
    _, scores = masked(scores, col_ref[here, :1], row_ref[:1, :], b, block)
    top = jnp.max(scores, axis=1, keepdims=True)
    powers = jnp.exp(scores - top)
    total = jnp.sum(powers, axis=1, keepdims=True)
    weights = (powers / total).astype(BF16)
    attended = contract(weights[:, :block], v_out[spot(0), :], ((1,), (0,)))
    for c in range(1, b + 1):
        attended = attended + contract(
            weights[:, c * block : (c + 1) * block], v_out[spot(c), :], ((1,), (0,))
        )
    att_ref[spot(b), :] = attended.astype(BF16)
    log_ref[0, here, :] = jnp.broadcast_to(top + jnp.log(total), (block, log_ref.shape[2]))


def forward_kernel(
    me_ref, q_ref, k_ref, v_ref, cos_ref, low_ref, high_ref, col_ref, row_ref,
    q_out, k_out, v_out, att_ref, log_ref, *, size, block,
):
    spot = spots(me_ref, size, block)
    for b in range(size):
        here = slice(b * block, (b + 1) * block)
        at = spot(b)
        tables = cos_ref[here, :], low_ref[here, :], high_ref[here, :]
        q_out[at, :] = turn(q_ref[at, :], *tables, 1.0).astype(BF16)
        k_out[at, :] = turn(k_ref[at, :], *tables, 1.0).astype(BF16)
        v_out[at, :] = v_ref[at, :].astype(BF16)
    for b in range(size):
        forward_block(q_out, k_out, v_out, att_ref, log_ref, col_ref, row_ref, spot, b, block)


def joined_forward_kernel(
    me_ref, rows_ref, qa_ref, ka_ref, va_ref, qb_ref, kb_ref, vb_ref, q_bias, k_bias, v_bias,
    cos_ref, low_ref, high_ref, col_ref, row_ref,
    q_out, k_out, v_out, att_ref, log_ref, *, size, block,
):
    spot = spots(me_ref, size, block)
    middle = qa_ref.shape[0]
    for b in range(size):
        here = slice(b * block, (b + 1) * block)
        at = spot(b)
        tables = cos_ref[here, :], low_ref[here, :], high_ref[here, :]
        top, low = rows_ref[at, :middle], rows_ref[at, middle:]

        def project(one, two, bias):
            return contract(top, one[:, :], ((1,), (0,))) + contract(low, two[:, :], ((1,), (0,))) + bias[:, :]

        q_out[at, :] = turn(project(qa_ref, qb_ref, q_bias), *tables, 1.0).astype(BF16)
        k_out[at, :] = turn(project(ka_ref, kb_ref, k_bias), *tables, 1.0).astype(BF16)
        v_out[at, :] = project(va_ref, vb_ref, v_bias).astype(BF16)
        forward_block(q_out, k_out, v_out, att_ref, log_ref, col_ref, row_ref, spot, b, block)


def backward_pass(
    q_ref, k_ref, v_ref, g_ref, log_ref, cos_ref, low_ref, high_ref, col_ref, row_ref,
    put, k_acc, v_acc, spot, size, block,
):
    scale = q_ref.shape[-1] ** (-0.5)
    for b in range(size):
        here = slice(b * block, (b + 1) * block)
        query, grad = q_ref[spot(b), :], g_ref[spot(b), :]
        scores = jnp.concatenate(
            [contract(query, k_ref[spot(c), :], ((1,), (1,))) for c in range(b + 1)], axis=1
        ) * scale
        allowed, scores = masked(scores, col_ref[here, :1], row_ref[:1, :], b, block)
        probs = jnp.where(allowed, jnp.exp(scores - log_ref[0, here, :1]), 0.0)
        grad_probs = jnp.concatenate(
            [contract(grad, v_ref[spot(c), :], ((1,), (1,))) for c in range(b + 1)], axis=1
        )
        inner = jnp.sum(probs * grad_probs, axis=1, keepdims=True)
        weights = probs.astype(BF16)
        grad_scores = (probs * (grad_probs - inner)).astype(BF16)
        back = None
        for c in range(b + 1):
            part = slice(c * block, (c + 1) * block)
            key_term = contract(grad_scores[:, part], query, ((0,), (0,)))
            value_term = contract(weights[:, part], grad, ((0,), (0,)))
            query_term = contract(grad_scores[:, part], k_ref[spot(c), :], ((1,), (0,)))
            back = query_term if c == 0 else back + query_term
            if c == b:
                k_acc[part, :] = key_term
                v_acc[part, :] = value_term
            else:
                k_acc[part, :] += key_term
                v_acc[part, :] += value_term
        tables = cos_ref[here, :], low_ref[here, :], high_ref[here, :]
        put(0, spot(b), turn(back * scale, *tables, -1.0).astype(BF16))
    for b in range(size):
        here = slice(b * block, (b + 1) * block)
        tables = cos_ref[here, :], low_ref[here, :], high_ref[here, :]
        put(1, spot(b), turn(k_acc[here, :] * scale, *tables, -1.0).astype(BF16))
        put(2, spot(b), v_acc[here, :].astype(BF16))


def backward_kernel(
    me_ref, q_ref, k_ref, v_ref, g_ref, log_ref, cos_ref, low_ref, high_ref, col_ref, row_ref,
    dq_ref, dk_ref, dv_ref, k_acc, v_acc, *, size, block,
):
    outs = (dq_ref, dk_ref, dv_ref)

    def put(k, at, value):
        outs[k][at, :] = value

    backward_pass(
        q_ref, k_ref, v_ref, g_ref, log_ref, cos_ref, low_ref, high_ref, col_ref, row_ref,
        put, k_acc, v_acc, spots(me_ref, size, block), size, block,
    )


def mixed_backward_kernel(
    me_ref, q_ref, k_ref, v_ref, g_ref, a_ref, b_ref, log_ref, cos_ref, low_ref, high_ref, col_ref, row_ref,
    d_ref, k_acc, v_acc, g_acc, *, size, block, heads,
):
    middle = a_ref.shape[0]
    head = q_ref.shape[1]
    for b in range(size):
        here = slice(b * block, (b + 1) * block)
        g_acc[here, :] = (
            contract(g_ref[here, :middle], a_ref[:, :], ((1,), (0,)))
            + contract(g_ref[here, middle:], b_ref[:, :], ((1,), (0,)))
        ).astype(BF16)
    h = pl.program_id(0)

    def put(k, at, value):
        d_ref[at, pl.ds(pl.multiple_of((k * heads + h) * head, head), head)] = value

    backward_pass(
        q_ref, k_ref, v_ref, g_acc, log_ref, cos_ref, low_ref, high_ref, col_ref, row_ref,
        put, k_acc, v_acc, spots(me_ref, size, block), size, block,
    )


def hidden_kernel(rows_ref, a_ref, b_ref, bias_ref, act_ref, slope_ref, *, step):
    middle = a_ref.shape[0]
    for i in range(rows_ref.shape[0] // step):
        here = slice(i * step, (i + 1) * step)
        hidden = contract(rows_ref[here, :middle], a_ref[:, :], ((1,), (0,)))
        hidden = hidden + contract(rows_ref[here, middle:], b_ref[:, :], ((1,), (0,))) + bias_ref[:, :]
        bell = lax.erf(hidden * (0.5**0.5))
        act_ref[here, :] = (0.5 * hidden * (1.0 + bell)).astype(BF16)
        slope = 0.5 * (1.0 + bell) + hidden * jnp.exp(-0.5 * hidden * hidden) * 0.3989422804014327
        slope_ref[here, :] = slope.astype(BF16)


def hidden_half(rows, top, low, bias):
    count, width = rows.shape
    out = top.shape[1]
    tile = 512
    half = pl.BlockSpec((top.shape[0], tile), lambda j: (0, j))
    made = pl.BlockSpec((count, tile), lambda j: (0, j))
    return pl.pallas_call(
        functools.partial(hidden_kernel, step=256),
        out_shape=(jax.ShapeDtypeStruct((count, out), BF16),) * 2,
        grid=(out // tile,),
        in_specs=[
            pl.BlockSpec((count, width), lambda j: (0, 0)), half, half, pl.BlockSpec((1, tile), lambda j: (0, j))
        ],
        out_specs=(made, made),
        cost_estimate=SMALL,
        name="hidden",
    )(rows, top, low, bias.reshape(1, -1))


def slope_kernel(rows_ref, a_ref, b_ref, slope_ref, out_ref, *, step):
    middle = a_ref.shape[0]
    for i in range(rows_ref.shape[0] // step):
        here = slice(i * step, (i + 1) * step)
        active = contract(rows_ref[here, :middle], a_ref[:, :], ((1,), (0,)))
        active = active + contract(rows_ref[here, middle:], b_ref[:, :], ((1,), (0,)))
        out_ref[here, :] = (active * slope_ref[here, :].astype(F32)).astype(BF16)


def hidden_back(rows, top, low, slope):
    count, width = rows.shape
    out = top.shape[1]
    tile = 512
    half = pl.BlockSpec((top.shape[0], tile), lambda j: (0, j))
    made = pl.BlockSpec((count, tile), lambda j: (0, j))
    return pl.pallas_call(
        functools.partial(slope_kernel, step=256),
        out_shape=jax.ShapeDtypeStruct((count, out), BF16),
        grid=(out // tile,),
        in_specs=[pl.BlockSpec((count, width), lambda j: (0, 0)), half, half, made],
        out_specs=made,
        cost_estimate=SMALL,
        name="hidden_back",
    )(rows, top, low, slope)


def branch_kernel(att_ref, mix_ref, act_ref, down_ref, out_ref, *, step):
    for i in range(att_ref.shape[0] // step):
        here = slice(i * step, (i + 1) * step)
        total = contract(att_ref[here, :], mix_ref[:, :], ((1,), (1,)))
        total = total + contract(act_ref[here, :], down_ref[:, :], ((1,), (1,)))
        out_ref[here, :] = total.astype(BF16)


def branch_half(attended, mixed, activated, down):
    count, inner = attended.shape
    units = activated.shape[1]
    width = down.shape[0]
    tile = 256
    spot = mixed.shape[1] // inner - 1
    return pl.pallas_call(
        functools.partial(branch_kernel, step=256),
        out_shape=jax.ShapeDtypeStruct((count, width), BF16),
        grid=(width // tile,),
        in_specs=[
            pl.BlockSpec((count, inner), lambda j: (0, 0)),
            pl.BlockSpec((tile, inner), lambda j: (j, spot)),
            pl.BlockSpec((count, units), lambda j: (0, 0)),
            pl.BlockSpec((tile, units), lambda j: (j, 0)),
        ],
        out_specs=pl.BlockSpec((count, tile), lambda j: (0, j)),
        cost_estimate=SMALL,
        name="branches",
    )(attended, mixed, activated, down)


def back_kernel(
    hid_ref, proj_ref, up_ref, join_ref, tok_ref, mean_ref, scale_ref, gain_ref, back_ref, sum_ref, *, step
):
    sums = [0.0] * 4
    for i in range(hid_ref.shape[0] // step):
        here = slice(i * step, (i + 1) * step)
        two = contract(hid_ref[here, :], up_ref[:, :], ((1,), (1,)))
        one = contract(proj_ref[here, :], join_ref[:, :], ((1,), (1,)))
        back_ref[here, :] = (one * gain_ref[:1, :] + two * gain_ref[1:2, :]).astype(BF16)
        xhat = (tok_ref[here, :].astype(F32) - mean_ref[here, :1]) * scale_ref[here, :1]
        for k, term in enumerate((one * xhat, two * xhat, one, two)):
            sums[k] = sums[k] + jnp.sum(term, axis=0, keepdims=True)
    for k in range(4):
        sum_ref[k : k + 1, :] = sums[k]


def back_half(grad_hidden, grad_projected, up, mixed, token_rows, mean, scale, gains, part):
    count, units = grad_hidden.shape
    joined = grad_projected.shape[1]
    width = up.shape[0]
    tile = 256
    tiles = width // tile
    whole = lambda j: (0, 0)
    return pl.pallas_call(
        functools.partial(back_kernel, step=256),
        out_shape=(jax.ShapeDtypeStruct((count, width), BF16), jax.ShapeDtypeStruct((8, width), F32)),
        grid=(tiles,),
        in_specs=[
            pl.BlockSpec((count, units), whole),
            pl.BlockSpec((count, joined), whole),
            pl.BlockSpec((tile, units), lambda j: (j, 0)),
            pl.BlockSpec((tile, joined), lambda j: (j, 0)),
            pl.BlockSpec((count, tile), lambda j: (0, j + part * tiles)),
            pl.BlockSpec((count, 128), whole),
            pl.BlockSpec((count, 128), whole),
            pl.BlockSpec((2, tile), lambda j: (0, j + part * tiles)),
        ],
        out_specs=(pl.BlockSpec((count, tile), lambda j: (0, j)), pl.BlockSpec((8, tile), lambda j: (0, j))),
        cost_estimate=SMALL,
        name="back",
    )(grad_hidden, grad_projected, up, mixed, token_rows, mean, scale, gains)


def joined_forward(rows, top, low, bias, tables, me, heads, head, size):
    count, width = rows.shape
    block = count // size
    whole = lambda h, s: (0, 0)
    table_specs = [pl.BlockSpec((count, 128), whole)] * 4 + [pl.BlockSpec((8, count), whole)]
    by_head = pl.BlockSpec((count, head), lambda h, s: (0, h))
    wide = jax.ShapeDtypeStruct((count, heads * head), BF16)

    def thirds(n):
        return [pl.BlockSpec((n, head), lambda h, s, k=k: (0, k * heads + h)) for k in range(3)]

    return pl.pallas_call(
        functools.partial(joined_forward_kernel, size=size, block=block),
        out_shape=(wide, wide, wide, wide, jax.ShapeDtypeStruct((heads, count, 128), F32)),
        grid_spec=pltpu.PrefetchScalarGridSpec(
            num_scalar_prefetch=1,
            grid=(heads,),
            in_specs=[pl.BlockSpec((count, width), whole)]
            + thirds(top.shape[0]) + thirds(low.shape[0]) + thirds(1) + table_specs,
            out_specs=(by_head,) * 4 + (pl.BlockSpec((1, count, 128), lambda h, s: (h, 0, 0)),),
        ),
        cost_estimate=SMALL,
        name="joined_forward",
    )(me, rows, top, top, top, low, low, low, bias, bias, bias, *tables)


def mixed_backward(queries, keys, values, grads, top, low, log_total, tables, me, heads, size):
    count = queries.shape[0]
    head = queries.shape[1] // heads
    block = count // size
    whole = lambda h, s: (0, 0)
    table_specs = [pl.BlockSpec((count, 128), whole)] * 4 + [pl.BlockSpec((8, count), whole)]
    by_head = pl.BlockSpec((count, head), lambda h, s: (0, h))
    mix = pl.BlockSpec((top.shape[0], head), lambda h, s: (0, 3 * heads + h))
    return pl.pallas_call(
        functools.partial(mixed_backward_kernel, size=size, block=block, heads=heads),
        out_shape=jax.ShapeDtypeStruct((count, 3 * heads * head), BF16),
        grid_spec=pltpu.PrefetchScalarGridSpec(
            num_scalar_prefetch=1,
            grid=(heads,),
            in_specs=[by_head] * 3
            + [pl.BlockSpec((count, grads.shape[1]), whole), mix, mix]
            + [pl.BlockSpec((1, count, 128), lambda h, s: (h, 0, 0))]
            + table_specs,
            out_specs=pl.BlockSpec((count, 3 * heads * head), whole),
            scratch_shapes=[pltpu.VMEM((count, head), F32)] * 2 + [pltpu.VMEM((count, head), BF16)],
        ),
        cost_estimate=SMALL,
        name="mixed_backward",
    )(me, queries, keys, values, grads, top, low, log_total, *tables)


def attention_tables(positions, starts):
    half = ROT // 2
    frequency = ROTARY_BASE ** (-(jnp.arange(half, dtype=F32) * 2.0) / ROT)
    angles = positions.astype(F32)[:, None] * frequency[None, :]
    cosine, sine = jnp.cos(angles), jnp.sin(angles)
    rows = positions.shape[0]
    cosines = jnp.concatenate([cosine, cosine, jnp.ones((rows, 128 - ROT), F32)], axis=1)
    low = jnp.concatenate([sine, jnp.zeros((rows, 128 - half), F32)], axis=1)
    high = jnp.concatenate([jnp.zeros((rows, half), F32), sine, jnp.zeros((rows, 128 - ROT), F32)], axis=1)
    columns = jnp.broadcast_to(starts[:, None], (rows, 128))
    across = jnp.broadcast_to(starts[None, :], (8, rows))
    return cosines, low, high, columns, across


def attention_forward(projected, tables, me, heads, size):
    rows = projected.shape[0]
    head = projected.shape[1] // (3 * heads)
    block = rows // size
    whole = lambda h, s: (0, 0)
    table_specs = [pl.BlockSpec((rows, 128), whole)] * 4 + [pl.BlockSpec((8, rows), whole)]
    by_head = pl.BlockSpec((rows, head), lambda h, s: (0, h))
    wide = jax.ShapeDtypeStruct((rows, heads * head), BF16)
    return pl.pallas_call(
        functools.partial(forward_kernel, size=size, block=block),
        out_shape=(wide, wide, wide, wide, jax.ShapeDtypeStruct((heads, rows, 128), F32)),
        grid_spec=pltpu.PrefetchScalarGridSpec(
            num_scalar_prefetch=1,
            grid=(heads,),
            in_specs=[
                pl.BlockSpec((rows, head), lambda h, s, k=k: (0, k * heads + h)) for k in range(3)
            ]
            + table_specs,
            out_specs=(by_head,) * 4 + (pl.BlockSpec((1, rows, 128), lambda h, s: (h, 0, 0)),),
        ),
        cost_estimate=pl.CostEstimate(
            flops=heads * rows * rows * head * 40, bytes_accessed=rows * head * heads * 24,
            transcendentals=heads * rows * rows // 2,
        ),
        name="attention_forward",
    )(me, projected, projected, projected, *tables)


def attention_backward(queries, keys, values, grads, log_total, tables, me, heads, size):
    rows = queries.shape[0]
    head = queries.shape[1] // heads
    block = rows // size
    whole = lambda h, s: (0, 0)
    table_specs = [pl.BlockSpec((rows, 128), whole)] * 4 + [pl.BlockSpec((8, rows), whole)]
    by_head = pl.BlockSpec((rows, head), lambda h, s: (0, h))
    wide = jax.ShapeDtypeStruct((rows, heads * head), BF16)
    return pl.pallas_call(
        functools.partial(backward_kernel, size=size, block=block),
        out_shape=(wide, wide, wide),
        grid_spec=pltpu.PrefetchScalarGridSpec(
            num_scalar_prefetch=1,
            grid=(heads,),
            in_specs=[by_head] * 4
            + [pl.BlockSpec((1, rows, 128), lambda h, s: (h, 0, 0))]
            + table_specs,
            out_specs=(by_head,) * 3,
            scratch_shapes=[pltpu.VMEM((rows, head), F32)] * 2,
        ),
        cost_estimate=pl.CostEstimate(
            flops=heads * rows * rows * head * 60, bytes_accessed=rows * head * heads * 24,
            transcendentals=heads * rows * rows // 2,
        ),
        name="attention_backward",
    )(me, queries, keys, values, grads, log_total, *tables)


def standardize(values):
    values = values.astype(F32)
    centered = values - jnp.mean(values, axis=-1, keepdims=True)
    spread = jnp.mean(centered * centered, axis=-1, keepdims=True)
    scale = lax.rsqrt(spread + EPSILON)
    return centered * scale, scale


def norm_rows(token_rows, gain_rows, shift_rows):
    xhat, _ = standardize(token_rows)
    first_rows = (xhat * gain_rows[0] + shift_rows[0]).astype(BF16)
    second_rows = (xhat * gain_rows[1] + shift_rows[1]).astype(BF16)
    return first_rows, second_rows


def hidden_units(second_rows, up_rows, hidden_bias):
    hidden = jnp.dot(second_rows, up_rows, preferred_element_type=F32) + hidden_bias
    bell = lax.erf(hidden * (0.5**0.5))
    activated = (0.5 * hidden * (1.0 + bell)).astype(BF16)
    slope = 0.5 * (1.0 + bell) + hidden * jnp.exp(-0.5 * hidden * hidden) * 0.3989422804014327
    return activated, slope.astype(BF16)


def branch_rows(attended, mix_rows, activated, down_rows):
    return (
        jnp.einsum("ne,de->nd", attended, mix_rows, preferred_element_type=F32)
        + jnp.einsum("nf,df->nd", activated, down_rows, preferred_element_type=F32)
    ).astype(BF16)


def hidden_grads(grad_rows, down_rows, slope):
    grad_active = jnp.einsum("nd,df->nf", grad_rows, down_rows, preferred_element_type=F32)
    return (grad_active * slope.astype(F32)).astype(BF16)


def attended_grads(grad_rows, mix_rows):
    return jnp.einsum("nd,de->ne", grad_rows, mix_rows, preferred_element_type=F32).astype(BF16)


def back_rows(grads, weight_rows):
    return jnp.einsum("nf,df->nd", grads, weight_rows, preferred_element_type=F32)


def grad_half(rows, columns, part):
    width = rows.shape[1] // 2
    chosen = rows[:, part * width : (part + 1) * width]
    return jnp.einsum("nd,nf->df", chosen, columns, preferred_element_type=F32).astype(BF16)


def plus(*terms):
    return functools.reduce(lambda a, b: a + b, [t.astype(F32) for t in terms])


def width_sums(grad_first, grad_second, xhat, grad_local):
    return jnp.stack(
        [
            jnp.sum(grad_first * xhat, axis=0),
            jnp.sum(grad_second * xhat, axis=0),
            jnp.sum(grad_first, axis=0),
            jnp.sum(grad_second, axis=0),
            jnp.sum(grad_local.astype(F32), axis=0),
        ],
        axis=0,
    )


def shards(
    tokens,
    seq_start,
    proj_weight,
    proj_bias,
    out_weight,
    up_weight,
    up_bias,
    down_weight,
    norm_gains,
    biases,
    cotangent,
):
    local_rows, width = tokens.shape
    n_dp, n_tensor = lax.axis_size("dp"), lax.axis_size("tensor")
    dp_index, tensor_index = lax.axis_index("dp"), lax.axis_index("tensor")
    row_count = local_rows * n_tensor
    hidden_width = up_weight.shape[1]
    heads_here = proj_bias.shape[1]
    head_size = proj_bias.shape[2] * n_dp
    local_width = heads_here * head_size
    joined_width = 3 * local_width
    columns = norm_gains.shape[1]

    vectors = jnp.concatenate(
        [norm_gains.reshape(1, -1), biases.reshape(1, -1), proj_bias.reshape(1, -1), up_bias.reshape(1, -1)],
        axis=1,
    )
    table = jnp.zeros((n_dp * n_tensor, vectors.shape[1]), BF16)
    table = lax.dynamic_update_slice(table, vectors, (dp_index * n_tensor + tensor_index, 0))
    local_tokens, local_grads = to_frame(tokens), to_frame(cotangent)
    positions = dp_index * row_count + jnp.arange(row_count, dtype=jnp.int32) - seq_start
    tables = attention_tables(positions, seq_start)
    me = tensor_index.astype(jnp.int32).reshape(1)
    flat_proj = proj_weight.reshape(-1, joined_width)

    def small_parameters(table):
        six_rows = table[:, : 6 * columns].reshape(n_dp * n_tensor, 6, columns).transpose(1, 0, 2)
        six_rows = to_frame(six_rows.reshape(6, width).astype(F32))
        of_tensor = lax.dynamic_index_in_dim(
            table[:, 6 * columns :].reshape(n_dp, n_tensor, -1), tensor_index, 1, keepdims=False
        ).astype(F32)
        joined_bias = (
            of_tensor[:, : proj_bias.size]
            .reshape(n_dp, 3, heads_here, -1)
            .transpose(1, 2, 0, 3)
            .reshape(joined_width)
        )
        hidden_bias = of_tensor[:, proj_bias.size :].reshape(hidden_width)
        return six_rows[:2], six_rows[2:], joined_bias, hidden_bias

    def attend(first_rows, joined_rows, joined_bias):
        projected = jnp.dot(first_rows, joined_rows, preferred_element_type=F32) + joined_bias
        return attention_forward(projected, tables, me, heads_here, n_tensor)

    def attend_back(kept, grad_attended):
        queries, keys, values, log_total = kept
        backs = attention_backward(
            queries, keys, values, grad_attended, log_total, tables, me, heads_here, n_tensor
        )
        return jnp.concatenate(backs, axis=1)

    def finish_output(branches, shift_rows):
        output = local_tokens.astype(F32) + branches + shift_rows[2] + shift_rows[3]
        return from_frame(output.astype(BF16))

    def finish_input_grad(back):
        xhat_local, scale_local = standardize(local_tokens)
        grad_norm_in = (
            back
            - jnp.mean(back, axis=-1, keepdims=True)
            - xhat_local * jnp.mean(back * xhat_local, axis=-1, keepdims=True)
        ) * scale_local
        return from_frame(local_grads.astype(F32) + grad_norm_in)

    def small_shares(five, joined_bias_sums, up_bias_sums):
        five = five.reshape(5, width)
        mine = lax.dynamic_slice_in_dim(
            five, (dp_index * n_tensor + tensor_index) * columns, columns, 1
        )
        biases_grad = jnp.concatenate([mine[2:], mine[4:]], axis=0)
        joined_bias_sum = lax.dynamic_slice_in_dim(
            joined_bias_sums.reshape(3, heads_here, head_size),
            dp_index * proj_bias.shape[2],
            proj_bias.shape[2],
            2,
        )
        up_bias_sum = lax.dynamic_slice_in_dim(
            up_bias_sums.reshape(1, -1), dp_index * up_bias.shape[1], up_bias.shape[1], 1
        )
        return mine[:2], biases_grad, joined_bias_sum, up_bias_sum

    def small_grads(five, joined_bias_term, up_bias_term):
        five = from_frame(five).reshape(1, -1)
        terms = jnp.concatenate([five, joined_bias_term[None], up_bias_term[None]], axis=1)
        terms = butterfly(terms, "dp")
        five = butterfly(terms[:, : 5 * width], "tensor")
        return small_shares(
            five, terms[0, 5 * width : 5 * width + joined_width], terms[:, 5 * width + joined_width :]
        )

    def plain():
        token_rows, grad_rows = line_gather(local_tokens), line_gather(local_grads)
        up_rows, down_rows = dp_gather(up_weight), dp_gather(down_weight.T)
        joined_rows, mix_rows = dp_gather(flat_proj), dp_gather(out_weight.T)
        up_rows, down_rows, joined_rows, mix_rows = (
            join(w, 0, None) for w in (up_rows, down_rows, joined_rows, mix_rows)
        )
        gain_rows, shift_rows, joined_bias, hidden_bias = small_parameters(
            butterfly(butterfly(table, "dp"), "tensor")
        )
        first_rows, second_rows = norm_rows(token_rows, gain_rows, shift_rows)
        activated, slope = cut(*hidden_units(second_rows, up_rows, hidden_bias))
        *kept, attended, log_total = attend(first_rows, joined_rows, joined_bias)
        branches = line_scatter(branch_rows(attended, mix_rows, activated, down_rows))
        output = finish_output(branches, shift_rows)
        grad_hidden = hidden_grads(grad_rows, down_rows, slope)
        down_sum = weight_grad(grad_rows, activated)
        up_sum = weight_grad(second_rows, grad_hidden)
        grad_second = back_rows(grad_hidden, up_rows)
        grad_attended = attended_grads(grad_rows, mix_rows)
        mix_sum = weight_grad(grad_rows, attended)
        grad_projected = attend_back((*kept, log_total), grad_attended)
        joined_sum = weight_grad(first_rows, grad_projected)
        grad_first = back_rows(grad_projected, joined_rows)
        back = grad_first * gain_rows[0] + grad_second * gain_rows[1]
        input_grad = finish_input_grad(line_scatter(back.astype(BF16)))
        five = width_sums(grad_first, grad_second, standardize(token_rows)[0], local_grads)
        small = small_grads(
            five, jnp.sum(grad_projected, axis=0, dtype=F32), jnp.sum(grad_hidden, axis=0, dtype=F32)
        )
        return output, input_grad, joined_sum, mix_sum, up_sum, down_sum, small

    def staged():
        half = local_rows // 2
        first, second = slice(0, half), slice(half, 2 * half)

        def x(values):
            return xor_shift(values, "dp", 2)

        def y(values):
            return xor_shift(values, "dp", 4)

        def core(values):
            return xor_shift(values, "dp", 1)

        def gather_step(up, down, s):
            up = lax.ppermute(up, "tensor", [(i, i + 1) for i in range(s, 3)])
            down = lax.ppermute(down, "tensor", [(i + 1, i) for i in range(3 - s)])
            return up, down

        def scatter_step(halves, up, down, s):
            def block(r):
                return jnp.concatenate([h[r * local_rows : (r + 1) * local_rows] for h in halves], axis=1)

            to_up, to_down = block(4 - s), block(s)
            if s > 1:
                to_up, to_down = plus(to_up, up).astype(BF16), plus(to_down, down).astype(BF16)
            up = lax.ppermute(to_up, "tensor", [(i, i + 1) for i in range(s)])
            down = lax.ppermute(to_down, "tensor", [(i, i - 1) for i in range(4 - s, 4)])
            return up, down

        def in_turn(block, ups, downs):
            blocks = [block] + [
                jnp.where(tensor_index + r < 4, downs[r - 1], ups[3 - r]) for r in range(1, 4)
            ]
            return jnp.concatenate(blocks, axis=0)

        def pair(top, low):
            return jnp.concatenate([top, low], axis=0)

        def lay(own, from_x, far_x, far_y, from_y):
            return jnp.concatenate(
                [own, from_x[second], from_x[first], far_x, far_y, from_y[second], from_y[first]], axis=0
            )

        wa = up_weight
        wb = jnp.concatenate([flat_proj, out_weight.T], axis=1)
        wc = down_weight.T

        tu1, td1 = gather_step(local_tokens, local_tokens, 0)
        table1 = table + core(table)
        table1 = table1 + x(table1) + y(table1) + xor_shift(table1, "dp", 6)
        wa1, table1 = cut(wa, table1)
        ax, ay = x(wa1), y(wa1)
        table1 = table1 + xor_shift(table1, "tensor", 1)
        tu1, td1, ax, ay, table1, wb, wc, tables1 = cut(tu1, td1, ax, ay, table1, wb, wc, tables)
        tu2, td2 = gather_step(tu1, td1, 1)
        p2x, p2y = x(pair(ay[first], wb[second])), y(pair(ax[second], wb[first]))
        table2 = table1 + xor_shift(table1, "tensor", 2)
        tu2, td2, p2x, p2y, table2 = cut(tu2, td2, p2x, p2y, table2)
        tu3, td3 = gather_step(tu2, td2, 2)
        p3x, p3y = x(pair(p2y[second], wb[first])), y(pair(p2x[second], wb[second]))
        up_1 = lay(wa, ax, p2x[first], p2y[first], ay)
        up_2 = core(up_1)
        gain_rows, shift_rows, joined_bias, hidden_bias = small_parameters(table2)
        tu3, td3, p3x, p3y, up_1, up_2, local_grads1, gain_rows, shift_rows = cut(
            tu3, td3, p3x, p3y, up_1, up_2, local_grads, gain_rows, shift_rows
        )
        cu1, cd1 = gather_step(local_grads1, local_grads1, 0)
        cx, cy = x(wc), y(wc)
        mix_1 = pair(
            jnp.concatenate([wb, p2x[second], p3x[second], p3x[first]], axis=0),
            jnp.concatenate([p3y[first], p3y[second], p2y[second]], axis=0),
        )
        mix_2 = core(mix_1)
        token_rows = in_turn(local_tokens, (tu1, tu2, tu3), (td1, td2, td3))
        first_rows, second_rows = norm_rows(token_rows, gain_rows, shift_rows)
        activated, slope = hidden_half(second_rows, up_1, up_2, hidden_bias)
        cu1, cd1, cx, cy, mix_1, mix_2, first_rows, activated, slope = cut(
            cu1, cd1, cx, cy, mix_1, mix_2, first_rows, activated, slope
        )
        cu2, cd2 = gather_step(cu1, cd1, 1)
        fcx, fcy = x(cy[first]), y(cx[second])
        *kept, attended, log_total = joined_forward(
            first_rows, mix_1, mix_2, joined_bias.reshape(1, -1), tables1, me, heads_here, head_size, n_tensor
        )
        cu2, cd2, fcx, fcy, attended = cut(cu2, cd2, fcx, fcy, attended)
        cu3, cd3 = gather_step(cu2, cd2, 2)
        down_1 = lay(wc, cx, fcx, fcy, cy)
        down_2 = core(down_1)
        branch_1 = branch_half(attended, mix_1, activated, down_1)
        branch_2 = branch_half(attended, mix_2, activated, down_2)
        cu3, cd3, branch_1, branch_2, activated = cut(cu3, cd3, branch_1, branch_2, activated)
        branches = (branch_1, branch_2)
        bu, bd = scatter_step(branches, None, None, 1)
        grad_rows = in_turn(local_grads1, (cu1, cu2, cu3), (cd1, cd2, cd3))
        came_d = core(grad_half(grad_rows, activated, 1))
        keep_d = grad_half(grad_rows, activated, 0)
        grad_hidden = hidden_back(grad_rows, down_1, down_2, slope)
        bu, bd, came_d, keep_d, grad_hidden, grad_rows = cut(
            bu, bd, came_d, keep_d, grad_hidden, grad_rows
        )

        def at(keep, came, start, stop):
            return plus(keep[start * half : stop * half], came[start * half : stop * half])

        bu, bd = scatter_step(branches, bu, bd, 2)
        d1x = x(at(keep_d, came_d, 3, 5).astype(BF16))
        d1y = y(at(keep_d, came_d, 5, 7).astype(BF16))
        came_u = core(grad_half(second_rows, grad_hidden, 1))
        keep_u = grad_half(second_rows, grad_hidden, 0)
        grad_projected = mixed_backward(
            *kept, grad_rows, mix_1, mix_2, log_total, tables1, me, heads_here, n_tensor
        )
        bu, bd, d1x, d1y, came_u, keep_u, grad_projected, grad_hidden = cut(
            bu, bd, d1x, d1y, came_u, keep_u, grad_projected, grad_hidden
        )
        bu, bd = scatter_step(branches, bu, bd, 3)
        d2x = plus(at(keep_d, came_d, 2, 3), d1y[first]).astype(BF16)
        d2y = plus(at(keep_d, came_d, 7, 8), d1x[second]).astype(BF16)
        s9x = x(pair(d2x, at(keep_u, came_u, 4, 5).astype(BF16)))
        s9y = y(pair(d2y, at(keep_u, came_u, 5, 6).astype(BF16)))

        def joined_half(part):
            return jnp.concatenate(
                [grad_half(first_rows, grad_projected, part), grad_half(grad_rows, attended, part)], axis=1
            )

        came_j = core(joined_half(1))
        values = token_rows.astype(F32)
        mean = jnp.mean(values, axis=-1, keepdims=True)
        _, scale = standardize(token_rows)
        mean, scale = (jnp.broadcast_to(v, (row_count, 128)) for v in (mean, scale))
        back_1, sums_1 = back_half(grad_hidden, grad_projected, up_1, mix_1, token_rows, mean, scale, gain_rows, 0)
        back_2, sums_2 = back_half(grad_hidden, grad_projected, up_2, mix_2, token_rows, mean, scale, gain_rows, 1)
        bu, bd, s9x, s9y, came_j, back_1, back_2, sums_1, sums_2, grad_projected, attended = cut(
            bu, bd, s9x, s9y, came_j, back_1, back_2, sums_1, sums_2, grad_projected, attended
        )
        backs = (back_1, back_2)
        eu, ed = scatter_step(backs, None, None, 1)
        s10x = x(pair(plus(at(keep_u, came_u, 2, 3), s9y[second]), at(keep_u, came_u, 3, 4)).astype(BF16))
        s10y = y(pair(at(keep_u, came_u, 6, 7), plus(at(keep_u, came_u, 7, 8), s9x[second])).astype(BF16))
        five = jnp.concatenate(
            [
                jnp.concatenate([sums_1[:4], sums_2[:4]], axis=1),
                jnp.sum(local_grads.astype(F32), axis=0, keepdims=True),
            ],
            axis=0,
        )
        five = from_frame(five).reshape(1, -1)
        five = five + xor_shift(five, "tensor", 1)
        keep_j = joined_half(0)
        own = jnp.concatenate([h[:local_rows] for h in branches], axis=1)
        output = finish_output(plus(own, bu, bd), shift_rows)
        down_sum = pair(
            plus(at(keep_d, came_d, 0, 1), d1x[first], s9y[first]),
            plus(at(keep_d, came_d, 1, 2), d1y[second], s9x[first]),
        )
        eu, ed, s10x, s10y, keep_j, five = cut(eu, ed, s10x, s10y, keep_j, five)
        eu, ed = scatter_step(backs, eu, ed, 2)
        j1x = x(at(keep_j, came_j, 3, 5).astype(BF16))
        j1y = y(at(keep_j, came_j, 5, 7).astype(BF16))
        five = five + xor_shift(five, "tensor", 2)
        up_sum = pair(
            plus(at(keep_u, came_u, 0, 1), s10x[second], s10y[second]),
            plus(at(keep_u, came_u, 1, 2), s10x[first], s10y[first]),
        )
        terms = jnp.concatenate(
            [
                five,
                jnp.sum(grad_projected, axis=0, dtype=F32, keepdims=True),
                jnp.sum(grad_hidden, axis=0, dtype=F32, keepdims=True),
            ],
            axis=1,
        )
        eu, ed, j1x, j1y, terms = cut(eu, ed, j1x, j1y, terms)
        eu, ed = scatter_step(backs, eu, ed, 3)
        j2x = x(plus(at(keep_j, came_j, 2, 3), j1y[first]).astype(BF16))
        j2y = y(plus(at(keep_j, came_j, 7, 8), j1x[second]).astype(BF16))
        terms = butterfly(terms, "dp")
        small = small_shares(
            terms[:, : 5 * width], terms[0, 5 * width : 5 * width + joined_width],
            terms[:, 5 * width + joined_width :],
        )
        joined_mix = pair(
            plus(at(keep_j, came_j, 0, 1), j1x[first], j2y),
            plus(at(keep_j, came_j, 1, 2), j1y[second], j2x),
        )
        own = jnp.concatenate([h[:local_rows] for h in backs], axis=1)
        input_grad = finish_input_grad(plus(own, eu, ed))
        return (
            output, input_grad, joined_mix[:, :joined_width], joined_mix[:, joined_width:], up_sum, down_sum, small
        )

    parts = staged() if fast_dp() and n_tensor == 4 else plain()
    output, input_grad, joined_sum, mix_sum, up_sum, down_sum, small = parts
    gains_grad, biases_grad, joined_bias_sum, up_bias_sum = small
    return (
        output,
        input_grad,
        joined_sum.reshape(proj_weight.shape),
        joined_bias_sum,
        mix_sum.T,
        up_sum,
        up_bias_sum,
        down_sum.T,
        gains_grad,
        biases_grad,
    )


def solution(mesh):
    in_specs = (
        P(("dp", "tensor"), None),
        P("dp"),
        P("dp", None, "tensor"),
        P(None, "tensor", "dp"),
        P("tensor", "dp"),
        P("dp", "tensor"),
        P("tensor", "dp"),
        P("tensor", "dp"),
        P(None, ("dp", "tensor")),
        P(None, ("dp", "tensor")),
        P(("dp", "tensor"), None),
    )
    out_specs = (
        P(("dp", "tensor"), None),
        P(("dp", "tensor"), None),
        P("dp", None, "tensor"),
        P(None, "tensor", "dp"),
        P("tensor", "dp"),
        P("dp", "tensor"),
        P("tensor", "dp"),
        P("tensor", "dp"),
        P(None, ("dp", "tensor")),
        P(None, ("dp", "tensor")),
    )
    return jax.shard_map(shards, mesh=mesh, in_specs=in_specs, out_specs=out_specs, check_vma=False)
```

```python
import functools

import jax
import jax.numpy as jnp
from jax import lax
from jax.experimental import pallas as pl
from jax.experimental.pallas import tpu as pltpu
from jax.sharding import PartitionSpec as P

ROT = 64
EPSILON = 1e-05
ROTARY_BASE = 10000.0
F32 = jnp.float32
BF16 = jnp.bfloat16
HALVES = [(0, 0), (0, 1), (2, 1), (2, 0), (6, 0), (6, 1), (4, 1), (4, 0)]
ORDER = HALVES + [(p ^ 1, h) for p, h in HALVES]


def cut(*values):
    return lax.optimization_barrier(values)


def is_power(n):
    return n & (n - 1) == 0


def fast_dp():
    return lax.axis_size("dp") == 8


def xor_shift(values, axis, bit):
    size = lax.axis_size(axis)
    return lax.ppermute(values, axis, [(i, i ^ bit) for i in range(size)])


def butterfly(values, axis):
    size = lax.axis_size(axis)
    if not is_power(size):
        return lax.psum(values, axis)
    bit = 1
    while bit < size:
        values = values + xor_shift(values, axis, bit)
        bit *= 2
    return values


def columns_kernel(index_ref, x_ref, o_ref, *, count, step):
    for j in range(count):
        at = pl.multiple_of(index_ref[j] * step, step)
        o_ref[:, j * step : (j + 1) * step] = x_ref[:, pl.ds(at, step)]


def take_columns(values, index):
    rows, width = values.shape
    count = index.shape[0]
    tile = rows // 2 if rows % 64 == 0 else rows
    return pl.pallas_call(
        functools.partial(columns_kernel, count=count, step=width // count),
        out_shape=jax.ShapeDtypeStruct(values.shape, values.dtype),
        grid_spec=pltpu.PrefetchScalarGridSpec(
            num_scalar_prefetch=1,
            grid=(rows // tile,),
            in_specs=[pl.BlockSpec((tile, width), lambda i, s: (i, 0))],
            out_specs=pl.BlockSpec((tile, width), lambda i, s: (i, 0)),
        ),
        name="columns",
    )(index, values)


FRAME = [[(me ^ p) * 2 + h for p, h in ORDER] for me in range(8)]
PLAIN = [[row.index(k) for k in range(16)] for row in FRAME]


def frame_index():
    return lax.dynamic_index_in_dim(jnp.array(FRAME, jnp.int32), lax.axis_index("dp"), 0, keepdims=False)


def plain_index():
    return lax.dynamic_index_in_dim(jnp.array(PLAIN, jnp.int32), lax.axis_index("dp"), 0, keepdims=False)


def to_frame(values):
    return take_columns(values, frame_index()) if fast_dp() else values


def from_frame(values):
    return take_columns(values, plain_index()) if fast_dp() else values


def dp_gather(shard):
    if not fast_dp():
        return [lax.all_gather(shard, "dp", axis=0, tiled=True)]
    half = shard.shape[0] // 2
    from_x = xor_shift(shard, "dp", 2)
    from_y = xor_shift(shard, "dp", 4)
    far_1 = xor_shift(from_y[:half], "dp", 2)
    far_2 = xor_shift(from_x[half:], "dp", 4)
    far = jnp.concatenate([far_1, far_2], axis=0)
    near = xor_shift(shard, "dp", 1)
    near_x = xor_shift(from_x, "dp", 1)
    near_y = xor_shift(from_y, "dp", 1)
    near_far = xor_shift(far, "dp", 1)
    out = []
    for own, x, f, y in ((shard, from_x, far, from_y), (near, near_x, near_far, near_y)):
        out += [own, x[half:], x[:half], f, y[half:], y[:half]]
    return out


def join(pieces, start, stop):
    return jnp.concatenate([p[:, start:stop] for p in pieces], axis=0)


def dp_scatter(make):
    away = make(1)
    came = xor_shift(away, "dp", 1)
    kept = make(0)
    rows = kept.shape[0] // 4
    half = rows // 2

    def summed(start, stop):
        return kept[start:stop].astype(F32) + came[start:stop].astype(F32)

    first_x = xor_shift(summed(rows + half, 2 * rows + half).astype(BF16), "dp", 2)
    first_y = xor_shift(summed(2 * rows + half, 3 * rows + half).astype(BF16), "dp", 4)
    last_x = summed(rows, rows + half) + first_y[:half].astype(F32)
    last_y = summed(3 * rows + half, 4 * rows) + first_x[half:].astype(F32)
    last_x = xor_shift(last_x.astype(BF16), "dp", 2)
    last_y = xor_shift(last_y.astype(BF16), "dp", 4)
    top = summed(0, half) + first_x[:half].astype(F32) + last_y.astype(F32)
    low = summed(half, rows) + first_y[half:].astype(F32) + last_x.astype(F32)
    return jnp.concatenate([top, low], axis=0)


def weight_grad(rows, columns):
    def make(part):
        width = rows.shape[1] // 2
        chosen = rows[:, part * width : (part + 1) * width]
        return jnp.einsum("nd,nf->df", chosen, columns, preferred_element_type=F32).astype(BF16)

    if fast_dp():
        return dp_scatter(make)
    whole = jnp.einsum("nd,nf->df", rows, columns, preferred_element_type=F32).astype(BF16)
    return lax.psum_scatter(whole, "dp", scatter_dimension=0, tiled=True).astype(F32)


def line_gather(block):
    size = lax.axis_size("tensor")
    me = lax.axis_index("tensor")
    up = down = block
    ups, downs = [block], [block]
    for s in range(size - 1):
        up = lax.ppermute(up, "tensor", [(i, i + 1) for i in range(s, size - 1)])
        down = lax.ppermute(down, "tensor", [(i + 1, i) for i in range(size - 1 - s)])
        ups.append(up)
        downs.append(down)
    blocks = [block]
    for r in range(1, size):
        blocks.append(jnp.where(me + r < size, downs[r], ups[size - r]))
    return jnp.concatenate(blocks, axis=0)


def line_scatter(terms):
    size = lax.axis_size("tensor")
    rows = terms.shape[0] // size

    def block(r):
        return terms[r * rows : (r + 1) * rows]

    up = down = None
    for s in range(1, size):
        to_up, to_down = block(size - s), block(s)
        if s > 1:
            to_up = (to_up.astype(F32) + up.astype(F32)).astype(BF16)
            to_down = (to_down.astype(F32) + down.astype(F32)).astype(BF16)
        up = lax.ppermute(to_up, "tensor", [(i, i + 1) for i in range(s)])
        down = lax.ppermute(to_down, "tensor", [(i, i - 1) for i in range(size - s, size)])
    return block(0).astype(F32) + up.astype(F32) + down.astype(F32)


def turn(values, cosine, low_sine, high_sine, sign):
    half = ROT // 2
    lanes = cosine.shape[-1]
    head = values[:, :lanes]
    turned = (
        head * cosine
        - sign * pltpu.roll(head, lanes - half, 1) * low_sine
        + sign * pltpu.roll(head, half, 1) * high_sine
    )
    return jnp.concatenate([turned, values[:, lanes:]], axis=1)


def contract(a, b, dims):
    return lax.dot_general(a, b, (dims, ((), ())), preferred_element_type=F32)


def masked(scores, column_starts, row_starts, query_block, block):
    keys = scores.shape[1]
    query = lax.broadcasted_iota(jnp.int32, scores.shape, 0) + query_block * block
    key = lax.broadcasted_iota(jnp.int32, scores.shape, 1)
    allowed = (column_starts == row_starts[:, :keys]) & (key <= query)
    return allowed, jnp.where(allowed, scores, -1e30)


SMALL = pl.CostEstimate(flops=1000, bytes_accessed=1000, transcendentals=0)


def spots(me_ref, size, block):
    def spot(b):
        return pl.ds(pl.multiple_of(lax.rem(b - me_ref[0] + size, size) * block, block), block)

    return spot


def forward_block(q_out, k_out, v_out, att_ref, log_ref, col_ref, row_ref, spot, b, block):
    scale = q_out.shape[-1] ** (-0.5)
    here = slice(b * block, (b + 1) * block)
    query = q_out[spot(b), :]
    scores = jnp.concatenate(
        [contract(query, k_out[spot(c), :], ((1,), (1,))) for c in range(b + 1)], axis=1
    ) * scale
    _, scores = masked(scores, col_ref[here, :1], row_ref[:1, :], b, block)
    top = jnp.max(scores, axis=1, keepdims=True)
    powers = jnp.exp(scores - top)
    total = jnp.sum(powers, axis=1, keepdims=True)
    weights = (powers / total).astype(BF16)
    attended = contract(weights[:, :block], v_out[spot(0), :], ((1,), (0,)))
    for c in range(1, b + 1):
        attended = attended + contract(
            weights[:, c * block : (c + 1) * block], v_out[spot(c), :], ((1,), (0,))
        )
    att_ref[spot(b), :] = attended.astype(BF16)
    log_ref[0, here, :] = jnp.broadcast_to(top + jnp.log(total), (block, log_ref.shape[2]))


def forward_kernel(
    me_ref, q_ref, k_ref, v_ref, cos_ref, low_ref, high_ref, col_ref, row_ref,
    q_out, k_out, v_out, att_ref, log_ref, *, size, block,
):
    spot = spots(me_ref, size, block)
    for b in range(size):
        here = slice(b * block, (b + 1) * block)
        at = spot(b)
        tables = cos_ref[here, :], low_ref[here, :], high_ref[here, :]
        q_out[at, :] = turn(q_ref[at, :], *tables, 1.0).astype(BF16)
        k_out[at, :] = turn(k_ref[at, :], *tables, 1.0).astype(BF16)
        v_out[at, :] = v_ref[at, :].astype(BF16)
    for b in range(size):
        forward_block(q_out, k_out, v_out, att_ref, log_ref, col_ref, row_ref, spot, b, block)


def joined_forward_kernel(
    me_ref, rows_ref, qa_ref, ka_ref, va_ref, qb_ref, kb_ref, vb_ref, q_bias, k_bias, v_bias,
    cos_ref, low_ref, high_ref, col_ref, row_ref,
    q_out, k_out, v_out, att_ref, log_ref, *, size, block,
):
    spot = spots(me_ref, size, block)
    middle = qa_ref.shape[0]
    for b in range(size):
        here = slice(b * block, (b + 1) * block)
        at = spot(b)
        tables = cos_ref[here, :], low_ref[here, :], high_ref[here, :]
        top, low = rows_ref[at, :middle], rows_ref[at, middle:]

        def project(one, two, bias):
            return contract(top, one[:, :], ((1,), (0,))) + contract(low, two[:, :], ((1,), (0,))) + bias[:, :]

        q_out[at, :] = turn(project(qa_ref, qb_ref, q_bias), *tables, 1.0).astype(BF16)
        k_out[at, :] = turn(project(ka_ref, kb_ref, k_bias), *tables, 1.0).astype(BF16)
        v_out[at, :] = project(va_ref, vb_ref, v_bias).astype(BF16)
        forward_block(q_out, k_out, v_out, att_ref, log_ref, col_ref, row_ref, spot, b, block)


def backward_pass(
    q_ref, k_ref, v_ref, g_ref, log_ref, cos_ref, low_ref, high_ref, col_ref, row_ref,
    put, k_acc, v_acc, spot, size, block,
):
    scale = q_ref.shape[-1] ** (-0.5)
    for b in range(size):
        here = slice(b * block, (b + 1) * block)
        query, grad = q_ref[spot(b), :], g_ref[spot(b), :]
        scores = jnp.concatenate(
            [contract(query, k_ref[spot(c), :], ((1,), (1,))) for c in range(b + 1)], axis=1
        ) * scale
        allowed, scores = masked(scores, col_ref[here, :1], row_ref[:1, :], b, block)
        probs = jnp.where(allowed, jnp.exp(scores - log_ref[0, here, :1]), 0.0)
        grad_probs = jnp.concatenate(
            [contract(grad, v_ref[spot(c), :], ((1,), (1,))) for c in range(b + 1)], axis=1
        )
        inner = jnp.sum(probs * grad_probs, axis=1, keepdims=True)
        weights = probs.astype(BF16)
        grad_scores = (probs * (grad_probs - inner)).astype(BF16)
        back = None
        for c in range(b + 1):
            part = slice(c * block, (c + 1) * block)
            key_term = contract(grad_scores[:, part], query, ((0,), (0,)))
            value_term = contract(weights[:, part], grad, ((0,), (0,)))
            query_term = contract(grad_scores[:, part], k_ref[spot(c), :], ((1,), (0,)))
            back = query_term if c == 0 else back + query_term
            if c == b:
                k_acc[part, :] = key_term
                v_acc[part, :] = value_term
            else:
                k_acc[part, :] += key_term
                v_acc[part, :] += value_term
        tables = cos_ref[here, :], low_ref[here, :], high_ref[here, :]
        put(0, spot(b), turn(back * scale, *tables, -1.0).astype(BF16))
    for b in range(size):
        here = slice(b * block, (b + 1) * block)
        tables = cos_ref[here, :], low_ref[here, :], high_ref[here, :]
        put(1, spot(b), turn(k_acc[here, :] * scale, *tables, -1.0).astype(BF16))
        put(2, spot(b), v_acc[here, :].astype(BF16))


def backward_kernel(
    me_ref, q_ref, k_ref, v_ref, g_ref, log_ref, cos_ref, low_ref, high_ref, col_ref, row_ref,
    dq_ref, dk_ref, dv_ref, k_acc, v_acc, *, size, block,
):
    outs = (dq_ref, dk_ref, dv_ref)

    def put(k, at, value):
        outs[k][at, :] = value

    backward_pass(
        q_ref, k_ref, v_ref, g_ref, log_ref, cos_ref, low_ref, high_ref, col_ref, row_ref,
        put, k_acc, v_acc, spots(me_ref, size, block), size, block,
    )


def mixed_backward_kernel(
    me_ref, q_ref, k_ref, v_ref, g_ref, a_ref, b_ref, log_ref, cos_ref, low_ref, high_ref, col_ref, row_ref,
    d_ref, k_acc, v_acc, g_acc, *, size, block, heads,
):
    middle = a_ref.shape[0]
    head = q_ref.shape[1]
    for b in range(size):
        here = slice(b * block, (b + 1) * block)
        g_acc[here, :] = (
            contract(g_ref[here, :middle], a_ref[:, :], ((1,), (0,)))
            + contract(g_ref[here, middle:], b_ref[:, :], ((1,), (0,)))
        ).astype(BF16)
    h = pl.program_id(0)

    def put(k, at, value):
        d_ref[at, pl.ds(pl.multiple_of((k * heads + h) * head, head), head)] = value

    backward_pass(
        q_ref, k_ref, v_ref, g_acc, log_ref, cos_ref, low_ref, high_ref, col_ref, row_ref,
        put, k_acc, v_acc, spots(me_ref, size, block), size, block,
    )


def hidden_kernel(rows_ref, a_ref, b_ref, bias_ref, act_ref, slope_ref, *, step):
    middle = a_ref.shape[0]
    for i in range(rows_ref.shape[0] // step):
        here = slice(i * step, (i + 1) * step)
        hidden = contract(rows_ref[here, :middle], a_ref[:, :], ((1,), (0,)))
        hidden = hidden + contract(rows_ref[here, middle:], b_ref[:, :], ((1,), (0,))) + bias_ref[:, :]
        bell = lax.erf(hidden * (0.5**0.5))
        act_ref[here, :] = (0.5 * hidden * (1.0 + bell)).astype(BF16)
        slope = 0.5 * (1.0 + bell) + hidden * jnp.exp(-0.5 * hidden * hidden) * 0.3989422804014327
        slope_ref[here, :] = slope.astype(BF16)


def hidden_half(rows, top, low, bias):
    count, width = rows.shape
    out = top.shape[1]
    tile = 512
    half = pl.BlockSpec((width // 2, tile), lambda j: (0, j))
    made = pl.BlockSpec((count, tile), lambda j: (0, j))
    return pl.pallas_call(
        functools.partial(hidden_kernel, step=256),
        out_shape=(jax.ShapeDtypeStruct((count, out), BF16),) * 2,
        grid=(out // tile,),
        in_specs=[
            pl.BlockSpec((count, width), lambda j: (0, 0)), half, half, pl.BlockSpec((1, tile), lambda j: (0, j))
        ],
        out_specs=(made, made),
        cost_estimate=SMALL,
        name="hidden",
    )(rows, top, low, bias.reshape(1, -1))


def slope_kernel(rows_ref, a_ref, b_ref, slope_ref, out_ref, *, step):
    middle = a_ref.shape[0]
    for i in range(rows_ref.shape[0] // step):
        here = slice(i * step, (i + 1) * step)
        active = contract(rows_ref[here, :middle], a_ref[:, :], ((1,), (0,)))
        active = active + contract(rows_ref[here, middle:], b_ref[:, :], ((1,), (0,)))
        out_ref[here, :] = (active * slope_ref[here, :].astype(F32)).astype(BF16)


def hidden_back(rows, top, low, slope):
    count, width = rows.shape
    out = top.shape[1]
    tile = 512
    half = pl.BlockSpec((top.shape[0], tile), lambda j: (0, j))
    made = pl.BlockSpec((count, tile), lambda j: (0, j))
    return pl.pallas_call(
        functools.partial(slope_kernel, step=256),
        out_shape=jax.ShapeDtypeStruct((count, out), BF16),
        grid=(out // tile,),
        in_specs=[pl.BlockSpec((count, width), lambda j: (0, 0)), half, half, made],
        out_specs=made,
        cost_estimate=SMALL,
        name="hidden_back",
    )(rows, top, low, slope)


def branch_kernel(att_ref, mix_ref, act_ref, down_ref, out_ref, *, step):
    for i in range(att_ref.shape[0] // step):
        here = slice(i * step, (i + 1) * step)
        total = contract(att_ref[here, :], mix_ref[:, :], ((1,), (1,)))
        total = total + contract(act_ref[here, :], down_ref[:, :], ((1,), (1,)))
        out_ref[here, :] = total.astype(BF16)


def branch_half(attended, mixed, activated, down):
    count, inner = attended.shape
    units = activated.shape[1]
    width = down.shape[0]
    tile = 256
    spot = mixed.shape[1] // inner - 1
    return pl.pallas_call(
        functools.partial(branch_kernel, step=256),
        out_shape=jax.ShapeDtypeStruct((count, width), BF16),
        grid=(width // tile,),
        in_specs=[
            pl.BlockSpec((count, inner), lambda j: (0, 0)),
            pl.BlockSpec((tile, inner), lambda j: (j + width // tile, spot)),
            pl.BlockSpec((count, units), lambda j: (0, 0)),
            pl.BlockSpec((tile, units), lambda j: (j, 0)),
        ],
        out_specs=pl.BlockSpec((count, tile), lambda j: (0, j)),
        cost_estimate=SMALL,
        name="branches",
    )(attended, mixed, activated, down)


def back_kernel(
    hid_ref, proj_ref, up_ref, join_ref, tok_ref, mean_ref, scale_ref, gain_ref, back_ref, sum_ref, *, step
):
    sums = [0.0] * 4
    for i in range(hid_ref.shape[0] // step):
        here = slice(i * step, (i + 1) * step)
        two = contract(hid_ref[here, :], up_ref[:, :], ((1,), (1,)))
        one = contract(proj_ref[here, :], join_ref[:, :], ((1,), (1,)))
        back_ref[here, :] = (one * gain_ref[:1, :] + two * gain_ref[1:2, :]).astype(BF16)
        xhat = (tok_ref[here, :].astype(F32) - mean_ref[here, :1]) * scale_ref[here, :1]
        for k, term in enumerate((one * xhat, two * xhat, one, two)):
            sums[k] = sums[k] + jnp.sum(term, axis=0, keepdims=True)
    for k in range(4):
        sum_ref[k : k + 1, :] = sums[k]


def back_half(grad_hidden, grad_projected, both, token_rows, mean, scale, gains, part):
    count, units = grad_hidden.shape
    joined = grad_projected.shape[1]
    width = both.shape[0] // 2
    tile = 256
    tiles = width // tile
    whole = lambda j: (0, 0)
    return pl.pallas_call(
        functools.partial(back_kernel, step=256),
        out_shape=(jax.ShapeDtypeStruct((count, width), BF16), jax.ShapeDtypeStruct((8, width), F32)),
        grid=(tiles,),
        in_specs=[
            pl.BlockSpec((count, units), whole),
            pl.BlockSpec((count, joined), whole),
            pl.BlockSpec((tile, units), lambda j: (j, 0)),
            pl.BlockSpec((tile, joined), lambda j: (j + tiles, 0)),
            pl.BlockSpec((count, tile), lambda j: (0, j + part * tiles)),
            pl.BlockSpec((count, 128), whole),
            pl.BlockSpec((count, 128), whole),
            pl.BlockSpec((2, tile), lambda j: (0, j + part * tiles)),
        ],
        out_specs=(pl.BlockSpec((count, tile), lambda j: (0, j)), pl.BlockSpec((8, tile), lambda j: (0, j))),
        cost_estimate=SMALL,
        name="back",
    )(grad_hidden, grad_projected, both, both, token_rows, mean, scale, gains)


def terms_kernel(*refs):
    *ins, to_up, to_down = refs
    up = jnp.concatenate([ins[0][:, :], ins[1][:, :]], axis=1)
    down = jnp.concatenate([ins[2][:, :], ins[3][:, :]], axis=1)
    if len(ins) > 4:
        up = (up.astype(F32) + ins[4][:, :].astype(F32)).astype(BF16)
        down = (down.astype(F32) + ins[5][:, :].astype(F32)).astype(BF16)
    to_up[:, :] = up
    to_down[:, :] = down


def step_terms(halves, up_block, down_block, rows, *came):
    width = halves[0].shape[1]
    tiles = 2
    tile = rows // tiles

    def of(block):
        return [pl.BlockSpec((tile, width), lambda i: (block * tiles + i, 0))] * 2

    full = pl.BlockSpec((tile, 2 * width), lambda i: (i, 0))
    return pl.pallas_call(
        terms_kernel,
        out_shape=(jax.ShapeDtypeStruct((rows, 2 * width), BF16),) * 2,
        grid=(tiles,),
        in_specs=of(up_block) + of(down_block) + [full] * len(came),
        out_specs=(full, full),
        cost_estimate=SMALL,
        name="terms",
    )(*halves, *halves, *came)


def input_grad_kernel(index_ref, one_ref, two_ref, up_ref, down_ref, tok_ref, grad_ref, out_ref):
    back = jnp.concatenate([one_ref[:, :], two_ref[:, :]], axis=1).astype(F32)
    back = back + up_ref[:, :].astype(F32) + down_ref[:, :].astype(F32)
    xhat, scale = standardize(tok_ref[:, :])
    back = back - jnp.mean(back, axis=-1, keepdims=True) - xhat * jnp.mean(back * xhat, axis=-1, keepdims=True)
    total = grad_ref[:, :].astype(F32) + back * scale
    count = index_ref.shape[0]
    step = total.shape[1] // count
    for j in range(count):
        out_ref[:, pl.ds(pl.multiple_of(index_ref[j] * step, step), step)] = total[:, j * step : (j + 1) * step]


def input_grad_rows(one, two, up, down, tokens, grads):
    rows, width = tokens.shape
    tile = rows // 4
    half = pl.BlockSpec((tile, width // 2), lambda i, s: (i, 0))
    full = pl.BlockSpec((tile, width), lambda i, s: (i, 0))
    return pl.pallas_call(
        input_grad_kernel,
        out_shape=jax.ShapeDtypeStruct((rows, width), F32),
        grid_spec=pltpu.PrefetchScalarGridSpec(
            num_scalar_prefetch=1,
            grid=(rows // tile,),
            in_specs=[half, half, full, full, full, full],
            out_specs=full,
        ),
        cost_estimate=SMALL,
        name="input_grad",
    )(frame_index(), one, two, up, down, tokens, grads)


def joined_forward(rows, top, low, bias, tables, me, heads, head, size):
    count, width = rows.shape
    block = count // size
    whole = lambda h, s: (0, 0)
    table_specs = [pl.BlockSpec((count, 128), whole)] * 4 + [pl.BlockSpec((8, count), whole)]
    by_head = pl.BlockSpec((count, head), lambda h, s: (0, h))
    wide = jax.ShapeDtypeStruct((count, heads * head), BF16)

    def thirds(n, spot):
        return [pl.BlockSpec((n, head), lambda h, s, k=k: (spot, k * heads + h)) for k in range(3)]

    return pl.pallas_call(
        functools.partial(joined_forward_kernel, size=size, block=block),
        out_shape=(wide, wide, wide, wide, jax.ShapeDtypeStruct((heads, count, 128), F32)),
        grid_spec=pltpu.PrefetchScalarGridSpec(
            num_scalar_prefetch=1,
            grid=(heads,),
            in_specs=[pl.BlockSpec((count, width), whole)]
            + thirds(width // 2, 1) + thirds(width // 2, 1) + thirds(1, 0) + table_specs,
            out_specs=(by_head,) * 4 + (pl.BlockSpec((1, count, 128), lambda h, s: (h, 0, 0)),),
        ),
        cost_estimate=SMALL,
        name="joined_forward",
    )(me, rows, top, top, top, low, low, low, bias, bias, bias, *tables)


def mixed_backward(queries, keys, values, grads, top, low, log_total, tables, me, heads, size):
    count = queries.shape[0]
    head = queries.shape[1] // heads
    block = count // size
    whole = lambda h, s: (0, 0)
    table_specs = [pl.BlockSpec((count, 128), whole)] * 4 + [pl.BlockSpec((8, count), whole)]
    by_head = pl.BlockSpec((count, head), lambda h, s: (0, h))
    mix = pl.BlockSpec((grads.shape[1] // 2, head), lambda h, s: (1, 3 * heads + h))
    return pl.pallas_call(
        functools.partial(mixed_backward_kernel, size=size, block=block, heads=heads),
        out_shape=jax.ShapeDtypeStruct((count, 3 * heads * head), BF16),
        grid_spec=pltpu.PrefetchScalarGridSpec(
            num_scalar_prefetch=1,
            grid=(heads,),
            in_specs=[by_head] * 3
            + [pl.BlockSpec((count, grads.shape[1]), whole), mix, mix]
            + [pl.BlockSpec((1, count, 128), lambda h, s: (h, 0, 0))]
            + table_specs,
            out_specs=pl.BlockSpec((count, 3 * heads * head), whole),
            scratch_shapes=[pltpu.VMEM((count, head), F32)] * 2 + [pltpu.VMEM((count, head), BF16)],
        ),
        cost_estimate=SMALL,
        name="mixed_backward",
    )(me, queries, keys, values, grads, top, low, log_total, *tables)


def attention_tables(positions, starts):
    half = ROT // 2
    frequency = ROTARY_BASE ** (-(jnp.arange(half, dtype=F32) * 2.0) / ROT)
    angles = positions.astype(F32)[:, None] * frequency[None, :]
    cosine, sine = jnp.cos(angles), jnp.sin(angles)
    rows = positions.shape[0]
    cosines = jnp.concatenate([cosine, cosine, jnp.ones((rows, 128 - ROT), F32)], axis=1)
    low = jnp.concatenate([sine, jnp.zeros((rows, 128 - half), F32)], axis=1)
    high = jnp.concatenate([jnp.zeros((rows, half), F32), sine, jnp.zeros((rows, 128 - ROT), F32)], axis=1)
    columns = jnp.broadcast_to(starts[:, None], (rows, 128))
    across = jnp.broadcast_to(starts[None, :], (8, rows))
    return cosines, low, high, columns, across


def attention_forward(projected, tables, me, heads, size):
    rows = projected.shape[0]
    head = projected.shape[1] // (3 * heads)
    block = rows // size
    whole = lambda h, s: (0, 0)
    table_specs = [pl.BlockSpec((rows, 128), whole)] * 4 + [pl.BlockSpec((8, rows), whole)]
    by_head = pl.BlockSpec((rows, head), lambda h, s: (0, h))
    wide = jax.ShapeDtypeStruct((rows, heads * head), BF16)
    return pl.pallas_call(
        functools.partial(forward_kernel, size=size, block=block),
        out_shape=(wide, wide, wide, wide, jax.ShapeDtypeStruct((heads, rows, 128), F32)),
        grid_spec=pltpu.PrefetchScalarGridSpec(
            num_scalar_prefetch=1,
            grid=(heads,),
            in_specs=[
                pl.BlockSpec((rows, head), lambda h, s, k=k: (0, k * heads + h)) for k in range(3)
            ]
            + table_specs,
            out_specs=(by_head,) * 4 + (pl.BlockSpec((1, rows, 128), lambda h, s: (h, 0, 0)),),
        ),
        cost_estimate=pl.CostEstimate(
            flops=heads * rows * rows * head * 40, bytes_accessed=rows * head * heads * 24,
            transcendentals=heads * rows * rows // 2,
        ),
        name="attention_forward",
    )(me, projected, projected, projected, *tables)


def attention_backward(queries, keys, values, grads, log_total, tables, me, heads, size):
    rows = queries.shape[0]
    head = queries.shape[1] // heads
    block = rows // size
    whole = lambda h, s: (0, 0)
    table_specs = [pl.BlockSpec((rows, 128), whole)] * 4 + [pl.BlockSpec((8, rows), whole)]
    by_head = pl.BlockSpec((rows, head), lambda h, s: (0, h))
    wide = jax.ShapeDtypeStruct((rows, heads * head), BF16)
    return pl.pallas_call(
        functools.partial(backward_kernel, size=size, block=block),
        out_shape=(wide, wide, wide),
        grid_spec=pltpu.PrefetchScalarGridSpec(
            num_scalar_prefetch=1,
            grid=(heads,),
            in_specs=[by_head] * 4
            + [pl.BlockSpec((1, rows, 128), lambda h, s: (h, 0, 0))]
            + table_specs,
            out_specs=(by_head,) * 3,
            scratch_shapes=[pltpu.VMEM((rows, head), F32)] * 2,
        ),
        cost_estimate=pl.CostEstimate(
            flops=heads * rows * rows * head * 60, bytes_accessed=rows * head * heads * 24,
            transcendentals=heads * rows * rows // 2,
        ),
        name="attention_backward",
    )(me, queries, keys, values, grads, log_total, *tables)


def standardize(values):
    values = values.astype(F32)
    centered = values - jnp.mean(values, axis=-1, keepdims=True)
    spread = jnp.mean(centered * centered, axis=-1, keepdims=True)
    scale = lax.rsqrt(spread + EPSILON)
    return centered * scale, scale


def norm_rows(token_rows, gain_rows, shift_rows):
    xhat, _ = standardize(token_rows)
    first_rows = (xhat * gain_rows[0] + shift_rows[0]).astype(BF16)
    second_rows = (xhat * gain_rows[1] + shift_rows[1]).astype(BF16)
    return first_rows, second_rows


def hidden_units(second_rows, up_rows, hidden_bias):
    hidden = jnp.dot(second_rows, up_rows, preferred_element_type=F32) + hidden_bias
    bell = lax.erf(hidden * (0.5**0.5))
    activated = (0.5 * hidden * (1.0 + bell)).astype(BF16)
    slope = 0.5 * (1.0 + bell) + hidden * jnp.exp(-0.5 * hidden * hidden) * 0.3989422804014327
    return activated, slope.astype(BF16)


def branch_rows(attended, mix_rows, activated, down_rows):
    return (
        jnp.einsum("ne,de->nd", attended, mix_rows, preferred_element_type=F32)
        + jnp.einsum("nf,df->nd", activated, down_rows, preferred_element_type=F32)
    ).astype(BF16)


def hidden_grads(grad_rows, down_rows, slope):
    grad_active = jnp.einsum("nd,df->nf", grad_rows, down_rows, preferred_element_type=F32)
    return (grad_active * slope.astype(F32)).astype(BF16)


def attended_grads(grad_rows, mix_rows):
    return jnp.einsum("nd,de->ne", grad_rows, mix_rows, preferred_element_type=F32).astype(BF16)


def back_rows(grads, weight_rows):
    return jnp.einsum("nf,df->nd", grads, weight_rows, preferred_element_type=F32)


def grad_half(rows, columns, part):
    width = rows.shape[1] // 2
    chosen = rows[:, part * width : (part + 1) * width]
    return jnp.einsum("nd,nf->df", chosen, columns, preferred_element_type=F32).astype(BF16)


def plus(*terms):
    return functools.reduce(lambda a, b: a + b, [t.astype(F32) for t in terms])


def width_sums(grad_first, grad_second, xhat, grad_local):
    return jnp.stack(
        [
            jnp.sum(grad_first * xhat, axis=0),
            jnp.sum(grad_second * xhat, axis=0),
            jnp.sum(grad_first, axis=0),
            jnp.sum(grad_second, axis=0),
            jnp.sum(grad_local.astype(F32), axis=0),
        ],
        axis=0,
    )


def shards(
    tokens,
    seq_start,
    proj_weight,
    proj_bias,
    out_weight,
    up_weight,
    up_bias,
    down_weight,
    norm_gains,
    biases,
    cotangent,
):
    local_rows, width = tokens.shape
    n_dp, n_tensor = lax.axis_size("dp"), lax.axis_size("tensor")
    dp_index, tensor_index = lax.axis_index("dp"), lax.axis_index("tensor")
    row_count = local_rows * n_tensor
    hidden_width = up_weight.shape[1]
    heads_here = proj_bias.shape[1]
    head_size = proj_bias.shape[2] * n_dp
    local_width = heads_here * head_size
    joined_width = 3 * local_width
    columns = norm_gains.shape[1]

    vectors = jnp.concatenate(
        [norm_gains.reshape(1, -1), biases.reshape(1, -1), proj_bias.reshape(1, -1), up_bias.reshape(1, -1)],
        axis=1,
    )
    table = jnp.zeros((n_dp * n_tensor, vectors.shape[1]), BF16)
    table = lax.dynamic_update_slice(table, vectors, (dp_index * n_tensor + tensor_index, 0))
    local_tokens, local_grads = to_frame(tokens), to_frame(cotangent)
    positions = dp_index * row_count + jnp.arange(row_count, dtype=jnp.int32) - seq_start
    tables = attention_tables(positions, seq_start)
    me = tensor_index.astype(jnp.int32).reshape(1)
    flat_proj = proj_weight.reshape(-1, joined_width)

    def small_parameters(table):
        six_rows = table[:, : 6 * columns].reshape(n_dp * n_tensor, 6, columns).transpose(1, 0, 2)
        six_rows = to_frame(six_rows.reshape(6, width).astype(F32))
        of_tensor = lax.dynamic_index_in_dim(
            table[:, 6 * columns :].reshape(n_dp, n_tensor, -1), tensor_index, 1, keepdims=False
        ).astype(F32)
        joined_bias = (
            of_tensor[:, : proj_bias.size]
            .reshape(n_dp, 3, heads_here, -1)
            .transpose(1, 2, 0, 3)
            .reshape(joined_width)
        )
        hidden_bias = of_tensor[:, proj_bias.size :].reshape(hidden_width)
        return six_rows[:2], six_rows[2:], joined_bias, hidden_bias

    def attend(first_rows, joined_rows, joined_bias):
        projected = jnp.dot(first_rows, joined_rows, preferred_element_type=F32) + joined_bias
        return attention_forward(projected, tables, me, heads_here, n_tensor)

    def attend_back(kept, grad_attended):
        queries, keys, values, log_total = kept
        backs = attention_backward(
            queries, keys, values, grad_attended, log_total, tables, me, heads_here, n_tensor
        )
        return jnp.concatenate(backs, axis=1)

    def finish_output(branches, shift_rows):
        output = local_tokens.astype(F32) + branches + shift_rows[2] + shift_rows[3]
        return from_frame(output.astype(BF16))

    def finish_input_grad(back):
        xhat_local, scale_local = standardize(local_tokens)
        grad_norm_in = (
            back
            - jnp.mean(back, axis=-1, keepdims=True)
            - xhat_local * jnp.mean(back * xhat_local, axis=-1, keepdims=True)
        ) * scale_local
        return from_frame(local_grads.astype(F32) + grad_norm_in)

    def small_shares(five, joined_bias_sums, up_bias_sums):
        five = five.reshape(5, width)
        mine = lax.dynamic_slice_in_dim(
            five, (dp_index * n_tensor + tensor_index) * columns, columns, 1
        )
        biases_grad = jnp.concatenate([mine[2:], mine[4:]], axis=0)
        joined_bias_sum = lax.dynamic_slice_in_dim(
            joined_bias_sums.reshape(3, heads_here, head_size),
            dp_index * proj_bias.shape[2],
            proj_bias.shape[2],
            2,
        )
        up_bias_sum = lax.dynamic_slice_in_dim(
            up_bias_sums.reshape(1, -1), dp_index * up_bias.shape[1], up_bias.shape[1], 1
        )
        return mine[:2], biases_grad, joined_bias_sum, up_bias_sum

    def small_grads(five, joined_bias_term, up_bias_term):
        five = from_frame(five).reshape(1, -1)
        terms = jnp.concatenate([five, joined_bias_term[None], up_bias_term[None]], axis=1)
        terms = butterfly(terms, "dp")
        five = butterfly(terms[:, : 5 * width], "tensor")
        return small_shares(
            five, terms[0, 5 * width : 5 * width + joined_width], terms[:, 5 * width + joined_width :]
        )

    def plain():
        token_rows, grad_rows = line_gather(local_tokens), line_gather(local_grads)
        up_rows, down_rows = dp_gather(up_weight), dp_gather(down_weight.T)
        joined_rows, mix_rows = dp_gather(flat_proj), dp_gather(out_weight.T)
        up_rows, down_rows, joined_rows, mix_rows = (
            join(w, 0, None) for w in (up_rows, down_rows, joined_rows, mix_rows)
        )
        gain_rows, shift_rows, joined_bias, hidden_bias = small_parameters(
            butterfly(butterfly(table, "dp"), "tensor")
        )
        first_rows, second_rows = norm_rows(token_rows, gain_rows, shift_rows)
        activated, slope = cut(*hidden_units(second_rows, up_rows, hidden_bias))
        *kept, attended, log_total = attend(first_rows, joined_rows, joined_bias)
        branches = line_scatter(branch_rows(attended, mix_rows, activated, down_rows))
        output = finish_output(branches, shift_rows)
        grad_hidden = hidden_grads(grad_rows, down_rows, slope)
        down_sum = weight_grad(grad_rows, activated)
        up_sum = weight_grad(second_rows, grad_hidden)
        grad_second = back_rows(grad_hidden, up_rows)
        grad_attended = attended_grads(grad_rows, mix_rows)
        mix_sum = weight_grad(grad_rows, attended)
        grad_projected = attend_back((*kept, log_total), grad_attended)
        joined_sum = weight_grad(first_rows, grad_projected)
        grad_first = back_rows(grad_projected, joined_rows)
        back = grad_first * gain_rows[0] + grad_second * gain_rows[1]
        input_grad = finish_input_grad(line_scatter(back.astype(BF16)))
        five = width_sums(grad_first, grad_second, standardize(token_rows)[0], local_grads)
        small = small_grads(
            five, jnp.sum(grad_projected, axis=0, dtype=F32), jnp.sum(grad_hidden, axis=0, dtype=F32)
        )
        return output, input_grad, joined_sum, mix_sum.T, up_sum, down_sum.T, small

    def staged():
        half = local_rows // 2
        first, second = slice(0, half), slice(half, 2 * half)

        def x(values):
            return xor_shift(values, "dp", 2)

        def y(values):
            return xor_shift(values, "dp", 4)

        def core(values):
            return xor_shift(values, "dp", 1)

        def gather_step(up, down, s):
            up = lax.ppermute(up, "tensor", [(i, i + 1) for i in range(s, 3)])
            down = lax.ppermute(down, "tensor", [(i + 1, i) for i in range(3 - s)])
            return up, down

        def scatter_terms(halves, up, down, s):
            came = () if s == 1 else (up, down)
            return step_terms(halves, 4 - s, s, local_rows, *came)

        def scatter_step(to_up, to_down, s):
            up = lax.ppermute(to_up, "tensor", [(i, i + 1) for i in range(s)])
            down = lax.ppermute(to_down, "tensor", [(i, i - 1) for i in range(4 - s, 4)])
            return up, down

        def in_turn(block, ups, downs):
            blocks = [block] + [
                jnp.where(tensor_index + r < 4, downs[r - 1], ups[3 - r]) for r in range(1, 4)
            ]
            return jnp.concatenate(blocks, axis=0)

        def pair(top, low):
            return jnp.concatenate([top, low], axis=0)

        def laid(own, from_x, from_y):
            return [own, from_x[second], from_x[first], jnp.zeros_like(own), from_y[second], from_y[first]]

        def place(base, piece, part):
            return lax.dynamic_update_slice(base, piece, ((4 * part + 2) * local_rows, 0))

        def at(keep, came, start, stop):
            return plus(keep[start * half : stop * half], came[start * half : stop * half])

        def joined_half(first_rows, grad_projected, grad_rows, attended, part):
            return jnp.concatenate(
                [grad_half(first_rows, grad_projected, part), grad_half(grad_rows, attended, part)], axis=1
            )

        wa = up_weight
        wb = jnp.concatenate([flat_proj, out_weight.T], axis=1)
        wc = down_weight.T

        ax, ay = x(wa), y(wa)
        tu1, td1 = gather_step(local_tokens, local_tokens, 0)
        table1 = table + core(table)
        table1, ax, ay = cut(table1, ax, ay)
        table1 = table1 + x(table1) + y(table1) + xor_shift(table1, "dp", 6)
        tu1, td1, ax, ay, table1, wb, wc, tables1 = cut(tu1, td1, ax, ay, table1, wb, wc, tables)
        tu2, td2 = gather_step(tu1, td1, 1)
        bx, by = x(wb), y(wb)
        table2 = table1 + xor_shift(table1, "tensor", 1)
        tu2, td2, bx, by, table2, local_grads1 = cut(tu2, td2, bx, by, table2, local_grads)
        tu3, td3 = gather_step(tu2, td2, 2)
        fa, fb = x(ay), y(bx)
        table3 = table2 + xor_shift(table2, "tensor", 2)
        both = jnp.concatenate(laid(wa, ax, ay) + laid(wb, bx, by), axis=0)
        tu3, td3, fa, fb, table3, both = cut(tu3, td3, fa, fb, table3, both)
        both_1 = place(place(both, fa, 0), fb, 1)
        both_1, wc, local_grads1 = cut(both_1, wc, local_grads1)
        cu1, cd1 = gather_step(local_grads1, local_grads1, 0)
        cx, cy = x(wc), y(wc)
        both_2 = core(both_1)
        gain_rows, shift_rows, joined_bias, hidden_bias = small_parameters(table3)
        token_rows = in_turn(local_tokens, (tu1, tu2, tu3), (td1, td2, td3))
        first_rows, second_rows = norm_rows(token_rows, gain_rows, shift_rows)
        mean = jnp.mean(token_rows.astype(F32), axis=-1, keepdims=True)
        _, scale = standardize(token_rows)
        mean, scale = (jnp.broadcast_to(v, (row_count, 128)) for v in (mean, scale))
        activated, slope = hidden_half(second_rows, both_1, both_2, hidden_bias)
        cu1, cd1, cx, cy, both_1, both_2, first_rows, activated, slope = cut(
            cu1, cd1, cx, cy, both_1, both_2, first_rows, activated, slope
        )
        cu2, cd2 = gather_step(cu1, cd1, 1)
        fc = x(cy)
        down_0 = jnp.concatenate(laid(wc, cx, cy), axis=0)
        *kept, attended, log_total = joined_forward(
            first_rows, both_1, both_2, joined_bias.reshape(1, -1), tables1, me, heads_here, head_size, n_tensor
        )
        cu2, cd2, fc, attended, down_0, mean, scale = cut(cu2, cd2, fc, attended, down_0, mean, scale)
        cu3, cd3 = gather_step(cu2, cd2, 2)
        down_1 = place(down_0, fc, 0)
        down_2 = core(down_1)
        branch_1 = branch_half(attended, both_1, activated, down_1)
        branch_2 = branch_half(attended, both_2, activated, down_2)
        cu3, cd3, branch_1, branch_2, activated = cut(cu3, cd3, branch_1, branch_2, activated)
        branches = (branch_1, branch_2)
        zu, zd, activated, cu3, cd3 = cut(*scatter_terms(branches, None, None, 1), activated, cu3, cd3)
        bu, bd = scatter_step(zu, zd, 1)
        grad_rows = in_turn(local_grads1, (cu1, cu2, cu3), (cd1, cd2, cd3))
        came_d = core(grad_half(grad_rows, activated, 1))
        keep_d = grad_half(grad_rows, activated, 0)
        grad_hidden = hidden_back(grad_rows, down_1, down_2, slope)
        bu, bd, came_d, keep_d, grad_hidden, grad_rows = cut(
            bu, bd, came_d, keep_d, grad_hidden, grad_rows
        )
        zu, zd, sx, sy, second_rows, grad_hidden, grad_rows = cut(
            *scatter_terms(branches, bu, bd, 2),
            at(keep_d, came_d, 3, 5).astype(BF16),
            at(keep_d, came_d, 5, 7).astype(BF16),
            second_rows, grad_hidden, grad_rows,
        )
        bu, bd = scatter_step(zu, zd, 2)
        d1x, d1y = x(sx), y(sy)
        came_u = core(grad_half(second_rows, grad_hidden, 1))
        keep_u = grad_half(second_rows, grad_hidden, 0)
        grad_projected = mixed_backward(
            *kept, grad_rows, both_1, both_2, log_total, tables1, me, heads_here, n_tensor
        )
        bu, bd, d1x, d1y, came_u, keep_u, grad_projected, grad_hidden = cut(
            bu, bd, d1x, d1y, came_u, keep_u, grad_projected, grad_hidden
        )
        d2x = plus(at(keep_d, came_d, 2, 3), d1y[first]).astype(BF16)
        d2y = plus(at(keep_d, came_d, 7, 8), d1x[second]).astype(BF16)
        zu, zd, sx, sy, grad_hidden, grad_projected = cut(
            *scatter_terms(branches, bu, bd, 3),
            pair(d2x, at(keep_u, came_u, 4, 5).astype(BF16)),
            pair(d2y, at(keep_u, came_u, 5, 6).astype(BF16)),
            grad_hidden, grad_projected,
        )
        bu, bd = scatter_step(zu, zd, 3)
        s9x, s9y = x(sx), y(sy)
        back_1, sums_1 = back_half(grad_hidden, grad_projected, both_1, token_rows, mean, scale, gain_rows, 0)
        back_2, sums_2 = back_half(grad_hidden, grad_projected, both_2, token_rows, mean, scale, gain_rows, 1)
        bu, bd, s9x, s9y, back_1, back_2, sums_1, sums_2, first_rows, grad_rows, grad_projected, attended = cut(
            bu, bd, s9x, s9y, back_1, back_2, sums_1, sums_2, first_rows, grad_rows, grad_projected, attended
        )
        backs = (back_1, back_2)
        none = jnp.zeros((half, s9x.shape[1]), BF16)
        zu, zd, sx, sy, first_rows, grad_rows, bu, bd, sums_1, sums_2 = cut(
            *scatter_terms(backs, None, None, 1),
            plus(at(keep_u, came_u, 2, 4), pair(s9y[second], none)).astype(BF16),
            plus(at(keep_u, came_u, 6, 8), pair(none, s9x[second])).astype(BF16),
            first_rows, grad_rows, bu, bd, sums_1, sums_2,
        )
        eu, ed = scatter_step(zu, zd, 1)
        s10x, s10y = x(sx), y(sy)
        came_j = core(joined_half(first_rows, grad_projected, grad_rows, attended, 1))
        keep_j = joined_half(first_rows, grad_projected, grad_rows, attended, 0)
        five = jnp.concatenate(
            [
                jnp.concatenate([sums_1[:4], sums_2[:4]], axis=1),
                jnp.sum(local_grads.astype(F32), axis=0, keepdims=True),
            ],
            axis=0,
        )
        eu, ed, s10x, s10y, keep_j, five, bu, bd = cut(eu, ed, s10x, s10y, keep_j, five, bu, bd)
        zu, zd, sx, sy, s10x, s10y, five = cut(
            *scatter_terms(backs, eu, ed, 2),
            at(keep_j, came_j, 3, 5).astype(BF16),
            at(keep_j, came_j, 5, 7).astype(BF16),
            s10x, s10y, five,
        )
        eu, ed = scatter_step(zu, zd, 2)
        j1x, j1y = x(sx), y(sy)
        five = five.reshape(1, -1)
        five = five + xor_shift(five, "tensor", 1)
        own = jnp.concatenate([h[:local_rows] for h in branches], axis=1)
        output = finish_output(plus(own, bu, bd), shift_rows)
        down_sum = pair(
            plus(at(keep_d, came_d, 0, 1), d1x[first], s9y[first]),
            plus(at(keep_d, came_d, 1, 2), d1y[second], s9x[first]),
        ).T
        up_sum = pair(
            plus(at(keep_u, came_u, 0, 1), s10x[second], s10y[second]),
            plus(at(keep_u, came_u, 1, 2), s10x[first], s10y[first]),
        )
        five = from_frame(five.reshape(5, width)).reshape(1, -1)
        terms = jnp.concatenate(
            [
                five,
                jnp.sum(grad_projected, axis=0, dtype=F32, keepdims=True),
                jnp.sum(grad_hidden, axis=0, dtype=F32, keepdims=True),
            ],
            axis=1,
        )
        eu, ed, j1x, j1y, terms, down_sum, up_sum, output = cut(
            eu, ed, j1x, j1y, terms, down_sum, up_sum, output
        )
        zu, zd, sx, sy, terms = cut(
            *scatter_terms(backs, eu, ed, 3),
            plus(at(keep_j, came_j, 2, 3), j1y[first]).astype(BF16),
            plus(at(keep_j, came_j, 7, 8), j1x[second]).astype(BF16),
            terms,
        )
        eu, ed = scatter_step(zu, zd, 3)
        j2x, j2y = x(sx), y(sy)
        terms, j2x, j2y = cut(terms, j2x, j2y)
        terms = butterfly(terms, "dp")
        five = terms[:, : 5 * width]
        five = five + xor_shift(five, "tensor", 2)
        small = small_shares(
            five, terms[0, 5 * width : 5 * width + joined_width], terms[:, 5 * width + joined_width :]
        )
        joined_mix = pair(
            plus(at(keep_j, came_j, 0, 1), j1x[first], j2y),
            plus(at(keep_j, came_j, 1, 2), j1y[second], j2x),
        )
        joined_sum, mix_sum = joined_mix[:, :joined_width], joined_mix[:, joined_width:].T
        eu, ed, joined_sum, mix_sum = cut(eu, ed, joined_sum, mix_sum)
        input_grad = input_grad_rows(*backs, eu, ed, local_tokens, local_grads)
        return output, input_grad, joined_sum, mix_sum, up_sum, down_sum, small

    parts = staged() if fast_dp() and n_tensor == 4 else plain()
    output, input_grad, joined_sum, mix_sum, up_sum, down_sum, small = parts
    gains_grad, biases_grad, joined_bias_sum, up_bias_sum = small
    return (
        output,
        input_grad,
        joined_sum.reshape(proj_weight.shape),
        joined_bias_sum,
        mix_sum,
        up_sum,
        up_bias_sum,
        down_sum,
        gains_grad,
        biases_grad,
    )


def solution(mesh):
    in_specs = (
        P(("dp", "tensor"), None),
        P("dp"),
        P("dp", None, "tensor"),
        P(None, "tensor", "dp"),
        P("tensor", "dp"),
        P("dp", "tensor"),
        P("tensor", "dp"),
        P("tensor", "dp"),
        P(None, ("dp", "tensor")),
        P(None, ("dp", "tensor")),
        P(("dp", "tensor"), None),
    )
    out_specs = (
        P(("dp", "tensor"), None),
        P(("dp", "tensor"), None),
        P("dp", None, "tensor"),
        P(None, "tensor", "dp"),
        P("tensor", "dp"),
        P("dp", "tensor"),
        P("tensor", "dp"),
        P("tensor", "dp"),
        P(None, ("dp", "tensor")),
        P(None, ("dp", "tensor")),
    )
    return jax.shard_map(shards, mesh=mesh, in_specs=in_specs, out_specs=out_specs, check_vma=False)
```

```python
import functools

import jax
import jax.numpy as jnp
from jax import lax
from jax.experimental import pallas as pl
from jax.experimental.pallas import tpu as pltpu
from jax.sharding import PartitionSpec as P

ROT = 64
EPSILON = 1e-05
ROTARY_BASE = 10000.0
F32 = jnp.float32
BF16 = jnp.bfloat16
HALVES = [(0, 0), (0, 1), (2, 1), (2, 0), (6, 0), (6, 1), (4, 1), (4, 0)]
ORDER = HALVES + [(p ^ 1, h) for p, h in HALVES]


def cut(*values):
    return lax.optimization_barrier(values)


def is_power(n):
    return n & (n - 1) == 0


def fast_dp():
    return lax.axis_size("dp") == 8


def xor_shift(values, axis, bit):
    size = lax.axis_size(axis)
    return lax.ppermute(values, axis, [(i, i ^ bit) for i in range(size)])


def butterfly(values, axis):
    size = lax.axis_size(axis)
    if not is_power(size):
        return lax.psum(values, axis)
    bit = 1
    while bit < size:
        values = values + xor_shift(values, axis, bit)
        bit *= 2
    return values


def columns_kernel(index_ref, x_ref, o_ref, *, count, step):
    for j in range(count):
        at = pl.multiple_of(index_ref[j] * step, step)
        o_ref[:, j * step : (j + 1) * step] = x_ref[:, pl.ds(at, step)]


def take_columns(values, index):
    rows, width = values.shape
    count = index.shape[0]
    tile = rows // 2 if rows % 64 == 0 else rows
    return pl.pallas_call(
        functools.partial(columns_kernel, count=count, step=width // count),
        out_shape=jax.ShapeDtypeStruct(values.shape, values.dtype),
        grid_spec=pltpu.PrefetchScalarGridSpec(
            num_scalar_prefetch=1,
            grid=(rows // tile,),
            in_specs=[pl.BlockSpec((tile, width), lambda i, s: (i, 0))],
            out_specs=pl.BlockSpec((tile, width), lambda i, s: (i, 0)),
        ),
        name="columns",
    )(index, values)


FRAME = [[(me ^ p) * 2 + h for p, h in ORDER] for me in range(8)]
PLAIN = [[row.index(k) for k in range(16)] for row in FRAME]


def frame_index():
    return lax.dynamic_index_in_dim(jnp.array(FRAME, jnp.int32), lax.axis_index("dp"), 0, keepdims=False)


def plain_index():
    return lax.dynamic_index_in_dim(jnp.array(PLAIN, jnp.int32), lax.axis_index("dp"), 0, keepdims=False)


def to_frame(values):
    return take_columns(values, frame_index()) if fast_dp() else values


def from_frame(values):
    return take_columns(values, plain_index()) if fast_dp() else values


def dp_gather(shard):
    if not fast_dp():
        return [lax.all_gather(shard, "dp", axis=0, tiled=True)]
    half = shard.shape[0] // 2
    from_x = xor_shift(shard, "dp", 2)
    from_y = xor_shift(shard, "dp", 4)
    far_1 = xor_shift(from_y[:half], "dp", 2)
    far_2 = xor_shift(from_x[half:], "dp", 4)
    far = jnp.concatenate([far_1, far_2], axis=0)
    near = xor_shift(shard, "dp", 1)
    near_x = xor_shift(from_x, "dp", 1)
    near_y = xor_shift(from_y, "dp", 1)
    near_far = xor_shift(far, "dp", 1)
    out = []
    for own, x, f, y in ((shard, from_x, far, from_y), (near, near_x, near_far, near_y)):
        out += [own, x[half:], x[:half], f, y[half:], y[:half]]
    return out


def join(pieces, start, stop):
    return jnp.concatenate([p[:, start:stop] for p in pieces], axis=0)


def dp_scatter(make):
    away = make(1)
    came = xor_shift(away, "dp", 1)
    kept = make(0)
    rows = kept.shape[0] // 4
    half = rows // 2

    def summed(start, stop):
        return kept[start:stop].astype(F32) + came[start:stop].astype(F32)

    first_x = xor_shift(summed(rows + half, 2 * rows + half).astype(BF16), "dp", 2)
    first_y = xor_shift(summed(2 * rows + half, 3 * rows + half).astype(BF16), "dp", 4)
    last_x = summed(rows, rows + half) + first_y[:half].astype(F32)
    last_y = summed(3 * rows + half, 4 * rows) + first_x[half:].astype(F32)
    last_x = xor_shift(last_x.astype(BF16), "dp", 2)
    last_y = xor_shift(last_y.astype(BF16), "dp", 4)
    top = summed(0, half) + first_x[:half].astype(F32) + last_y.astype(F32)
    low = summed(half, rows) + first_y[half:].astype(F32) + last_x.astype(F32)
    return jnp.concatenate([top, low], axis=0)


def weight_grad(rows, columns):
    def make(part):
        width = rows.shape[1] // 2
        chosen = rows[:, part * width : (part + 1) * width]
        return jnp.einsum("nd,nf->df", chosen, columns, preferred_element_type=F32).astype(BF16)

    if fast_dp():
        return dp_scatter(make)
    whole = jnp.einsum("nd,nf->df", rows, columns, preferred_element_type=F32).astype(BF16)
    return lax.psum_scatter(whole, "dp", scatter_dimension=0, tiled=True).astype(F32)


def line_gather(block):
    size = lax.axis_size("tensor")
    me = lax.axis_index("tensor")
    up = down = block
    ups, downs = [block], [block]
    for s in range(size - 1):
        up = lax.ppermute(up, "tensor", [(i, i + 1) for i in range(s, size - 1)])
        down = lax.ppermute(down, "tensor", [(i + 1, i) for i in range(size - 1 - s)])
        ups.append(up)
        downs.append(down)
    blocks = [block]
    for r in range(1, size):
        blocks.append(jnp.where(me + r < size, downs[r], ups[size - r]))
    return jnp.concatenate(blocks, axis=0)


def line_scatter(terms):
    size = lax.axis_size("tensor")
    rows = terms.shape[0] // size

    def block(r):
        return terms[r * rows : (r + 1) * rows]

    up = down = None
    for s in range(1, size):
        to_up, to_down = block(size - s), block(s)
        if s > 1:
            to_up = (to_up.astype(F32) + up.astype(F32)).astype(BF16)
            to_down = (to_down.astype(F32) + down.astype(F32)).astype(BF16)
        up = lax.ppermute(to_up, "tensor", [(i, i + 1) for i in range(s)])
        down = lax.ppermute(to_down, "tensor", [(i, i - 1) for i in range(size - s, size)])
    return block(0).astype(F32) + up.astype(F32) + down.astype(F32)


def turn(values, cosine, low_sine, high_sine, sign):
    half = ROT // 2
    lanes = cosine.shape[-1]
    head = values[:, :lanes]
    turned = (
        head * cosine
        - sign * pltpu.roll(head, lanes - half, 1) * low_sine
        + sign * pltpu.roll(head, half, 1) * high_sine
    )
    return jnp.concatenate([turned, values[:, lanes:]], axis=1)


def contract(a, b, dims):
    return lax.dot_general(a, b, (dims, ((), ())), preferred_element_type=F32)


def masked(scores, column_starts, row_starts, query_block, block):
    keys = scores.shape[1]
    query = lax.broadcasted_iota(jnp.int32, scores.shape, 0) + query_block * block
    key = lax.broadcasted_iota(jnp.int32, scores.shape, 1)
    allowed = (column_starts == row_starts[:, :keys]) & (key <= query)
    return allowed, jnp.where(allowed, scores, -1e30)


SMALL = pl.CostEstimate(flops=1000, bytes_accessed=1000, transcendentals=0)


def spots(me_ref, size, block):
    def spot(b):
        return pl.ds(pl.multiple_of(lax.rem(b - me_ref[0] + size, size) * block, block), block)

    return spot


def forward_block(q_out, k_out, v_out, att_ref, log_ref, col_ref, row_ref, spot, b, block):
    scale = q_out.shape[-1] ** (-0.5)
    here = slice(b * block, (b + 1) * block)
    query = q_out[spot(b), :]
    scores = jnp.concatenate(
        [contract(query, k_out[spot(c), :], ((1,), (1,))) for c in range(b + 1)], axis=1
    ) * scale
    _, scores = masked(scores, col_ref[here, :1], row_ref[:1, :], b, block)
    top = jnp.max(scores, axis=1, keepdims=True)
    powers = jnp.exp(scores - top)
    total = jnp.sum(powers, axis=1, keepdims=True)
    weights = (powers / total).astype(BF16)
    attended = contract(weights[:, :block], v_out[spot(0), :], ((1,), (0,)))
    for c in range(1, b + 1):
        attended = attended + contract(
            weights[:, c * block : (c + 1) * block], v_out[spot(c), :], ((1,), (0,))
        )
    att_ref[spot(b), :] = attended.astype(BF16)
    log_ref[0, here, :] = jnp.broadcast_to(top + jnp.log(total), (block, log_ref.shape[2]))


def forward_kernel(
    me_ref, q_ref, k_ref, v_ref, cos_ref, low_ref, high_ref, col_ref, row_ref,
    q_out, k_out, v_out, att_ref, log_ref, *, size, block,
):
    spot = spots(me_ref, size, block)
    for b in range(size):
        here = slice(b * block, (b + 1) * block)
        at = spot(b)
        tables = cos_ref[here, :], low_ref[here, :], high_ref[here, :]
        q_out[at, :] = turn(q_ref[at, :], *tables, 1.0).astype(BF16)
        k_out[at, :] = turn(k_ref[at, :], *tables, 1.0).astype(BF16)
        v_out[at, :] = v_ref[at, :].astype(BF16)
    for b in range(size):
        forward_block(q_out, k_out, v_out, att_ref, log_ref, col_ref, row_ref, spot, b, block)


def joined_forward_kernel(
    me_ref, rows_ref, qa_ref, ka_ref, va_ref, qb_ref, kb_ref, vb_ref, q_bias, k_bias, v_bias,
    cos_ref, low_ref, high_ref, col_ref, row_ref,
    q_out, k_out, v_out, att_ref, log_ref, *, size, block,
):
    spot = spots(me_ref, size, block)
    middle = qa_ref.shape[0]
    for b in range(size):
        here = slice(b * block, (b + 1) * block)
        at = spot(b)
        tables = cos_ref[here, :], low_ref[here, :], high_ref[here, :]
        top, low = rows_ref[at, :middle], rows_ref[at, middle:]

        def project(one, two, bias):
            return contract(top, one[:, :], ((1,), (0,))) + contract(low, two[:, :], ((1,), (0,))) + bias[:, :]

        q_out[at, :] = turn(project(qa_ref, qb_ref, q_bias), *tables, 1.0).astype(BF16)
        k_out[at, :] = turn(project(ka_ref, kb_ref, k_bias), *tables, 1.0).astype(BF16)
        v_out[at, :] = project(va_ref, vb_ref, v_bias).astype(BF16)
        forward_block(q_out, k_out, v_out, att_ref, log_ref, col_ref, row_ref, spot, b, block)


def backward_pass(
    q_ref, k_ref, v_ref, g_ref, log_ref, cos_ref, low_ref, high_ref, col_ref, row_ref,
    put, k_acc, v_acc, spot, size, block,
):
    scale = q_ref.shape[-1] ** (-0.5)
    for b in range(size):
        here = slice(b * block, (b + 1) * block)
        query, grad = q_ref[spot(b), :], g_ref[spot(b), :]
        scores = jnp.concatenate(
            [contract(query, k_ref[spot(c), :], ((1,), (1,))) for c in range(b + 1)], axis=1
        ) * scale
        allowed, scores = masked(scores, col_ref[here, :1], row_ref[:1, :], b, block)
        probs = jnp.where(allowed, jnp.exp(scores - log_ref[0, here, :1]), 0.0)
        grad_probs = jnp.concatenate(
            [contract(grad, v_ref[spot(c), :], ((1,), (1,))) for c in range(b + 1)], axis=1
        )
        inner = jnp.sum(probs * grad_probs, axis=1, keepdims=True)
        weights = probs.astype(BF16)
        grad_scores = (probs * (grad_probs - inner)).astype(BF16)
        back = None
        for c in range(b + 1):
            part = slice(c * block, (c + 1) * block)
            key_term = contract(grad_scores[:, part], query, ((0,), (0,)))
            value_term = contract(weights[:, part], grad, ((0,), (0,)))
            query_term = contract(grad_scores[:, part], k_ref[spot(c), :], ((1,), (0,)))
            back = query_term if c == 0 else back + query_term
            if c == b:
                k_acc[part, :] = key_term
                v_acc[part, :] = value_term
            else:
                k_acc[part, :] += key_term
                v_acc[part, :] += value_term
        tables = cos_ref[here, :], low_ref[here, :], high_ref[here, :]
        put(0, spot(b), turn(back * scale, *tables, -1.0).astype(BF16))
    for b in range(size):
        here = slice(b * block, (b + 1) * block)
        tables = cos_ref[here, :], low_ref[here, :], high_ref[here, :]
        put(1, spot(b), turn(k_acc[here, :] * scale, *tables, -1.0).astype(BF16))
        put(2, spot(b), v_acc[here, :].astype(BF16))


def backward_kernel(
    me_ref, q_ref, k_ref, v_ref, g_ref, log_ref, cos_ref, low_ref, high_ref, col_ref, row_ref,
    dq_ref, dk_ref, dv_ref, k_acc, v_acc, *, size, block,
):
    outs = (dq_ref, dk_ref, dv_ref)

    def put(k, at, value):
        outs[k][at, :] = value

    backward_pass(
        q_ref, k_ref, v_ref, g_ref, log_ref, cos_ref, low_ref, high_ref, col_ref, row_ref,
        put, k_acc, v_acc, spots(me_ref, size, block), size, block,
    )


def mixed_backward_kernel(
    me_ref, q_ref, k_ref, v_ref, g_ref, a_ref, b_ref, log_ref, cos_ref, low_ref, high_ref, col_ref, row_ref,
    d_ref, k_acc, v_acc, g_acc, *, size, block, heads,
):
    middle = a_ref.shape[0]
    head = q_ref.shape[1]
    for b in range(size):
        here = slice(b * block, (b + 1) * block)
        g_acc[here, :] = (
            contract(g_ref[here, :middle], a_ref[:, :], ((1,), (0,)))
            + contract(g_ref[here, middle:], b_ref[:, :], ((1,), (0,)))
        ).astype(BF16)
    h = pl.program_id(0)

    def put(k, at, value):
        d_ref[at, pl.ds(pl.multiple_of((k * heads + h) * head, head), head)] = value

    backward_pass(
        q_ref, k_ref, v_ref, g_acc, log_ref, cos_ref, low_ref, high_ref, col_ref, row_ref,
        put, k_acc, v_acc, spots(me_ref, size, block), size, block,
    )


def hidden_kernel(rows_ref, a_ref, b_ref, bias_ref, act_ref, slope_ref, *, step):
    middle = a_ref.shape[0]
    for i in range(rows_ref.shape[0] // step):
        here = slice(i * step, (i + 1) * step)
        hidden = contract(rows_ref[here, :middle], a_ref[:, :], ((1,), (0,)))
        hidden = hidden + contract(rows_ref[here, middle:], b_ref[:, :], ((1,), (0,))) + bias_ref[:, :]
        bell = lax.erf(hidden * (0.5**0.5))
        act_ref[here, :] = (0.5 * hidden * (1.0 + bell)).astype(BF16)
        slope = 0.5 * (1.0 + bell) + hidden * jnp.exp(-0.5 * hidden * hidden) * 0.3989422804014327
        slope_ref[here, :] = slope.astype(BF16)


def hidden_half(rows, top, low, bias):
    count, width = rows.shape
    out = top.shape[1]
    tile = 512
    half = pl.BlockSpec((width // 2, tile), lambda j: (0, j))
    made = pl.BlockSpec((count, tile), lambda j: (0, j))
    return pl.pallas_call(
        functools.partial(hidden_kernel, step=256),
        out_shape=(jax.ShapeDtypeStruct((count, out), BF16),) * 2,
        grid=(out // tile,),
        in_specs=[
            pl.BlockSpec((count, width), lambda j: (0, 0)), half, half, pl.BlockSpec((1, tile), lambda j: (0, j))
        ],
        out_specs=(made, made),
        cost_estimate=SMALL,
        name="hidden",
    )(rows, top, low, bias.reshape(1, -1))


def slope_kernel(rows_ref, a_ref, b_ref, slope_ref, out_ref, *, step):
    middle = a_ref.shape[0]
    for i in range(rows_ref.shape[0] // step):
        here = slice(i * step, (i + 1) * step)
        active = contract(rows_ref[here, :middle], a_ref[:, :], ((1,), (0,)))
        active = active + contract(rows_ref[here, middle:], b_ref[:, :], ((1,), (0,)))
        out_ref[here, :] = (active * slope_ref[here, :].astype(F32)).astype(BF16)


def hidden_back(rows, top, low, slope):
    count, width = rows.shape
    out = top.shape[1]
    tile = 512
    half = pl.BlockSpec((top.shape[0], tile), lambda j: (0, j))
    made = pl.BlockSpec((count, tile), lambda j: (0, j))
    return pl.pallas_call(
        functools.partial(slope_kernel, step=256),
        out_shape=jax.ShapeDtypeStruct((count, out), BF16),
        grid=(out // tile,),
        in_specs=[pl.BlockSpec((count, width), lambda j: (0, 0)), half, half, made],
        out_specs=made,
        cost_estimate=SMALL,
        name="hidden_back",
    )(rows, top, low, slope)


def branch_kernel(att_ref, mix_ref, act_ref, down_ref, out_ref, *, step):
    for i in range(att_ref.shape[0] // step):
        here = slice(i * step, (i + 1) * step)
        total = contract(att_ref[here, :], mix_ref[:, :], ((1,), (1,)))
        total = total + contract(act_ref[here, :], down_ref[:, :], ((1,), (1,)))
        out_ref[here, :] = total.astype(BF16)


def branch_half(attended, mixed, activated, down):
    count, inner = attended.shape
    units = activated.shape[1]
    width = down.shape[0]
    tile = 256
    spot = mixed.shape[1] // inner - 1
    return pl.pallas_call(
        functools.partial(branch_kernel, step=256),
        out_shape=jax.ShapeDtypeStruct((count, width), BF16),
        grid=(width // tile,),
        in_specs=[
            pl.BlockSpec((count, inner), lambda j: (0, 0)),
            pl.BlockSpec((tile, inner), lambda j: (j + width // tile, spot)),
            pl.BlockSpec((count, units), lambda j: (0, 0)),
            pl.BlockSpec((tile, units), lambda j: (j, 0)),
        ],
        out_specs=pl.BlockSpec((count, tile), lambda j: (0, j)),
        cost_estimate=SMALL,
        name="branches",
    )(attended, mixed, activated, down)


def back_kernel(
    hid_ref, proj_ref, up_ref, join_ref, tok_ref, mean_ref, scale_ref, gain_ref, back_ref, sum_ref, *, step
):
    sums = [0.0] * 4
    for i in range(hid_ref.shape[0] // step):
        here = slice(i * step, (i + 1) * step)
        two = contract(hid_ref[here, :], up_ref[:, :], ((1,), (1,)))
        one = contract(proj_ref[here, :], join_ref[:, :], ((1,), (1,)))
        back_ref[here, :] = (one * gain_ref[:1, :] + two * gain_ref[1:2, :]).astype(BF16)
        xhat = (tok_ref[here, :].astype(F32) - mean_ref[here, :1]) * scale_ref[here, :1]
        for k, term in enumerate((one * xhat, two * xhat, one, two)):
            sums[k] = sums[k] + jnp.sum(term, axis=0, keepdims=True)
    for k in range(4):
        sum_ref[k : k + 1, :] = sums[k]


def back_half(grad_hidden, grad_projected, both, token_rows, mean, scale, gains, part):
    count, units = grad_hidden.shape
    joined = grad_projected.shape[1]
    width = both.shape[0] // 2
    tile = 256
    tiles = width // tile
    whole = lambda j: (0, 0)
    return pl.pallas_call(
        functools.partial(back_kernel, step=256),
        out_shape=(jax.ShapeDtypeStruct((count, width), BF16), jax.ShapeDtypeStruct((8, width), F32)),
        grid=(tiles,),
        in_specs=[
            pl.BlockSpec((count, units), whole),
            pl.BlockSpec((count, joined), whole),
            pl.BlockSpec((tile, units), lambda j: (j, 0)),
            pl.BlockSpec((tile, joined), lambda j: (j + tiles, 0)),
            pl.BlockSpec((count, tile), lambda j: (0, j + part * tiles)),
            pl.BlockSpec((count, 128), whole),
            pl.BlockSpec((count, 128), whole),
            pl.BlockSpec((2, tile), lambda j: (0, j + part * tiles)),
        ],
        out_specs=(pl.BlockSpec((count, tile), lambda j: (0, j)), pl.BlockSpec((8, tile), lambda j: (0, j))),
        cost_estimate=SMALL,
        name="back",
    )(grad_hidden, grad_projected, both, both, token_rows, mean, scale, gains)


def lay_kernel(*refs):
    *ins, out_ref = refs
    rows = ins[0].shape[0]
    half = rows // 2
    for w in range(len(ins) // 3):
        own, from_x, from_y = ins[3 * w : 3 * w + 3]
        base = 4 * w * rows
        out_ref[base : base + rows, :] = own[:, :]
        out_ref[base + 2 * rows : base + 3 * rows, :] = jnp.zeros(own.shape, BF16)
        for piece, at in ((from_x, base + rows), (from_y, base + 3 * rows)):
            out_ref[at : at + half, :] = piece[half:, :]
            out_ref[at + half : at + rows, :] = piece[:half, :]


def lay(*pieces):
    rows, width = pieces[0].shape
    weights = len(pieces) // 3
    tile = width // 4
    return pl.pallas_call(
        lay_kernel,
        out_shape=jax.ShapeDtypeStruct((4 * rows * weights, width), BF16),
        grid=(4,),
        in_specs=[pl.BlockSpec((rows, tile), lambda j: (0, j))] * len(pieces),
        out_specs=pl.BlockSpec((4 * rows * weights, tile), lambda j: (0, j)),
        cost_estimate=SMALL,
        name="lay",
    )(*pieces)


def terms_kernel(*refs):
    *ins, to_up, to_down = refs
    up = jnp.concatenate([ins[0][:, :], ins[1][:, :]], axis=1)
    down = jnp.concatenate([ins[2][:, :], ins[3][:, :]], axis=1)
    if len(ins) > 4:
        up = (up.astype(F32) + ins[4][:, :].astype(F32)).astype(BF16)
        down = (down.astype(F32) + ins[5][:, :].astype(F32)).astype(BF16)
    to_up[:, :] = up
    to_down[:, :] = down


def step_terms(halves, up_block, down_block, rows, *came):
    width = halves[0].shape[1]
    tiles = 2
    tile = rows // tiles

    def of(block):
        return [pl.BlockSpec((tile, width), lambda i: (block * tiles + i, 0))] * 2

    full = pl.BlockSpec((tile, 2 * width), lambda i: (i, 0))
    return pl.pallas_call(
        terms_kernel,
        out_shape=(jax.ShapeDtypeStruct((rows, 2 * width), BF16),) * 2,
        grid=(tiles,),
        in_specs=of(up_block) + of(down_block) + [full] * len(came),
        out_specs=(full, full),
        cost_estimate=SMALL,
        name="terms",
    )(*halves, *halves, *came)


def input_grad_kernel(index_ref, one_ref, two_ref, up_ref, down_ref, tok_ref, grad_ref, out_ref):
    back = jnp.concatenate([one_ref[:, :], two_ref[:, :]], axis=1).astype(F32)
    back = back + up_ref[:, :].astype(F32) + down_ref[:, :].astype(F32)
    xhat, scale = standardize(tok_ref[:, :])
    back = back - jnp.mean(back, axis=-1, keepdims=True) - xhat * jnp.mean(back * xhat, axis=-1, keepdims=True)
    total = grad_ref[:, :].astype(F32) + back * scale
    count = index_ref.shape[0]
    step = total.shape[1] // count
    for j in range(count):
        out_ref[:, pl.ds(pl.multiple_of(index_ref[j] * step, step), step)] = total[:, j * step : (j + 1) * step]


def input_grad_rows(one, two, up, down, tokens, grads):
    rows, width = tokens.shape
    tile = rows // 4
    half = pl.BlockSpec((tile, width // 2), lambda i, s: (i, 0))
    full = pl.BlockSpec((tile, width), lambda i, s: (i, 0))
    return pl.pallas_call(
        input_grad_kernel,
        out_shape=jax.ShapeDtypeStruct((rows, width), F32),
        grid_spec=pltpu.PrefetchScalarGridSpec(
            num_scalar_prefetch=1,
            grid=(rows // tile,),
            in_specs=[half, half, full, full, full, full],
            out_specs=full,
        ),
        cost_estimate=SMALL,
        name="input_grad",
    )(frame_index(), one, two, up, down, tokens, grads)


def joined_forward(rows, top, low, bias, tables, me, heads, head, size):
    count, width = rows.shape
    block = count // size
    whole = lambda h, s: (0, 0)
    table_specs = [pl.BlockSpec((count, 128), whole)] * 4 + [pl.BlockSpec((8, count), whole)]
    by_head = pl.BlockSpec((count, head), lambda h, s: (0, h))
    wide = jax.ShapeDtypeStruct((count, heads * head), BF16)

    def thirds(n, spot):
        return [pl.BlockSpec((n, head), lambda h, s, k=k: (spot, k * heads + h)) for k in range(3)]

    return pl.pallas_call(
        functools.partial(joined_forward_kernel, size=size, block=block),
        out_shape=(wide, wide, wide, wide, jax.ShapeDtypeStruct((heads, count, 128), F32)),
        grid_spec=pltpu.PrefetchScalarGridSpec(
            num_scalar_prefetch=1,
            grid=(heads,),
            in_specs=[pl.BlockSpec((count, width), whole)]
            + thirds(width // 2, 1) + thirds(width // 2, 1) + thirds(1, 0) + table_specs,
            out_specs=(by_head,) * 4 + (pl.BlockSpec((1, count, 128), lambda h, s: (h, 0, 0)),),
        ),
        cost_estimate=SMALL,
        name="joined_forward",
    )(me, rows, top, top, top, low, low, low, bias, bias, bias, *tables)


def mixed_backward(queries, keys, values, grads, top, low, log_total, tables, me, heads, size):
    count = queries.shape[0]
    head = queries.shape[1] // heads
    block = count // size
    whole = lambda h, s: (0, 0)
    table_specs = [pl.BlockSpec((count, 128), whole)] * 4 + [pl.BlockSpec((8, count), whole)]
    by_head = pl.BlockSpec((count, head), lambda h, s: (0, h))
    mix = pl.BlockSpec((grads.shape[1] // 2, head), lambda h, s: (1, 3 * heads + h))
    return pl.pallas_call(
        functools.partial(mixed_backward_kernel, size=size, block=block, heads=heads),
        out_shape=jax.ShapeDtypeStruct((count, 3 * heads * head), BF16),
        grid_spec=pltpu.PrefetchScalarGridSpec(
            num_scalar_prefetch=1,
            grid=(heads,),
            in_specs=[by_head] * 3
            + [pl.BlockSpec((count, grads.shape[1]), whole), mix, mix]
            + [pl.BlockSpec((1, count, 128), lambda h, s: (h, 0, 0))]
            + table_specs,
            out_specs=pl.BlockSpec((count, 3 * heads * head), whole),
            scratch_shapes=[pltpu.VMEM((count, head), F32)] * 2 + [pltpu.VMEM((count, head), BF16)],
        ),
        cost_estimate=SMALL,
        name="mixed_backward",
    )(me, queries, keys, values, grads, top, low, log_total, *tables)


def attention_tables(positions, starts):
    half = ROT // 2
    frequency = ROTARY_BASE ** (-(jnp.arange(half, dtype=F32) * 2.0) / ROT)
    angles = positions.astype(F32)[:, None] * frequency[None, :]
    cosine, sine = jnp.cos(angles), jnp.sin(angles)
    rows = positions.shape[0]
    cosines = jnp.concatenate([cosine, cosine, jnp.ones((rows, 128 - ROT), F32)], axis=1)
    low = jnp.concatenate([sine, jnp.zeros((rows, 128 - half), F32)], axis=1)
    high = jnp.concatenate([jnp.zeros((rows, half), F32), sine, jnp.zeros((rows, 128 - ROT), F32)], axis=1)
    columns = jnp.broadcast_to(starts[:, None], (rows, 128))
    across = jnp.broadcast_to(starts[None, :], (8, rows))
    return cosines, low, high, columns, across


def attention_forward(projected, tables, me, heads, size):
    rows = projected.shape[0]
    head = projected.shape[1] // (3 * heads)
    block = rows // size
    whole = lambda h, s: (0, 0)
    table_specs = [pl.BlockSpec((rows, 128), whole)] * 4 + [pl.BlockSpec((8, rows), whole)]
    by_head = pl.BlockSpec((rows, head), lambda h, s: (0, h))
    wide = jax.ShapeDtypeStruct((rows, heads * head), BF16)
    return pl.pallas_call(
        functools.partial(forward_kernel, size=size, block=block),
        out_shape=(wide, wide, wide, wide, jax.ShapeDtypeStruct((heads, rows, 128), F32)),
        grid_spec=pltpu.PrefetchScalarGridSpec(
            num_scalar_prefetch=1,
            grid=(heads,),
            in_specs=[
                pl.BlockSpec((rows, head), lambda h, s, k=k: (0, k * heads + h)) for k in range(3)
            ]
            + table_specs,
            out_specs=(by_head,) * 4 + (pl.BlockSpec((1, rows, 128), lambda h, s: (h, 0, 0)),),
        ),
        cost_estimate=pl.CostEstimate(
            flops=heads * rows * rows * head * 40, bytes_accessed=rows * head * heads * 24,
            transcendentals=heads * rows * rows // 2,
        ),
        name="attention_forward",
    )(me, projected, projected, projected, *tables)


def attention_backward(queries, keys, values, grads, log_total, tables, me, heads, size):
    rows = queries.shape[0]
    head = queries.shape[1] // heads
    block = rows // size
    whole = lambda h, s: (0, 0)
    table_specs = [pl.BlockSpec((rows, 128), whole)] * 4 + [pl.BlockSpec((8, rows), whole)]
    by_head = pl.BlockSpec((rows, head), lambda h, s: (0, h))
    wide = jax.ShapeDtypeStruct((rows, heads * head), BF16)
    return pl.pallas_call(
        functools.partial(backward_kernel, size=size, block=block),
        out_shape=(wide, wide, wide),
        grid_spec=pltpu.PrefetchScalarGridSpec(
            num_scalar_prefetch=1,
            grid=(heads,),
            in_specs=[by_head] * 4
            + [pl.BlockSpec((1, rows, 128), lambda h, s: (h, 0, 0))]
            + table_specs,
            out_specs=(by_head,) * 3,
            scratch_shapes=[pltpu.VMEM((rows, head), F32)] * 2,
        ),
        cost_estimate=pl.CostEstimate(
            flops=heads * rows * rows * head * 60, bytes_accessed=rows * head * heads * 24,
            transcendentals=heads * rows * rows // 2,
        ),
        name="attention_backward",
    )(me, queries, keys, values, grads, log_total, *tables)


def standardize(values):
    values = values.astype(F32)
    centered = values - jnp.mean(values, axis=-1, keepdims=True)
    spread = jnp.mean(centered * centered, axis=-1, keepdims=True)
    scale = lax.rsqrt(spread + EPSILON)
    return centered * scale, scale


def norm_rows(token_rows, gain_rows, shift_rows):
    xhat, _ = standardize(token_rows)
    first_rows = (xhat * gain_rows[0] + shift_rows[0]).astype(BF16)
    second_rows = (xhat * gain_rows[1] + shift_rows[1]).astype(BF16)
    return first_rows, second_rows


def hidden_units(second_rows, up_rows, hidden_bias):
    hidden = jnp.dot(second_rows, up_rows, preferred_element_type=F32) + hidden_bias
    bell = lax.erf(hidden * (0.5**0.5))
    activated = (0.5 * hidden * (1.0 + bell)).astype(BF16)
    slope = 0.5 * (1.0 + bell) + hidden * jnp.exp(-0.5 * hidden * hidden) * 0.3989422804014327
    return activated, slope.astype(BF16)


def branch_rows(attended, mix_rows, activated, down_rows):
    return (
        jnp.einsum("ne,de->nd", attended, mix_rows, preferred_element_type=F32)
        + jnp.einsum("nf,df->nd", activated, down_rows, preferred_element_type=F32)
    ).astype(BF16)


def hidden_grads(grad_rows, down_rows, slope):
    grad_active = jnp.einsum("nd,df->nf", grad_rows, down_rows, preferred_element_type=F32)
    return (grad_active * slope.astype(F32)).astype(BF16)


def attended_grads(grad_rows, mix_rows):
    return jnp.einsum("nd,de->ne", grad_rows, mix_rows, preferred_element_type=F32).astype(BF16)


def back_rows(grads, weight_rows):
    return jnp.einsum("nf,df->nd", grads, weight_rows, preferred_element_type=F32)


def grad_half(rows, columns, part):
    width = rows.shape[1] // 2
    chosen = rows[:, part * width : (part + 1) * width]
    return jnp.einsum("nd,nf->df", chosen, columns, preferred_element_type=F32).astype(BF16)


def plus(*terms):
    return functools.reduce(lambda a, b: a + b, [t.astype(F32) for t in terms])


def width_sums(grad_first, grad_second, xhat, grad_local):
    return jnp.stack(
        [
            jnp.sum(grad_first * xhat, axis=0),
            jnp.sum(grad_second * xhat, axis=0),
            jnp.sum(grad_first, axis=0),
            jnp.sum(grad_second, axis=0),
            jnp.sum(grad_local.astype(F32), axis=0),
        ],
        axis=0,
    )


def shards(
    tokens,
    seq_start,
    proj_weight,
    proj_bias,
    out_weight,
    up_weight,
    up_bias,
    down_weight,
    norm_gains,
    biases,
    cotangent,
):
    local_rows, width = tokens.shape
    n_dp, n_tensor = lax.axis_size("dp"), lax.axis_size("tensor")
    dp_index, tensor_index = lax.axis_index("dp"), lax.axis_index("tensor")
    row_count = local_rows * n_tensor
    hidden_width = up_weight.shape[1]
    heads_here = proj_bias.shape[1]
    head_size = proj_bias.shape[2] * n_dp
    local_width = heads_here * head_size
    joined_width = 3 * local_width
    columns = norm_gains.shape[1]

    vectors = jnp.concatenate(
        [norm_gains.reshape(1, -1), biases.reshape(1, -1), proj_bias.reshape(1, -1), up_bias.reshape(1, -1)],
        axis=1,
    )
    table = jnp.zeros((n_dp * n_tensor, vectors.shape[1]), BF16)
    table = lax.dynamic_update_slice(table, vectors, (dp_index * n_tensor + tensor_index, 0))
    local_tokens, local_grads = to_frame(tokens), to_frame(cotangent)
    positions = dp_index * row_count + jnp.arange(row_count, dtype=jnp.int32) - seq_start
    tables = attention_tables(positions, seq_start)
    me = tensor_index.astype(jnp.int32).reshape(1)
    flat_proj = proj_weight.reshape(-1, joined_width)

    def small_parameters(table):
        six_rows = table[:, : 6 * columns].reshape(n_dp * n_tensor, 6, columns).transpose(1, 0, 2)
        six_rows = to_frame(six_rows.reshape(6, width).astype(F32))
        of_tensor = lax.dynamic_index_in_dim(
            table[:, 6 * columns :].reshape(n_dp, n_tensor, -1), tensor_index, 1, keepdims=False
        ).astype(F32)
        joined_bias = (
            of_tensor[:, : proj_bias.size]
            .reshape(n_dp, 3, heads_here, -1)
            .transpose(1, 2, 0, 3)
            .reshape(joined_width)
        )
        hidden_bias = of_tensor[:, proj_bias.size :].reshape(hidden_width)
        return six_rows[:2], six_rows[2:], joined_bias, hidden_bias

    def attend(first_rows, joined_rows, joined_bias):
        projected = jnp.dot(first_rows, joined_rows, preferred_element_type=F32) + joined_bias
        return attention_forward(projected, tables, me, heads_here, n_tensor)

    def attend_back(kept, grad_attended):
        queries, keys, values, log_total = kept
        backs = attention_backward(
            queries, keys, values, grad_attended, log_total, tables, me, heads_here, n_tensor
        )
        return jnp.concatenate(backs, axis=1)

    def finish_output(branches, shift_rows):
        output = local_tokens.astype(F32) + branches + shift_rows[2] + shift_rows[3]
        return from_frame(output.astype(BF16))

    def finish_input_grad(back):
        xhat_local, scale_local = standardize(local_tokens)
        grad_norm_in = (
            back
            - jnp.mean(back, axis=-1, keepdims=True)
            - xhat_local * jnp.mean(back * xhat_local, axis=-1, keepdims=True)
        ) * scale_local
        return from_frame(local_grads.astype(F32) + grad_norm_in)

    def small_shares(five, joined_bias_sums, up_bias_sums):
        five = five.reshape(5, width)
        mine = lax.dynamic_slice_in_dim(
            five, (dp_index * n_tensor + tensor_index) * columns, columns, 1
        )
        biases_grad = jnp.concatenate([mine[2:], mine[4:]], axis=0)
        joined_bias_sum = lax.dynamic_slice_in_dim(
            joined_bias_sums.reshape(3, heads_here, head_size),
            dp_index * proj_bias.shape[2],
            proj_bias.shape[2],
            2,
        )
        up_bias_sum = lax.dynamic_slice_in_dim(
            up_bias_sums.reshape(1, -1), dp_index * up_bias.shape[1], up_bias.shape[1], 1
        )
        return mine[:2], biases_grad, joined_bias_sum, up_bias_sum

    def small_grads(five, joined_bias_term, up_bias_term):
        five = from_frame(five).reshape(1, -1)
        terms = jnp.concatenate([five, joined_bias_term[None], up_bias_term[None]], axis=1)
        terms = butterfly(terms, "dp")
        five = butterfly(terms[:, : 5 * width], "tensor")
        return small_shares(
            five, terms[0, 5 * width : 5 * width + joined_width], terms[:, 5 * width + joined_width :]
        )

    def plain():
        token_rows, grad_rows = line_gather(local_tokens), line_gather(local_grads)
        up_rows, down_rows = dp_gather(up_weight), dp_gather(down_weight.T)
        joined_rows, mix_rows = dp_gather(flat_proj), dp_gather(out_weight.T)
        up_rows, down_rows, joined_rows, mix_rows = (
            join(w, 0, None) for w in (up_rows, down_rows, joined_rows, mix_rows)
        )
        gain_rows, shift_rows, joined_bias, hidden_bias = small_parameters(
            butterfly(butterfly(table, "dp"), "tensor")
        )
        first_rows, second_rows = norm_rows(token_rows, gain_rows, shift_rows)
        activated, slope = cut(*hidden_units(second_rows, up_rows, hidden_bias))
        *kept, attended, log_total = attend(first_rows, joined_rows, joined_bias)
        branches = line_scatter(branch_rows(attended, mix_rows, activated, down_rows))
        output = finish_output(branches, shift_rows)
        grad_hidden = hidden_grads(grad_rows, down_rows, slope)
        down_sum = weight_grad(grad_rows, activated)
        up_sum = weight_grad(second_rows, grad_hidden)
        grad_second = back_rows(grad_hidden, up_rows)
        grad_attended = attended_grads(grad_rows, mix_rows)
        mix_sum = weight_grad(grad_rows, attended)
        grad_projected = attend_back((*kept, log_total), grad_attended)
        joined_sum = weight_grad(first_rows, grad_projected)
        grad_first = back_rows(grad_projected, joined_rows)
        back = grad_first * gain_rows[0] + grad_second * gain_rows[1]
        input_grad = finish_input_grad(line_scatter(back.astype(BF16)))
        five = width_sums(grad_first, grad_second, standardize(token_rows)[0], local_grads)
        small = small_grads(
            five, jnp.sum(grad_projected, axis=0, dtype=F32), jnp.sum(grad_hidden, axis=0, dtype=F32)
        )
        return output, input_grad, joined_sum, mix_sum.T, up_sum, down_sum.T, small

    def staged():
        half = local_rows // 2
        first, second = slice(0, half), slice(half, 2 * half)

        def x(values):
            return xor_shift(values, "dp", 2)

        def y(values):
            return xor_shift(values, "dp", 4)

        def core(values):
            return xor_shift(values, "dp", 1)

        def gather_step(up, down, s):
            up = lax.ppermute(up, "tensor", [(i, i + 1) for i in range(s, 3)])
            down = lax.ppermute(down, "tensor", [(i + 1, i) for i in range(3 - s)])
            return up, down

        def scatter_terms(halves, up, down, s):
            came = () if s == 1 else (up, down)
            return step_terms(halves, 4 - s, s, local_rows, *came)

        def scatter_step(to_up, to_down, s):
            up = lax.ppermute(to_up, "tensor", [(i, i + 1) for i in range(s)])
            down = lax.ppermute(to_down, "tensor", [(i, i - 1) for i in range(4 - s, 4)])
            return up, down

        def in_turn(block, ups, downs):
            blocks = [block] + [
                jnp.where(tensor_index + r < 4, downs[r - 1], ups[3 - r]) for r in range(1, 4)
            ]
            return jnp.concatenate(blocks, axis=0)

        def pair(top, low):
            return jnp.concatenate([top, low], axis=0)

        def place(base, piece, part):
            return lax.dynamic_update_slice(base, piece, ((4 * part + 2) * local_rows, 0))

        def at(keep, came, start, stop):
            return plus(keep[start * half : stop * half], came[start * half : stop * half])

        def joined_half(first_rows, grad_projected, grad_rows, attended, part):
            return jnp.concatenate(
                [grad_half(first_rows, grad_projected, part), grad_half(grad_rows, attended, part)], axis=1
            )

        wa = up_weight
        wb = jnp.concatenate([flat_proj, out_weight.T], axis=1)
        wc = down_weight.T

        ax, ay = x(wa), y(wa)
        tu1, td1 = gather_step(local_tokens, local_tokens, 0)
        table1 = table + core(table)
        table1, ax, ay = cut(table1, ax, ay)
        table1 = table1 + x(table1) + y(table1) + xor_shift(table1, "dp", 6)
        tu1, td1, ax, ay, table1, wb, wc, tables1 = cut(tu1, td1, ax, ay, table1, wb, wc, tables)
        tu2, td2 = gather_step(tu1, td1, 1)
        bx, by = x(wb), y(wb)
        table2 = table1 + xor_shift(table1, "tensor", 1)
        tu2, td2, bx, by, table2, local_grads1 = cut(tu2, td2, bx, by, table2, local_grads)
        tu3, td3 = gather_step(tu2, td2, 2)
        fa, fb = x(ay), y(bx)
        table3 = table2 + xor_shift(table2, "tensor", 2)
        both = lay(wa, ax, ay, wb, bx, by)
        tu3, td3, fa, fb, table3, both = cut(tu3, td3, fa, fb, table3, both)
        both_1 = place(place(both, fa, 0), fb, 1)
        both_1, wc, local_grads1 = cut(both_1, wc, local_grads1)
        cu1, cd1 = gather_step(local_grads1, local_grads1, 0)
        cx, cy = x(wc), y(wc)
        both_2 = core(both_1)
        gain_rows, shift_rows, joined_bias, hidden_bias = small_parameters(table3)
        token_rows = in_turn(local_tokens, (tu1, tu2, tu3), (td1, td2, td3))
        first_rows, second_rows = norm_rows(token_rows, gain_rows, shift_rows)
        mean = jnp.mean(token_rows.astype(F32), axis=-1, keepdims=True)
        _, scale = standardize(token_rows)
        mean, scale = (jnp.broadcast_to(v, (row_count, 128)) for v in (mean, scale))
        activated, slope = hidden_half(second_rows, both_1, both_2, hidden_bias)
        cu1, cd1, cx, cy, both_1, both_2, first_rows, activated, slope = cut(
            cu1, cd1, cx, cy, both_1, both_2, first_rows, activated, slope
        )
        cu2, cd2 = gather_step(cu1, cd1, 1)
        fc = x(cy)
        down_0 = lay(wc, cx, cy)
        *kept, attended, log_total = joined_forward(
            first_rows, both_1, both_2, joined_bias.reshape(1, -1), tables1, me, heads_here, head_size, n_tensor
        )
        cu2, cd2, fc, attended, down_0, mean, scale = cut(cu2, cd2, fc, attended, down_0, mean, scale)
        cu3, cd3 = gather_step(cu2, cd2, 2)
        down_1 = place(down_0, fc, 0)
        down_2 = core(down_1)
        branch_1 = branch_half(attended, both_1, activated, down_1)
        branch_2 = branch_half(attended, both_2, activated, down_2)
        cu3, cd3, branch_1, branch_2, activated = cut(cu3, cd3, branch_1, branch_2, activated)
        branches = (branch_1, branch_2)
        zu, zd, activated, cu3, cd3 = cut(*scatter_terms(branches, None, None, 1), activated, cu3, cd3)
        bu, bd = scatter_step(zu, zd, 1)
        grad_rows = in_turn(local_grads1, (cu1, cu2, cu3), (cd1, cd2, cd3))
        came_d = core(grad_half(grad_rows, activated, 1))
        keep_d = grad_half(grad_rows, activated, 0)
        grad_hidden = hidden_back(grad_rows, down_1, down_2, slope)
        bu, bd, came_d, keep_d, grad_hidden, grad_rows = cut(
            bu, bd, came_d, keep_d, grad_hidden, grad_rows
        )
        zu, zd, sx, sy, second_rows, grad_hidden, grad_rows = cut(
            *scatter_terms(branches, bu, bd, 2),
            at(keep_d, came_d, 3, 5).astype(BF16),
            at(keep_d, came_d, 5, 7).astype(BF16),
            second_rows, grad_hidden, grad_rows,
        )
        bu, bd = scatter_step(zu, zd, 2)
        d1x, d1y = x(sx), y(sy)
        came_u = core(grad_half(second_rows, grad_hidden, 1))
        keep_u = grad_half(second_rows, grad_hidden, 0)
        grad_projected = mixed_backward(
            *kept, grad_rows, both_1, both_2, log_total, tables1, me, heads_here, n_tensor
        )
        bu, bd, d1x, d1y, came_u, keep_u, grad_projected, grad_hidden = cut(
            bu, bd, d1x, d1y, came_u, keep_u, grad_projected, grad_hidden
        )
        d2x = plus(at(keep_d, came_d, 2, 3), d1y[first]).astype(BF16)
        d2y = plus(at(keep_d, came_d, 7, 8), d1x[second]).astype(BF16)
        zu, zd, sx, sy, grad_hidden, grad_projected = cut(
            *scatter_terms(branches, bu, bd, 3),
            pair(d2x, at(keep_u, came_u, 4, 5).astype(BF16)),
            pair(d2y, at(keep_u, came_u, 5, 6).astype(BF16)),
            grad_hidden, grad_projected,
        )
        bu, bd = scatter_step(zu, zd, 3)
        s9x, s9y = x(sx), y(sy)
        came_j = core(joined_half(first_rows, grad_projected, grad_rows, attended, 1))
        back_1, sums_1 = back_half(grad_hidden, grad_projected, both_1, token_rows, mean, scale, gain_rows, 0)
        back_2, sums_2 = back_half(grad_hidden, grad_projected, both_2, token_rows, mean, scale, gain_rows, 1)
        bu, bd, s9x, s9y, came_j, back_1, back_2, sums_1, sums_2, grad_projected, attended = cut(
            bu, bd, s9x, s9y, came_j, back_1, back_2, sums_1, sums_2, grad_projected, attended
        )
        backs = (back_1, back_2)
        none = jnp.zeros((half, s9x.shape[1]), BF16)
        zu, zd, sx, sy, first_rows, grad_rows, bu, bd, sums_1, sums_2 = cut(
            *scatter_terms(backs, None, None, 1),
            plus(at(keep_u, came_u, 2, 4), pair(s9y[second], none)).astype(BF16),
            plus(at(keep_u, came_u, 6, 8), pair(none, s9x[second])).astype(BF16),
            first_rows, grad_rows, bu, bd, sums_1, sums_2,
        )
        eu, ed = scatter_step(zu, zd, 1)
        s10x, s10y = x(sx), y(sy)
        keep_j = joined_half(first_rows, grad_projected, grad_rows, attended, 0)
        five = jnp.concatenate(
            [
                jnp.concatenate([sums_1[:4], sums_2[:4]], axis=1),
                jnp.sum(local_grads.astype(F32), axis=0, keepdims=True),
            ],
            axis=0,
        )
        sx, sy = at(keep_j, came_j, 3, 5).astype(BF16), at(keep_j, came_j, 5, 7).astype(BF16)
        eu, ed, s10x, s10y, keep_j, five, bu, bd, sx, sy = cut(
            eu, ed, s10x, s10y, keep_j, five, bu, bd, sx, sy
        )
        zu, zd, sx, sy, s10x, s10y, five = cut(
            *scatter_terms(backs, eu, ed, 2), sx, sy, s10x, s10y, five
        )
        eu, ed = scatter_step(zu, zd, 2)
        j1x, j1y = x(sx), y(sy)
        five = five.reshape(1, -1)
        five = five + xor_shift(five, "tensor", 1)
        down_sum = pair(
            plus(at(keep_d, came_d, 0, 1), d1x[first], s9y[first]),
            plus(at(keep_d, came_d, 1, 2), d1y[second], s9x[first]),
        ).T
        up_sum = pair(
            plus(at(keep_u, came_u, 0, 1), s10x[second], s10y[second]),
            plus(at(keep_u, came_u, 1, 2), s10x[first], s10y[first]),
        )
        five = from_frame(five.reshape(5, width)).reshape(1, -1)
        terms = jnp.concatenate(
            [
                five,
                jnp.sum(grad_projected, axis=0, dtype=F32, keepdims=True),
                jnp.sum(grad_hidden, axis=0, dtype=F32, keepdims=True),
            ],
            axis=1,
        )
        eu, ed, j1x, j1y, terms, down_sum, up_sum, bu, bd = cut(
            eu, ed, j1x, j1y, terms, down_sum, up_sum, bu, bd
        )
        zu, zd, sx, sy, terms = cut(
            *scatter_terms(backs, eu, ed, 3),
            plus(at(keep_j, came_j, 2, 3), j1y[first]).astype(BF16),
            plus(at(keep_j, came_j, 7, 8), j1x[second]).astype(BF16),
            terms,
        )
        eu, ed = scatter_step(zu, zd, 3)
        j2x, j2y = x(sx), y(sy)
        terms, j2x, j2y, bu, bd = cut(terms, j2x, j2y, bu, bd)
        own = jnp.concatenate([h[:local_rows] for h in branches], axis=1)
        output = finish_output(plus(own, bu, bd), shift_rows)
        terms = butterfly(terms, "dp")
        five = terms[:, : 5 * width]
        five = five + xor_shift(five, "tensor", 2)
        small = small_shares(
            five, terms[0, 5 * width : 5 * width + joined_width], terms[:, 5 * width + joined_width :]
        )
        joined_mix = pair(
            plus(at(keep_j, came_j, 0, 1), j1x[first], j2y),
            plus(at(keep_j, came_j, 1, 2), j1y[second], j2x),
        )
        joined_sum, mix_sum = joined_mix[:, :joined_width], joined_mix[:, joined_width:].T
        input_grad = input_grad_rows(*backs, eu, ed, local_tokens, local_grads)
        return output, input_grad, joined_sum, mix_sum, up_sum, down_sum, small

    parts = staged() if fast_dp() and n_tensor == 4 else plain()
    output, input_grad, joined_sum, mix_sum, up_sum, down_sum, small = parts
    gains_grad, biases_grad, joined_bias_sum, up_bias_sum = small
    return (
        output,
        input_grad,
        joined_sum.reshape(proj_weight.shape),
        joined_bias_sum,
        mix_sum,
        up_sum,
        up_bias_sum,
        down_sum,
        gains_grad,
        biases_grad,
    )


def solution(mesh):
    in_specs = (
        P(("dp", "tensor"), None),
        P("dp"),
        P("dp", None, "tensor"),
        P(None, "tensor", "dp"),
        P("tensor", "dp"),
        P("dp", "tensor"),
        P("tensor", "dp"),
        P("tensor", "dp"),
        P(None, ("dp", "tensor")),
        P(None, ("dp", "tensor")),
        P(("dp", "tensor"), None),
    )
    out_specs = (
        P(("dp", "tensor"), None),
        P(("dp", "tensor"), None),
        P("dp", None, "tensor"),
        P(None, "tensor", "dp"),
        P("tensor", "dp"),
        P("dp", "tensor"),
        P("tensor", "dp"),
        P("tensor", "dp"),
        P(None, ("dp", "tensor")),
        P(None, ("dp", "tensor")),
    )
    return jax.shard_map(shards, mesh=mesh, in_specs=in_specs, out_specs=out_specs, check_vma=False)
```

```python
import functools

import jax
import jax.numpy as jnp
from jax import lax
from jax.experimental import pallas as pl
from jax.experimental.pallas import tpu as pltpu
from jax.sharding import PartitionSpec as P

ROT = 64
EPSILON = 1e-05
ROTARY_BASE = 10000.0
F32 = jnp.float32
BF16 = jnp.bfloat16
HALVES = [(0, 0), (0, 1), (2, 1), (2, 0), (6, 0), (6, 1), (4, 1), (4, 0)]
ORDER = HALVES + [(p ^ 1, h) for p, h in HALVES]


SMALL = pl.CostEstimate(flops=1000, bytes_accessed=1000, transcendentals=0)


def cut(*values):
    return lax.optimization_barrier(values)


def is_power(n):
    return n & (n - 1) == 0


def fast_dp():
    return lax.axis_size("dp") == 8


def xor_shift(values, axis, bit):
    size = lax.axis_size(axis)
    return lax.ppermute(values, axis, [(i, i ^ bit) for i in range(size)])


def butterfly(values, axis):
    size = lax.axis_size(axis)
    if not is_power(size):
        return lax.psum(values, axis)
    bit = 1
    while bit < size:
        values = values + xor_shift(values, axis, bit)
        bit *= 2
    return values


def columns_kernel(index_ref, x_ref, o_ref, *, count, step):
    for j in range(count):
        at = pl.multiple_of(index_ref[j] * step, step)
        o_ref[:, j * step : (j + 1) * step] = x_ref[:, pl.ds(at, step)]


def take_columns(values, index):
    rows, width = values.shape
    count = index.shape[0]
    tile = rows // 2 if rows % 64 == 0 else rows
    return pl.pallas_call(
        functools.partial(columns_kernel, count=count, step=width // count),
        out_shape=jax.ShapeDtypeStruct(values.shape, values.dtype),
        grid_spec=pltpu.PrefetchScalarGridSpec(
            num_scalar_prefetch=1,
            grid=(rows // tile,),
            in_specs=[pl.BlockSpec((tile, width), lambda i, s: (i, 0))],
            out_specs=pl.BlockSpec((tile, width), lambda i, s: (i, 0)),
        ),
        cost_estimate=SMALL,
        name="columns",
    )(index, values)


FRAME = [[(me ^ p) * 2 + h for p, h in ORDER] for me in range(8)]
PLAIN = [[row.index(k) for k in range(16)] for row in FRAME]


def frame_index():
    return lax.dynamic_index_in_dim(jnp.array(FRAME, jnp.int32), lax.axis_index("dp"), 0, keepdims=False)


def plain_index():
    return lax.dynamic_index_in_dim(jnp.array(PLAIN, jnp.int32), lax.axis_index("dp"), 0, keepdims=False)


def to_frame(values):
    return take_columns(values, frame_index()) if fast_dp() else values


def from_frame(values):
    return take_columns(values, plain_index()) if fast_dp() else values


def dp_gather(shard):
    if not fast_dp():
        return [lax.all_gather(shard, "dp", axis=0, tiled=True)]
    half = shard.shape[0] // 2
    from_x = xor_shift(shard, "dp", 2)
    from_y = xor_shift(shard, "dp", 4)
    far_1 = xor_shift(from_y[:half], "dp", 2)
    far_2 = xor_shift(from_x[half:], "dp", 4)
    far = jnp.concatenate([far_1, far_2], axis=0)
    near = xor_shift(shard, "dp", 1)
    near_x = xor_shift(from_x, "dp", 1)
    near_y = xor_shift(from_y, "dp", 1)
    near_far = xor_shift(far, "dp", 1)
    out = []
    for own, x, f, y in ((shard, from_x, far, from_y), (near, near_x, near_far, near_y)):
        out += [own, x[half:], x[:half], f, y[half:], y[:half]]
    return out


def join(pieces, start, stop):
    return jnp.concatenate([p[:, start:stop] for p in pieces], axis=0)


def dp_scatter(make):
    away = make(1)
    came = xor_shift(away, "dp", 1)
    kept = make(0)
    rows = kept.shape[0] // 4
    half = rows // 2

    def summed(start, stop):
        return kept[start:stop].astype(F32) + came[start:stop].astype(F32)

    first_x = xor_shift(summed(rows + half, 2 * rows + half).astype(BF16), "dp", 2)
    first_y = xor_shift(summed(2 * rows + half, 3 * rows + half).astype(BF16), "dp", 4)
    last_x = summed(rows, rows + half) + first_y[:half].astype(F32)
    last_y = summed(3 * rows + half, 4 * rows) + first_x[half:].astype(F32)
    last_x = xor_shift(last_x.astype(BF16), "dp", 2)
    last_y = xor_shift(last_y.astype(BF16), "dp", 4)
    top = summed(0, half) + first_x[:half].astype(F32) + last_y.astype(F32)
    low = summed(half, rows) + first_y[half:].astype(F32) + last_x.astype(F32)
    return jnp.concatenate([top, low], axis=0)


def weight_grad(rows, columns):
    def make(part):
        width = rows.shape[1] // 2
        chosen = rows[:, part * width : (part + 1) * width]
        return jnp.einsum("nd,nf->df", chosen, columns, preferred_element_type=F32).astype(BF16)

    if fast_dp():
        return dp_scatter(make)
    whole = jnp.einsum("nd,nf->df", rows, columns, preferred_element_type=F32).astype(BF16)
    return lax.psum_scatter(whole, "dp", scatter_dimension=0, tiled=True).astype(F32)


def line_gather(block):
    size = lax.axis_size("tensor")
    me = lax.axis_index("tensor")
    up = down = block
    ups, downs = [block], [block]
    for s in range(size - 1):
        up = lax.ppermute(up, "tensor", [(i, i + 1) for i in range(s, size - 1)])
        down = lax.ppermute(down, "tensor", [(i + 1, i) for i in range(size - 1 - s)])
        ups.append(up)
        downs.append(down)
    blocks = [block]
    for r in range(1, size):
        blocks.append(jnp.where(me + r < size, downs[r], ups[size - r]))
    return jnp.concatenate(blocks, axis=0)


def line_scatter(terms):
    size = lax.axis_size("tensor")
    rows = terms.shape[0] // size

    def block(r):
        return terms[r * rows : (r + 1) * rows]

    up = down = None
    for s in range(1, size):
        to_up, to_down = block(size - s), block(s)
        if s > 1:
            to_up = (to_up.astype(F32) + up.astype(F32)).astype(BF16)
            to_down = (to_down.astype(F32) + down.astype(F32)).astype(BF16)
        up = lax.ppermute(to_up, "tensor", [(i, i + 1) for i in range(s)])
        down = lax.ppermute(to_down, "tensor", [(i, i - 1) for i in range(size - s, size)])
    return block(0).astype(F32) + up.astype(F32) + down.astype(F32)


def turn(values, cosine, low_sine, high_sine, sign):
    half = ROT // 2
    lanes = cosine.shape[-1]
    head = values[:, :lanes]
    turned = (
        head * cosine
        - sign * pltpu.roll(head, lanes - half, 1) * low_sine
        + sign * pltpu.roll(head, half, 1) * high_sine
    )
    return jnp.concatenate([turned, values[:, lanes:]], axis=1)


def contract(a, b, dims):
    return lax.dot_general(a, b, (dims, ((), ())), preferred_element_type=F32)


def masked(scores, column_starts, row_starts, query_block, block):
    keys = scores.shape[1]
    query = lax.broadcasted_iota(jnp.int32, scores.shape, 0) + query_block * block
    key = lax.broadcasted_iota(jnp.int32, scores.shape, 1)
    allowed = (column_starts == row_starts[:, :keys]) & (key <= query)
    return allowed, jnp.where(allowed, scores, -1e30)


def spots(me_ref, size, block):
    def spot(b):
        return pl.ds(pl.multiple_of(lax.rem(b - me_ref[0] + size, size) * block, block), block)

    return spot


def forward_block(q_out, k_out, v_out, att_ref, log_ref, col_ref, row_ref, spot, b, block):
    scale = q_out.shape[-1] ** (-0.5)
    here = slice(b * block, (b + 1) * block)
    query = q_out[spot(b), :]
    scores = jnp.concatenate(
        [contract(query, k_out[spot(c), :], ((1,), (1,))) for c in range(b + 1)], axis=1
    ) * scale
    _, scores = masked(scores, col_ref[here, :1], row_ref[:1, :], b, block)
    top = jnp.max(scores, axis=1, keepdims=True)
    powers = jnp.exp(scores - top)
    total = jnp.sum(powers, axis=1, keepdims=True)
    weights = (powers / total).astype(BF16)
    attended = contract(weights[:, :block], v_out[spot(0), :], ((1,), (0,)))
    for c in range(1, b + 1):
        attended = attended + contract(
            weights[:, c * block : (c + 1) * block], v_out[spot(c), :], ((1,), (0,))
        )
    att_ref[spot(b), :] = attended.astype(BF16)
    log_ref[0, here, :] = jnp.broadcast_to(top + jnp.log(total), (block, log_ref.shape[2]))


def forward_kernel(
    me_ref, q_ref, k_ref, v_ref, cos_ref, low_ref, high_ref, col_ref, row_ref,
    q_out, k_out, v_out, att_ref, log_ref, *, size, block,
):
    spot = spots(me_ref, size, block)
    for b in range(size):
        here = slice(b * block, (b + 1) * block)
        at = spot(b)
        tables = cos_ref[here, :], low_ref[here, :], high_ref[here, :]
        q_out[at, :] = turn(q_ref[at, :], *tables, 1.0).astype(BF16)
        k_out[at, :] = turn(k_ref[at, :], *tables, 1.0).astype(BF16)
        v_out[at, :] = v_ref[at, :].astype(BF16)
    for b in range(size):
        forward_block(q_out, k_out, v_out, att_ref, log_ref, col_ref, row_ref, spot, b, block)


def joined_forward_kernel(
    me_ref, rows_ref, qa_ref, ka_ref, va_ref, qb_ref, kb_ref, vb_ref, q_bias, k_bias, v_bias,
    cos_ref, low_ref, high_ref, col_ref, row_ref,
    q_out, k_out, v_out, att_ref, log_ref, *, size, block,
):
    spot = spots(me_ref, size, block)
    middle = qa_ref.shape[0]
    for b in range(size):
        here = slice(b * block, (b + 1) * block)
        at = spot(b)
        tables = cos_ref[here, :], low_ref[here, :], high_ref[here, :]
        top, low = rows_ref[at, :middle], rows_ref[at, middle:]

        def project(one, two, bias):
            return contract(top, one[:, :], ((1,), (0,))) + contract(low, two[:, :], ((1,), (0,))) + bias[:, :]

        q_out[at, :] = turn(project(qa_ref, qb_ref, q_bias), *tables, 1.0).astype(BF16)
        k_out[at, :] = turn(project(ka_ref, kb_ref, k_bias), *tables, 1.0).astype(BF16)
        v_out[at, :] = project(va_ref, vb_ref, v_bias).astype(BF16)
        forward_block(q_out, k_out, v_out, att_ref, log_ref, col_ref, row_ref, spot, b, block)


def backward_pass(
    q_ref, k_ref, v_ref, g_ref, log_ref, cos_ref, low_ref, high_ref, col_ref, row_ref,
    put, k_acc, v_acc, spot, size, block,
):
    scale = q_ref.shape[-1] ** (-0.5)
    for b in range(size):
        here = slice(b * block, (b + 1) * block)
        query, grad = q_ref[spot(b), :], g_ref[spot(b), :]
        scores = jnp.concatenate(
            [contract(query, k_ref[spot(c), :], ((1,), (1,))) for c in range(b + 1)], axis=1
        ) * scale
        allowed, scores = masked(scores, col_ref[here, :1], row_ref[:1, :], b, block)
        probs = jnp.where(allowed, jnp.exp(scores - log_ref[0, here, :1]), 0.0)
        grad_probs = jnp.concatenate(
            [contract(grad, v_ref[spot(c), :], ((1,), (1,))) for c in range(b + 1)], axis=1
        )
        inner = jnp.sum(probs * grad_probs, axis=1, keepdims=True)
        weights = probs.astype(BF16)
        grad_scores = (probs * (grad_probs - inner)).astype(BF16)
        back = None
        for c in range(b + 1):
            part = slice(c * block, (c + 1) * block)
            key_term = contract(grad_scores[:, part], query, ((0,), (0,)))
            value_term = contract(weights[:, part], grad, ((0,), (0,)))
            query_term = contract(grad_scores[:, part], k_ref[spot(c), :], ((1,), (0,)))
            back = query_term if c == 0 else back + query_term
            if c == b:
                k_acc[part, :] = key_term
                v_acc[part, :] = value_term
            else:
                k_acc[part, :] += key_term
                v_acc[part, :] += value_term
        tables = cos_ref[here, :], low_ref[here, :], high_ref[here, :]
        put(0, spot(b), turn(back * scale, *tables, -1.0).astype(BF16))
    for b in range(size):
        here = slice(b * block, (b + 1) * block)
        tables = cos_ref[here, :], low_ref[here, :], high_ref[here, :]
        put(1, spot(b), turn(k_acc[here, :] * scale, *tables, -1.0).astype(BF16))
        put(2, spot(b), v_acc[here, :].astype(BF16))


def backward_kernel(
    me_ref, q_ref, k_ref, v_ref, g_ref, log_ref, cos_ref, low_ref, high_ref, col_ref, row_ref,
    dq_ref, dk_ref, dv_ref, k_acc, v_acc, *, size, block,
):
    outs = (dq_ref, dk_ref, dv_ref)

    def put(k, at, value):
        outs[k][at, :] = value

    backward_pass(
        q_ref, k_ref, v_ref, g_ref, log_ref, cos_ref, low_ref, high_ref, col_ref, row_ref,
        put, k_acc, v_acc, spots(me_ref, size, block), size, block,
    )


def mixed_backward_kernel(
    me_ref, q_ref, k_ref, v_ref, g_ref, a_ref, b_ref, log_ref, cos_ref, low_ref, high_ref, col_ref, row_ref,
    d_ref, k_acc, v_acc, g_acc, *, size, block, heads,
):
    middle = a_ref.shape[0]
    head = q_ref.shape[1]
    for b in range(size):
        here = slice(b * block, (b + 1) * block)
        g_acc[here, :] = (
            contract(g_ref[here, :middle], a_ref[:, :], ((1,), (0,)))
            + contract(g_ref[here, middle:], b_ref[:, :], ((1,), (0,)))
        ).astype(BF16)
    h = pl.program_id(0)

    def put(k, at, value):
        d_ref[at, pl.ds(pl.multiple_of((k * heads + h) * head, head), head)] = value

    backward_pass(
        q_ref, k_ref, v_ref, g_acc, log_ref, cos_ref, low_ref, high_ref, col_ref, row_ref,
        put, k_acc, v_acc, spots(me_ref, size, block), size, block,
    )


def hidden_kernel(rows_ref, a_ref, b_ref, bias_ref, act_ref, slope_ref, *, step):
    middle = a_ref.shape[0]
    for i in range(rows_ref.shape[0] // step):
        here = slice(i * step, (i + 1) * step)
        hidden = contract(rows_ref[here, :middle], a_ref[:, :], ((1,), (0,)))
        hidden = hidden + contract(rows_ref[here, middle:], b_ref[:, :], ((1,), (0,))) + bias_ref[:, :]
        bell = lax.erf(hidden * (0.5**0.5))
        act_ref[here, :] = (0.5 * hidden * (1.0 + bell)).astype(BF16)
        slope = 0.5 * (1.0 + bell) + hidden * jnp.exp(-0.5 * hidden * hidden) * 0.3989422804014327
        slope_ref[here, :] = slope.astype(BF16)


def hidden_half(rows, top, low, bias):
    count, width = rows.shape
    out = top.shape[1]
    tile = 512
    half = pl.BlockSpec((width // 2, tile), lambda j: (0, j))
    made = pl.BlockSpec((count, tile), lambda j: (0, j))
    return pl.pallas_call(
        functools.partial(hidden_kernel, step=256),
        out_shape=(jax.ShapeDtypeStruct((count, out), BF16),) * 2,
        grid=(out // tile,),
        in_specs=[
            pl.BlockSpec((count, width), lambda j: (0, 0)), half, half, pl.BlockSpec((1, tile), lambda j: (0, j))
        ],
        out_specs=(made, made),
        cost_estimate=SMALL,
        name="hidden",
    )(rows, top, low, bias.reshape(1, -1))


def slope_kernel(rows_ref, a_ref, b_ref, slope_ref, out_ref, sum_ref, *, step):
    middle = a_ref.shape[0]
    total = 0.0
    for i in range(rows_ref.shape[0] // step):
        here = slice(i * step, (i + 1) * step)
        active = contract(rows_ref[here, :middle], a_ref[:, :], ((1,), (0,)))
        active = active + contract(rows_ref[here, middle:], b_ref[:, :], ((1,), (0,)))
        made = (active * slope_ref[here, :].astype(F32)).astype(BF16)
        out_ref[here, :] = made
        total = total + jnp.sum(made.astype(F32), axis=0, keepdims=True)
    sum_ref[:, :] = total


def hidden_back(rows, top, low, slope):
    count, width = rows.shape
    out = top.shape[1]
    tile = 512
    half = pl.BlockSpec((top.shape[0], tile), lambda j: (0, j))
    made = pl.BlockSpec((count, tile), lambda j: (0, j))
    return pl.pallas_call(
        functools.partial(slope_kernel, step=256),
        out_shape=(jax.ShapeDtypeStruct((count, out), BF16), jax.ShapeDtypeStruct((1, out), F32)),
        grid=(out // tile,),
        in_specs=[pl.BlockSpec((count, width), lambda j: (0, 0)), half, half, made],
        out_specs=(made, pl.BlockSpec((1, tile), lambda j: (0, j))),
        cost_estimate=SMALL,
        name="hidden_back",
    )(rows, top, low, slope)


def branch_kernel(att_ref, mix_ref, act_ref, down_ref, out_ref, *, step):
    for i in range(att_ref.shape[0] // step):
        here = slice(i * step, (i + 1) * step)
        total = contract(att_ref[here, :], mix_ref[:, :], ((1,), (1,)))
        total = total + contract(act_ref[here, :], down_ref[:, :], ((1,), (1,)))
        out_ref[here, :] = total.astype(BF16)


def branch_half(attended, mixed, activated, down):
    count, inner = attended.shape
    units = activated.shape[1]
    width = down.shape[0]
    tile = 256
    spot = mixed.shape[1] // inner - 1
    return pl.pallas_call(
        functools.partial(branch_kernel, step=256),
        out_shape=jax.ShapeDtypeStruct((count, width), BF16),
        grid=(width // tile,),
        in_specs=[
            pl.BlockSpec((count, inner), lambda j: (0, 0)),
            pl.BlockSpec((tile, inner), lambda j: (j + width // tile, spot)),
            pl.BlockSpec((count, units), lambda j: (0, 0)),
            pl.BlockSpec((tile, units), lambda j: (j, 0)),
        ],
        out_specs=pl.BlockSpec((count, tile), lambda j: (0, j)),
        cost_estimate=SMALL,
        name="branches",
    )(attended, mixed, activated, down)


def back_kernel(
    hid_ref, proj_ref, up_ref, join_ref, tok_ref, mean_ref, scale_ref, gain_ref, back_ref, sum_ref, *, step
):
    sums = [0.0] * 4
    for i in range(hid_ref.shape[0] // step):
        here = slice(i * step, (i + 1) * step)
        two = contract(hid_ref[here, :], up_ref[:, :], ((1,), (1,)))
        one = contract(proj_ref[here, :], join_ref[:, :], ((1,), (1,)))
        back_ref[here, :] = (one * gain_ref[:1, :] + two * gain_ref[1:2, :]).astype(BF16)
        xhat = (tok_ref[here, :].astype(F32) - mean_ref[here, :1]) * scale_ref[here, :1]
        for k, term in enumerate((one * xhat, two * xhat, one, two)):
            sums[k] = sums[k] + jnp.sum(term, axis=0, keepdims=True)
    for k in range(4):
        sum_ref[k : k + 1, :] = sums[k]


def back_half(grad_hidden, grad_projected, both, token_rows, mean, scale, gains, part):
    count, units = grad_hidden.shape
    joined = grad_projected.shape[1]
    width = both.shape[0] // 2
    tile = 256
    tiles = width // tile
    whole = lambda j: (0, 0)
    return pl.pallas_call(
        functools.partial(back_kernel, step=256),
        out_shape=(jax.ShapeDtypeStruct((count, width), BF16), jax.ShapeDtypeStruct((8, width), F32)),
        grid=(tiles,),
        in_specs=[
            pl.BlockSpec((count, units), whole),
            pl.BlockSpec((count, joined), whole),
            pl.BlockSpec((tile, units), lambda j: (j, 0)),
            pl.BlockSpec((tile, joined), lambda j: (j + tiles, 0)),
            pl.BlockSpec((count, tile), lambda j: (0, j + part * tiles)),
            pl.BlockSpec((count, 128), whole),
            pl.BlockSpec((count, 128), whole),
            pl.BlockSpec((2, tile), lambda j: (0, j + part * tiles)),
        ],
        out_specs=(pl.BlockSpec((count, tile), lambda j: (0, j)), pl.BlockSpec((8, tile), lambda j: (0, j))),
        cost_estimate=SMALL,
        name="back",
    )(grad_hidden, grad_projected, both, both, token_rows, mean, scale, gains)


def lay_kernel(*refs):
    *ins, out_ref = refs
    rows = ins[0].shape[0]
    half = rows // 2
    for w in range(len(ins) // 3):
        own, from_x, from_y = ins[3 * w : 3 * w + 3]
        base = 4 * w * rows
        out_ref[base : base + rows, :] = own[:, :]
        out_ref[base + 2 * rows : base + 3 * rows, :] = jnp.zeros(own.shape, BF16)
        for piece, at in ((from_x, base + rows), (from_y, base + 3 * rows)):
            out_ref[at : at + half, :] = piece[half:, :]
            out_ref[at + half : at + rows, :] = piece[:half, :]


def lay(*pieces):
    rows, width = pieces[0].shape
    weights = len(pieces) // 3
    tile = width // 4
    return pl.pallas_call(
        lay_kernel,
        out_shape=jax.ShapeDtypeStruct((4 * rows * weights, width), BF16),
        grid=(4,),
        in_specs=[pl.BlockSpec((rows, tile), lambda j: (0, j))] * len(pieces),
        out_specs=pl.BlockSpec((4 * rows * weights, tile), lambda j: (0, j)),
        cost_estimate=SMALL,
        name="lay",
    )(*pieces)


def pair_sums_kernel(kept_x, came_x, kept_y, came_y, to_x, to_y):
    to_x[:, :] = (kept_x[:, :].astype(F32) + came_x[:, :].astype(F32)).astype(BF16)
    to_y[:, :] = (kept_y[:, :].astype(F32) + came_y[:, :].astype(F32)).astype(BF16)


def pair_sums(kept, came, half):
    width = kept.shape[1]
    of_x = pl.BlockSpec((half, width), lambda i: (3 + i, 0))
    of_y = pl.BlockSpec((half, width), lambda i: (5 + i, 0))
    out = pl.BlockSpec((half, width), lambda i: (i, 0))
    return pl.pallas_call(
        pair_sums_kernel,
        out_shape=(jax.ShapeDtypeStruct((2 * half, width), BF16),) * 2,
        grid=(2,),
        in_specs=[of_x, of_x, of_y, of_y],
        out_specs=(out, out),
        cost_estimate=SMALL,
        name="pair_sums",
    )(kept, came, kept, came)


def own_sums_kernel(kept, came, a, b, c, d, out):
    half = a.shape[0]
    top, low = slice(0, half), slice(half, 2 * half)
    for part, one, two in ((top, a, b), (low, c, d)):
        total = kept[part, :].astype(F32) + came[part, :].astype(F32)
        out[part, :] = total + one[:, :].astype(F32) + two[:, :].astype(F32)


def own_sums(kept, came, half, *came_in):
    width = kept.shape[1]
    tile = width // 4
    rows = pl.BlockSpec((2 * half, tile), lambda j: (0, j))
    return pl.pallas_call(
        own_sums_kernel,
        out_shape=jax.ShapeDtypeStruct((2 * half, width), F32),
        grid=(4,),
        in_specs=[rows, rows] + [pl.BlockSpec((half, tile), lambda j, k=k: (k, j)) for _, k in came_in],
        out_specs=rows,
        cost_estimate=SMALL,
        name="own_sums",
    )(kept, came, *(v for v, _ in came_in))


def terms_kernel(*refs):
    *ins, to_up, to_down = refs
    up = jnp.concatenate([ins[0][:, :], ins[1][:, :]], axis=1)
    down = jnp.concatenate([ins[2][:, :], ins[3][:, :]], axis=1)
    if len(ins) > 4:
        up = (up.astype(F32) + ins[4][:, :].astype(F32)).astype(BF16)
        down = (down.astype(F32) + ins[5][:, :].astype(F32)).astype(BF16)
    to_up[:, :] = up
    to_down[:, :] = down


def step_terms(halves, up_block, down_block, rows, *came):
    width = halves[0].shape[1]
    tiles = 2
    tile = rows // tiles

    def of(block):
        return [pl.BlockSpec((tile, width), lambda i: (block * tiles + i, 0))] * 2

    full = pl.BlockSpec((tile, 2 * width), lambda i: (i, 0))
    return pl.pallas_call(
        terms_kernel,
        out_shape=(jax.ShapeDtypeStruct((rows, 2 * width), BF16),) * 2,
        grid=(tiles,),
        in_specs=of(up_block) + of(down_block) + [full] * len(came),
        out_specs=(full, full),
        cost_estimate=SMALL,
        name="terms",
    )(*halves, *halves, *came)


def input_grad_kernel(index_ref, one_ref, two_ref, up_ref, down_ref, tok_ref, grad_ref, out_ref):
    back = jnp.concatenate([one_ref[:, :], two_ref[:, :]], axis=1).astype(F32)
    back = back + up_ref[:, :].astype(F32) + down_ref[:, :].astype(F32)
    xhat, scale = standardize(tok_ref[:, :])
    back = back - jnp.mean(back, axis=-1, keepdims=True) - xhat * jnp.mean(back * xhat, axis=-1, keepdims=True)
    total = grad_ref[:, :].astype(F32) + back * scale
    count = index_ref.shape[0]
    step = total.shape[1] // count
    for j in range(count):
        out_ref[:, pl.ds(pl.multiple_of(index_ref[j] * step, step), step)] = total[:, j * step : (j + 1) * step]


def input_grad_rows(one, two, up, down, tokens, grads):
    rows, width = tokens.shape
    tile = rows // 4
    half = pl.BlockSpec((tile, width // 2), lambda i, s: (i, 0))
    full = pl.BlockSpec((tile, width), lambda i, s: (i, 0))
    return pl.pallas_call(
        input_grad_kernel,
        out_shape=jax.ShapeDtypeStruct((rows, width), F32),
        grid_spec=pltpu.PrefetchScalarGridSpec(
            num_scalar_prefetch=1,
            grid=(rows // tile,),
            in_specs=[half, half, full, full, full, full],
            out_specs=full,
        ),
        cost_estimate=SMALL,
        name="input_grad",
    )(frame_index(), one, two, up, down, tokens, grads)


def joined_forward(rows, top, low, bias, tables, me, heads, head, size):
    count, width = rows.shape
    block = count // size
    whole = lambda h, s: (0, 0)
    table_specs = [pl.BlockSpec((count, 128), whole)] * 4 + [pl.BlockSpec((8, count), whole)]
    by_head = pl.BlockSpec((count, head), lambda h, s: (0, h))
    wide = jax.ShapeDtypeStruct((count, heads * head), BF16)

    def thirds(n, spot):
        return [pl.BlockSpec((n, head), lambda h, s, k=k: (spot, k * heads + h)) for k in range(3)]

    return pl.pallas_call(
        functools.partial(joined_forward_kernel, size=size, block=block),
        out_shape=(wide, wide, wide, wide, jax.ShapeDtypeStruct((heads, count, 128), F32)),
        grid_spec=pltpu.PrefetchScalarGridSpec(
            num_scalar_prefetch=1,
            grid=(heads,),
            in_specs=[pl.BlockSpec((count, width), whole)]
            + thirds(width // 2, 1) + thirds(width // 2, 1) + thirds(1, 0) + table_specs,
            out_specs=(by_head,) * 4 + (pl.BlockSpec((1, count, 128), lambda h, s: (h, 0, 0)),),
        ),
        cost_estimate=SMALL,
        name="joined_forward",
    )(me, rows, top, top, top, low, low, low, bias, bias, bias, *tables)


def mixed_backward(queries, keys, values, grads, top, low, log_total, tables, me, heads, size):
    count = queries.shape[0]
    head = queries.shape[1] // heads
    block = count // size
    whole = lambda h, s: (0, 0)
    table_specs = [pl.BlockSpec((count, 128), whole)] * 4 + [pl.BlockSpec((8, count), whole)]
    by_head = pl.BlockSpec((count, head), lambda h, s: (0, h))
    mix = pl.BlockSpec((grads.shape[1] // 2, head), lambda h, s: (1, 3 * heads + h))
    return pl.pallas_call(
        functools.partial(mixed_backward_kernel, size=size, block=block, heads=heads),
        out_shape=jax.ShapeDtypeStruct((count, 3 * heads * head), BF16),
        grid_spec=pltpu.PrefetchScalarGridSpec(
            num_scalar_prefetch=1,
            grid=(heads,),
            in_specs=[by_head] * 3
            + [pl.BlockSpec((count, grads.shape[1]), whole), mix, mix]
            + [pl.BlockSpec((1, count, 128), lambda h, s: (h, 0, 0))]
            + table_specs,
            out_specs=pl.BlockSpec((count, 3 * heads * head), whole),
            scratch_shapes=[pltpu.VMEM((count, head), F32)] * 2 + [pltpu.VMEM((count, head), BF16)],
        ),
        cost_estimate=SMALL,
        name="mixed_backward",
    )(me, queries, keys, values, grads, top, low, log_total, *tables)


def attention_tables(positions, starts):
    half = ROT // 2
    frequency = ROTARY_BASE ** (-(jnp.arange(half, dtype=F32) * 2.0) / ROT)
    angles = positions.astype(F32)[:, None] * frequency[None, :]
    cosine, sine = jnp.cos(angles), jnp.sin(angles)
    rows = positions.shape[0]
    cosines = jnp.concatenate([cosine, cosine, jnp.ones((rows, 128 - ROT), F32)], axis=1)
    low = jnp.concatenate([sine, jnp.zeros((rows, 128 - half), F32)], axis=1)
    high = jnp.concatenate([jnp.zeros((rows, half), F32), sine, jnp.zeros((rows, 128 - ROT), F32)], axis=1)
    columns = jnp.broadcast_to(starts[:, None], (rows, 128))
    across = jnp.broadcast_to(starts[None, :], (8, rows))
    return cosines, low, high, columns, across


def attention_forward(projected, tables, me, heads, size):
    rows = projected.shape[0]
    head = projected.shape[1] // (3 * heads)
    block = rows // size
    whole = lambda h, s: (0, 0)
    table_specs = [pl.BlockSpec((rows, 128), whole)] * 4 + [pl.BlockSpec((8, rows), whole)]
    by_head = pl.BlockSpec((rows, head), lambda h, s: (0, h))
    wide = jax.ShapeDtypeStruct((rows, heads * head), BF16)
    return pl.pallas_call(
        functools.partial(forward_kernel, size=size, block=block),
        out_shape=(wide, wide, wide, wide, jax.ShapeDtypeStruct((heads, rows, 128), F32)),
        grid_spec=pltpu.PrefetchScalarGridSpec(
            num_scalar_prefetch=1,
            grid=(heads,),
            in_specs=[
                pl.BlockSpec((rows, head), lambda h, s, k=k: (0, k * heads + h)) for k in range(3)
            ]
            + table_specs,
            out_specs=(by_head,) * 4 + (pl.BlockSpec((1, rows, 128), lambda h, s: (h, 0, 0)),),
        ),
        cost_estimate=pl.CostEstimate(
            flops=heads * rows * rows * head * 40, bytes_accessed=rows * head * heads * 24,
            transcendentals=heads * rows * rows // 2,
        ),
        name="attention_forward",
    )(me, projected, projected, projected, *tables)


def attention_backward(queries, keys, values, grads, log_total, tables, me, heads, size):
    rows = queries.shape[0]
    head = queries.shape[1] // heads
    block = rows // size
    whole = lambda h, s: (0, 0)
    table_specs = [pl.BlockSpec((rows, 128), whole)] * 4 + [pl.BlockSpec((8, rows), whole)]
    by_head = pl.BlockSpec((rows, head), lambda h, s: (0, h))
    wide = jax.ShapeDtypeStruct((rows, heads * head), BF16)
    return pl.pallas_call(
        functools.partial(backward_kernel, size=size, block=block),
        out_shape=(wide, wide, wide),
        grid_spec=pltpu.PrefetchScalarGridSpec(
            num_scalar_prefetch=1,
            grid=(heads,),
            in_specs=[by_head] * 4
            + [pl.BlockSpec((1, rows, 128), lambda h, s: (h, 0, 0))]
            + table_specs,
            out_specs=(by_head,) * 3,
            scratch_shapes=[pltpu.VMEM((rows, head), F32)] * 2,
        ),
        cost_estimate=pl.CostEstimate(
            flops=heads * rows * rows * head * 60, bytes_accessed=rows * head * heads * 24,
            transcendentals=heads * rows * rows // 2,
        ),
        name="attention_backward",
    )(me, queries, keys, values, grads, log_total, *tables)


def standardize(values):
    values = values.astype(F32)
    centered = values - jnp.mean(values, axis=-1, keepdims=True)
    spread = jnp.mean(centered * centered, axis=-1, keepdims=True)
    scale = lax.rsqrt(spread + EPSILON)
    return centered * scale, scale


def norm_rows(token_rows, gain_rows, shift_rows):
    xhat, _ = standardize(token_rows)
    first_rows = (xhat * gain_rows[0] + shift_rows[0]).astype(BF16)
    second_rows = (xhat * gain_rows[1] + shift_rows[1]).astype(BF16)
    return first_rows, second_rows


def hidden_units(second_rows, up_rows, hidden_bias):
    hidden = jnp.dot(second_rows, up_rows, preferred_element_type=F32) + hidden_bias
    bell = lax.erf(hidden * (0.5**0.5))
    activated = (0.5 * hidden * (1.0 + bell)).astype(BF16)
    slope = 0.5 * (1.0 + bell) + hidden * jnp.exp(-0.5 * hidden * hidden) * 0.3989422804014327
    return activated, slope.astype(BF16)


def branch_rows(attended, mix_rows, activated, down_rows):
    return (
        jnp.einsum("ne,de->nd", attended, mix_rows, preferred_element_type=F32)
        + jnp.einsum("nf,df->nd", activated, down_rows, preferred_element_type=F32)
    ).astype(BF16)


def hidden_grads(grad_rows, down_rows, slope):
    grad_active = jnp.einsum("nd,df->nf", grad_rows, down_rows, preferred_element_type=F32)
    return (grad_active * slope.astype(F32)).astype(BF16)


def attended_grads(grad_rows, mix_rows):
    return jnp.einsum("nd,de->ne", grad_rows, mix_rows, preferred_element_type=F32).astype(BF16)


def back_rows(grads, weight_rows):
    return jnp.einsum("nf,df->nd", grads, weight_rows, preferred_element_type=F32)


def grad_half(rows, columns, part):
    width = rows.shape[1] // 2
    chosen = rows[:, part * width : (part + 1) * width]
    return jnp.einsum("nd,nf->df", chosen, columns, preferred_element_type=F32).astype(BF16)


def plus(*terms):
    return functools.reduce(lambda a, b: a + b, [t.astype(F32) for t in terms])


def width_sums(grad_first, grad_second, xhat, grad_local):
    return jnp.stack(
        [
            jnp.sum(grad_first * xhat, axis=0),
            jnp.sum(grad_second * xhat, axis=0),
            jnp.sum(grad_first, axis=0),
            jnp.sum(grad_second, axis=0),
            jnp.sum(grad_local.astype(F32), axis=0),
        ],
        axis=0,
    )


def shards(
    tokens,
    seq_start,
    proj_weight,
    proj_bias,
    out_weight,
    up_weight,
    up_bias,
    down_weight,
    norm_gains,
    biases,
    cotangent,
):
    local_rows, width = tokens.shape
    n_dp, n_tensor = lax.axis_size("dp"), lax.axis_size("tensor")
    dp_index, tensor_index = lax.axis_index("dp"), lax.axis_index("tensor")
    row_count = local_rows * n_tensor
    hidden_width = up_weight.shape[1]
    heads_here = proj_bias.shape[1]
    head_size = proj_bias.shape[2] * n_dp
    local_width = heads_here * head_size
    joined_width = 3 * local_width
    columns = norm_gains.shape[1]

    vectors = jnp.concatenate(
        [norm_gains.reshape(1, -1), biases.reshape(1, -1), proj_bias.reshape(1, -1), up_bias.reshape(1, -1)],
        axis=1,
    )
    table = jnp.zeros((n_dp * n_tensor, vectors.shape[1]), BF16)
    table = lax.dynamic_update_slice(table, vectors, (dp_index * n_tensor + tensor_index, 0))
    local_tokens, local_grads = to_frame(tokens), to_frame(cotangent)
    positions = dp_index * row_count + jnp.arange(row_count, dtype=jnp.int32) - seq_start
    tables = attention_tables(positions, seq_start)
    me = tensor_index.astype(jnp.int32).reshape(1)
    flat_proj = proj_weight.reshape(-1, joined_width)

    def small_parameters(table):
        six_rows = table[:, : 6 * columns].reshape(n_dp * n_tensor, 6, columns).transpose(1, 0, 2)
        six_rows = to_frame(six_rows.reshape(6, width).astype(F32))
        of_tensor = lax.dynamic_index_in_dim(
            table[:, 6 * columns :].reshape(n_dp, n_tensor, -1), tensor_index, 1, keepdims=False
        ).astype(F32)
        joined_bias = (
            of_tensor[:, : proj_bias.size]
            .reshape(n_dp, 3, heads_here, -1)
            .transpose(1, 2, 0, 3)
            .reshape(joined_width)
        )
        hidden_bias = of_tensor[:, proj_bias.size :].reshape(hidden_width)
        return six_rows[:2], six_rows[2:], joined_bias, hidden_bias

    def attend(first_rows, joined_rows, joined_bias):
        projected = jnp.dot(first_rows, joined_rows, preferred_element_type=F32) + joined_bias
        return attention_forward(projected, tables, me, heads_here, n_tensor)

    def attend_back(kept, grad_attended):
        queries, keys, values, log_total = kept
        backs = attention_backward(
            queries, keys, values, grad_attended, log_total, tables, me, heads_here, n_tensor
        )
        return jnp.concatenate(backs, axis=1)

    def finish_output(branches, shift_rows):
        output = local_tokens.astype(F32) + branches + shift_rows[2] + shift_rows[3]
        return from_frame(output.astype(BF16))

    def finish_input_grad(back):
        xhat_local, scale_local = standardize(local_tokens)
        grad_norm_in = (
            back
            - jnp.mean(back, axis=-1, keepdims=True)
            - xhat_local * jnp.mean(back * xhat_local, axis=-1, keepdims=True)
        ) * scale_local
        return from_frame(local_grads.astype(F32) + grad_norm_in)

    def small_shares(five, joined_bias_sums, up_bias_sums):
        five = five.reshape(5, width)
        mine = lax.dynamic_slice_in_dim(
            five, (dp_index * n_tensor + tensor_index) * columns, columns, 1
        )
        biases_grad = jnp.concatenate([mine[2:], mine[4:]], axis=0)
        joined_bias_sum = lax.dynamic_slice_in_dim(
            joined_bias_sums.reshape(3, heads_here, head_size),
            dp_index * proj_bias.shape[2],
            proj_bias.shape[2],
            2,
        )
        up_bias_sum = lax.dynamic_slice_in_dim(
            up_bias_sums.reshape(1, -1), dp_index * up_bias.shape[1], up_bias.shape[1], 1
        )
        return mine[:2], biases_grad, joined_bias_sum, up_bias_sum

    def small_grads(five, joined_bias_term, up_bias_term):
        five = from_frame(five).reshape(1, -1)
        terms = jnp.concatenate([five, joined_bias_term[None], up_bias_term[None]], axis=1)
        terms = butterfly(terms, "dp")
        five = butterfly(terms[:, : 5 * width], "tensor")
        return small_shares(
            five, terms[0, 5 * width : 5 * width + joined_width], terms[:, 5 * width + joined_width :]
        )

    def plain():
        token_rows, grad_rows = line_gather(local_tokens), line_gather(local_grads)
        up_rows, down_rows = dp_gather(up_weight), dp_gather(down_weight.T)
        joined_rows, mix_rows = dp_gather(flat_proj), dp_gather(out_weight.T)
        up_rows, down_rows, joined_rows, mix_rows = (
            join(w, 0, None) for w in (up_rows, down_rows, joined_rows, mix_rows)
        )
        gain_rows, shift_rows, joined_bias, hidden_bias = small_parameters(
            butterfly(butterfly(table, "dp"), "tensor")
        )
        first_rows, second_rows = norm_rows(token_rows, gain_rows, shift_rows)
        activated, slope = cut(*hidden_units(second_rows, up_rows, hidden_bias))
        *kept, attended, log_total = attend(first_rows, joined_rows, joined_bias)
        branches = line_scatter(branch_rows(attended, mix_rows, activated, down_rows))
        output = finish_output(branches, shift_rows)
        grad_hidden = hidden_grads(grad_rows, down_rows, slope)
        down_sum = weight_grad(grad_rows, activated)
        up_sum = weight_grad(second_rows, grad_hidden)
        grad_second = back_rows(grad_hidden, up_rows)
        grad_attended = attended_grads(grad_rows, mix_rows)
        mix_sum = weight_grad(grad_rows, attended)
        grad_projected = attend_back((*kept, log_total), grad_attended)
        joined_sum = weight_grad(first_rows, grad_projected)
        grad_first = back_rows(grad_projected, joined_rows)
        back = grad_first * gain_rows[0] + grad_second * gain_rows[1]
        input_grad = finish_input_grad(line_scatter(back.astype(BF16)))
        five = width_sums(grad_first, grad_second, standardize(token_rows)[0], local_grads)
        small = small_grads(
            five, jnp.sum(grad_projected, axis=0, dtype=F32), jnp.sum(grad_hidden, axis=0, dtype=F32)
        )
        return output, input_grad, joined_sum, mix_sum.T, up_sum, down_sum.T, small

    def staged():
        half = local_rows // 2
        first, second = slice(0, half), slice(half, 2 * half)

        def x(values):
            return xor_shift(values, "dp", 2)

        def y(values):
            return xor_shift(values, "dp", 4)

        def core(values):
            return xor_shift(values, "dp", 1)

        def gather_step(up, down, s):
            up = lax.ppermute(up, "tensor", [(i, i + 1) for i in range(s, 3)])
            down = lax.ppermute(down, "tensor", [(i + 1, i) for i in range(3 - s)])
            return up, down

        def scatter_terms(halves, up, down, s):
            came = () if s == 1 else (up, down)
            return step_terms(halves, 4 - s, s, local_rows, *came)

        def scatter_step(to_up, to_down, s):
            up = lax.ppermute(to_up, "tensor", [(i, i + 1) for i in range(s)])
            down = lax.ppermute(to_down, "tensor", [(i, i - 1) for i in range(4 - s, 4)])
            return up, down

        def in_turn(block, ups, downs):
            blocks = [block] + [
                jnp.where(tensor_index + r < 4, downs[r - 1], ups[3 - r]) for r in range(1, 4)
            ]
            return jnp.concatenate(blocks, axis=0)

        def pair(top, low):
            return jnp.concatenate([top, low], axis=0)

        def place(base, piece, part):
            return lax.dynamic_update_slice(base, piece, ((4 * part + 2) * local_rows, 0))

        def at(keep, came, start, stop):
            return plus(keep[start * half : stop * half], came[start * half : stop * half])

        def joined_half(first_rows, grad_projected, grad_rows, attended, part):
            return jnp.concatenate(
                [grad_half(first_rows, grad_projected, part), grad_half(grad_rows, attended, part)], axis=1
            )

        wa = up_weight
        wb = jnp.concatenate([flat_proj, out_weight.T], axis=1)
        wc = down_weight.T

        ax, ay = x(wa), y(wa)
        tu1, td1 = gather_step(local_tokens, local_tokens, 0)
        table1 = table + core(table)
        table1, ax, ay = cut(table1, ax, ay)
        table1 = table1 + x(table1) + y(table1) + xor_shift(table1, "dp", 6)
        tu1, td1, ax, ay, table1, wb, wc, tables1 = cut(tu1, td1, ax, ay, table1, wb, wc, tables)
        tu2, td2 = gather_step(tu1, td1, 1)
        bx, by = x(wb), y(wb)
        table2 = table1 + xor_shift(table1, "tensor", 1)
        tu2, td2, bx, by, table2, local_grads1 = cut(tu2, td2, bx, by, table2, local_grads)
        tu3, td3 = gather_step(tu2, td2, 2)
        fa, fb = x(ay), y(bx)
        table3 = table2 + xor_shift(table2, "tensor", 2)
        both = lay(wa, ax, ay, wb, bx, by)
        tu3, td3, fa, fb, table3, both = cut(tu3, td3, fa, fb, table3, both)
        both_1 = place(place(both, fa, 0), fb, 1)
        both_1, wc, local_grads1 = cut(both_1, wc, local_grads1)
        cu1, cd1 = gather_step(local_grads1, local_grads1, 0)
        cx, cy = x(wc), y(wc)
        both_2 = core(both_1)
        gain_rows, shift_rows, joined_bias, hidden_bias = small_parameters(table3)
        token_rows = in_turn(local_tokens, (tu1, tu2, tu3), (td1, td2, td3))
        first_rows, second_rows = norm_rows(token_rows, gain_rows, shift_rows)
        mean = jnp.mean(token_rows.astype(F32), axis=-1, keepdims=True)
        _, scale = standardize(token_rows)
        mean, scale = (jnp.broadcast_to(v, (row_count, 128)) for v in (mean, scale))
        activated, slope = hidden_half(second_rows, both_1, both_2, hidden_bias)
        cu1, cd1, cx, cy, both_1, both_2, first_rows, activated, slope = cut(
            cu1, cd1, cx, cy, both_1, both_2, first_rows, activated, slope
        )
        cu2, cd2 = gather_step(cu1, cd1, 1)
        fc = x(cy)
        down_0 = lay(wc, cx, cy)
        *kept, attended, log_total = joined_forward(
            first_rows, both_1, both_2, joined_bias.reshape(1, -1), tables1, me, heads_here, head_size, n_tensor
        )
        cu2, cd2, fc, attended, down_0, mean, scale = cut(cu2, cd2, fc, attended, down_0, mean, scale)
        cu3, cd3 = gather_step(cu2, cd2, 2)
        down_1 = place(down_0, fc, 0)
        down_2 = core(down_1)
        branch_1 = branch_half(attended, both_1, activated, down_1)
        branch_2 = branch_half(attended, both_2, activated, down_2)
        cu3, cd3, branch_1, branch_2, activated = cut(cu3, cd3, branch_1, branch_2, activated)
        branches = (branch_1, branch_2)
        zu, zd, activated, cu3, cd3 = cut(*scatter_terms(branches, None, None, 1), activated, cu3, cd3)
        bu, bd = scatter_step(zu, zd, 1)
        grad_rows = in_turn(local_grads1, (cu1, cu2, cu3), (cd1, cd2, cd3))
        came_d = core(grad_half(grad_rows, activated, 1))
        keep_d = grad_half(grad_rows, activated, 0)
        grad_hidden, up_bias_term = hidden_back(grad_rows, down_1, down_2, slope)
        bu, bd, came_d, keep_d, grad_hidden, grad_rows = cut(
            bu, bd, came_d, keep_d, grad_hidden, grad_rows
        )
        zu, zd, sx, sy, second_rows, grad_hidden, grad_rows = cut(
            *scatter_terms(branches, bu, bd, 2),
            *pair_sums(keep_d, came_d, half),
            second_rows, grad_hidden, grad_rows,
        )
        bu, bd = scatter_step(zu, zd, 2)
        d1x, d1y = x(sx), y(sy)
        came_u = core(grad_half(second_rows, grad_hidden, 1))
        keep_u = grad_half(second_rows, grad_hidden, 0)
        grad_projected = mixed_backward(
            *kept, grad_rows, both_1, both_2, log_total, tables1, me, heads_here, n_tensor
        )
        bu, bd, d1x, d1y, came_u, keep_u, grad_projected, grad_hidden = cut(
            bu, bd, d1x, d1y, came_u, keep_u, grad_projected, grad_hidden
        )
        d2x = plus(at(keep_d, came_d, 2, 3), d1y[first]).astype(BF16)
        d2y = plus(at(keep_d, came_d, 7, 8), d1x[second]).astype(BF16)
        zu, zd, sx, sy, grad_hidden, grad_projected = cut(
            *scatter_terms(branches, bu, bd, 3),
            pair(d2x, at(keep_u, came_u, 4, 5).astype(BF16)),
            pair(d2y, at(keep_u, came_u, 5, 6).astype(BF16)),
            grad_hidden, grad_projected,
        )
        bu, bd = scatter_step(zu, zd, 3)
        s9x, s9y = x(sx), y(sy)
        came_j = core(joined_half(first_rows, grad_projected, grad_rows, attended, 1))
        back_1, sums_1 = back_half(grad_hidden, grad_projected, both_1, token_rows, mean, scale, gain_rows, 0)
        back_2, sums_2 = back_half(grad_hidden, grad_projected, both_2, token_rows, mean, scale, gain_rows, 1)
        bu, bd, s9x, s9y, came_j, back_1, back_2, sums_1, sums_2, grad_projected, attended = cut(
            bu, bd, s9x, s9y, came_j, back_1, back_2, sums_1, sums_2, grad_projected, attended
        )
        backs = (back_1, back_2)
        none = jnp.zeros((half, s9x.shape[1]), BF16)
        zu, zd, sx, sy, first_rows, grad_rows, bu, bd, sums_1, sums_2 = cut(
            *scatter_terms(backs, None, None, 1),
            plus(at(keep_u, came_u, 2, 4), pair(s9y[second], none)).astype(BF16),
            plus(at(keep_u, came_u, 6, 8), pair(none, s9x[second])).astype(BF16),
            first_rows, grad_rows, bu, bd, sums_1, sums_2,
        )
        eu, ed = scatter_step(zu, zd, 1)
        s10x, s10y = x(sx), y(sy)
        keep_j = joined_half(first_rows, grad_projected, grad_rows, attended, 0)
        five = jnp.concatenate(
            [
                jnp.concatenate([sums_1[:4], sums_2[:4]], axis=1),
                jnp.sum(local_grads.astype(F32), axis=0, keepdims=True),
            ],
            axis=0,
        )
        sx, sy = pair_sums(keep_j, came_j, half)
        five = five.reshape(1, -1)
        five = five + xor_shift(five, "tensor", 1)
        five = from_frame(five.reshape(5, width)).reshape(1, -1)
        eu, ed, s10x, s10y, keep_j, five, bu, bd, sx, sy = cut(
            eu, ed, s10x, s10y, keep_j, five, bu, bd, sx, sy
        )
        zu, zd, sx, sy, s10x, s10y, five = cut(
            *scatter_terms(backs, eu, ed, 2), sx, sy, s10x, s10y, five
        )
        eu, ed = scatter_step(zu, zd, 2)
        j1x, j1y = x(sx), y(sy)
        five = five + xor_shift(five, "tensor", 2)
        down_sum = own_sums(keep_d, came_d, half, (d1x, 0), (s9y, 0), (d1y, 1), (s9x, 0)).T
        up_sum = own_sums(keep_u, came_u, half, (s10x, 1), (s10y, 1), (s10x, 0), (s10y, 0))
        terms = jnp.concatenate(
            [
                jnp.sum(grad_projected, axis=0, dtype=F32, keepdims=True),
                up_bias_term,
            ],
            axis=1,
        )
        eu, ed, j1x, j1y, five, terms, down_sum, up_sum, bu, bd = cut(
            eu, ed, j1x, j1y, five, terms, down_sum, up_sum, bu, bd
        )
        zu, zd, sx, sy, five, bu, bd = cut(
            *scatter_terms(backs, eu, ed, 3),
            plus(at(keep_j, came_j, 2, 3), j1y[first]).astype(BF16),
            plus(at(keep_j, came_j, 7, 8), j1x[second]).astype(BF16),
            five, bu, bd,
        )
        eu, ed = scatter_step(zu, zd, 3)
        j2x, j2y = x(sx), y(sy)
        own = jnp.concatenate([h[:local_rows] for h in branches], axis=1)
        output = finish_output(plus(own, bu, bd), shift_rows)
        terms = butterfly(jnp.concatenate([five, terms], axis=1), "dp")
        small = small_shares(
            terms[:, : 5 * width], terms[0, 5 * width : 5 * width + joined_width],
            terms[:, 5 * width + joined_width :],
        )
        joined_mix = own_sums(keep_j, came_j, half, (j1x, 0), (j2y, 0), (j1y, 1), (j2x, 0))
        joined_sum = joined_mix[:, :joined_width].reshape(proj_weight.shape)
        eu, ed, joined_sum, mix_sum = cut(eu, ed, joined_sum, joined_mix[:, joined_width:].T)
        input_grad = input_grad_rows(*backs, eu, ed, local_tokens, local_grads)
        return output, input_grad, joined_sum, mix_sum, up_sum, down_sum, small

    parts = staged() if fast_dp() and n_tensor == 4 else plain()
    output, input_grad, joined_sum, mix_sum, up_sum, down_sum, small = parts
    gains_grad, biases_grad, joined_bias_sum, up_bias_sum = small
    return (
        output,
        input_grad,
        joined_sum.reshape(proj_weight.shape),
        joined_bias_sum,
        mix_sum,
        up_sum,
        up_bias_sum,
        down_sum,
        gains_grad,
        biases_grad,
    )


def solution(mesh):
    in_specs = (
        P(("dp", "tensor"), None),
        P("dp"),
        P("dp", None, "tensor"),
        P(None, "tensor", "dp"),
        P("tensor", "dp"),
        P("dp", "tensor"),
        P("tensor", "dp"),
        P("tensor", "dp"),
        P(None, ("dp", "tensor")),
        P(None, ("dp", "tensor")),
        P(("dp", "tensor"), None),
    )
    out_specs = (
        P(("dp", "tensor"), None),
        P(("dp", "tensor"), None),
        P("dp", None, "tensor"),
        P(None, "tensor", "dp"),
        P("tensor", "dp"),
        P("dp", "tensor"),
        P("tensor", "dp"),
        P("tensor", "dp"),
        P(None, ("dp", "tensor")),
        P(None, ("dp", "tensor")),
    )
    return jax.shard_map(shards, mesh=mesh, in_specs=in_specs, out_specs=out_specs, check_vma=False)
```

```python
import functools

import jax
import jax.numpy as jnp
from jax import lax
from jax.experimental import pallas as pl
from jax.experimental.pallas import tpu as pltpu
from jax.sharding import PartitionSpec as P

ROT = 64
EPSILON = 1e-05
ROTARY_BASE = 10000.0
F32 = jnp.float32
BF16 = jnp.bfloat16
HALVES = [(0, 0), (0, 1), (2, 1), (2, 0), (6, 0), (6, 1), (4, 1), (4, 0)]
ORDER = HALVES + [(p ^ 1, h) for p, h in HALVES]


SMALL = pl.CostEstimate(flops=1000, bytes_accessed=1000, transcendentals=0)


def cut(*values):
    return lax.optimization_barrier(values)


def is_power(n):
    return n & (n - 1) == 0


def fast_dp():
    return lax.axis_size("dp") == 8


def xor_shift(values, axis, bit):
    size = lax.axis_size(axis)
    return lax.ppermute(values, axis, [(i, i ^ bit) for i in range(size)])


def butterfly(values, axis):
    size = lax.axis_size(axis)
    if not is_power(size):
        return lax.psum(values, axis)
    bit = 1
    while bit < size:
        values = values + xor_shift(values, axis, bit)
        bit *= 2
    return values


def columns_kernel(index_ref, x_ref, o_ref, *, count, step):
    for j in range(count):
        at = pl.multiple_of(index_ref[j] * step, step)
        o_ref[:, j * step : (j + 1) * step] = x_ref[:, pl.ds(at, step)]


def take_columns(values, index):
    rows, width = values.shape
    count = index.shape[0]
    tile = rows // 2 if rows % 64 == 0 else rows
    return pl.pallas_call(
        functools.partial(columns_kernel, count=count, step=width // count),
        out_shape=jax.ShapeDtypeStruct(values.shape, values.dtype),
        grid_spec=pltpu.PrefetchScalarGridSpec(
            num_scalar_prefetch=1,
            grid=(rows // tile,),
            in_specs=[pl.BlockSpec((tile, width), lambda i, s: (i, 0))],
            out_specs=pl.BlockSpec((tile, width), lambda i, s: (i, 0)),
        ),
        cost_estimate=SMALL,
        name="columns",
    )(index, values)


FRAME = [[(me ^ p) * 2 + h for p, h in ORDER] for me in range(8)]
PLAIN = [[row.index(k) for k in range(16)] for row in FRAME]


def frame_index():
    return lax.dynamic_index_in_dim(jnp.array(FRAME, jnp.int32), lax.axis_index("dp"), 0, keepdims=False)


def plain_index():
    return lax.dynamic_index_in_dim(jnp.array(PLAIN, jnp.int32), lax.axis_index("dp"), 0, keepdims=False)


def to_frame(values):
    return take_columns(values, frame_index()) if fast_dp() else values


def from_frame(values):
    return take_columns(values, plain_index()) if fast_dp() else values


def dp_gather(shard):
    if not fast_dp():
        return [lax.all_gather(shard, "dp", axis=0, tiled=True)]
    half = shard.shape[0] // 2
    from_x = xor_shift(shard, "dp", 2)
    from_y = xor_shift(shard, "dp", 4)
    far_1 = xor_shift(from_y[:half], "dp", 2)
    far_2 = xor_shift(from_x[half:], "dp", 4)
    far = jnp.concatenate([far_1, far_2], axis=0)
    near = xor_shift(shard, "dp", 1)
    near_x = xor_shift(from_x, "dp", 1)
    near_y = xor_shift(from_y, "dp", 1)
    near_far = xor_shift(far, "dp", 1)
    out = []
    for own, x, f, y in ((shard, from_x, far, from_y), (near, near_x, near_far, near_y)):
        out += [own, x[half:], x[:half], f, y[half:], y[:half]]
    return out


def join(pieces, start, stop):
    return jnp.concatenate([p[:, start:stop] for p in pieces], axis=0)


def dp_scatter(make):
    away = make(1)
    came = xor_shift(away, "dp", 1)
    kept = make(0)
    rows = kept.shape[0] // 4
    half = rows // 2

    def summed(start, stop):
        return kept[start:stop].astype(F32) + came[start:stop].astype(F32)

    first_x = xor_shift(summed(rows + half, 2 * rows + half).astype(BF16), "dp", 2)
    first_y = xor_shift(summed(2 * rows + half, 3 * rows + half).astype(BF16), "dp", 4)
    last_x = summed(rows, rows + half) + first_y[:half].astype(F32)
    last_y = summed(3 * rows + half, 4 * rows) + first_x[half:].astype(F32)
    last_x = xor_shift(last_x.astype(BF16), "dp", 2)
    last_y = xor_shift(last_y.astype(BF16), "dp", 4)
    top = summed(0, half) + first_x[:half].astype(F32) + last_y.astype(F32)
    low = summed(half, rows) + first_y[half:].astype(F32) + last_x.astype(F32)
    return jnp.concatenate([top, low], axis=0)


def weight_grad(rows, columns):
    def make(part):
        width = rows.shape[1] // 2
        chosen = rows[:, part * width : (part + 1) * width]
        return jnp.einsum("nd,nf->df", chosen, columns, preferred_element_type=F32).astype(BF16)

    if fast_dp():
        return dp_scatter(make)
    whole = jnp.einsum("nd,nf->df", rows, columns, preferred_element_type=F32).astype(BF16)
    return lax.psum_scatter(whole, "dp", scatter_dimension=0, tiled=True).astype(F32)


def line_gather(block):
    size = lax.axis_size("tensor")
    me = lax.axis_index("tensor")
    up = down = block
    ups, downs = [block], [block]
    for s in range(size - 1):
        up = lax.ppermute(up, "tensor", [(i, i + 1) for i in range(s, size - 1)])
        down = lax.ppermute(down, "tensor", [(i + 1, i) for i in range(size - 1 - s)])
        ups.append(up)
        downs.append(down)
    blocks = [block]
    for r in range(1, size):
        blocks.append(jnp.where(me + r < size, downs[r], ups[size - r]))
    return jnp.concatenate(blocks, axis=0)


def line_scatter(terms):
    size = lax.axis_size("tensor")
    rows = terms.shape[0] // size

    def block(r):
        return terms[r * rows : (r + 1) * rows]

    up = down = None
    for s in range(1, size):
        to_up, to_down = block(size - s), block(s)
        if s > 1:
            to_up = (to_up.astype(F32) + up.astype(F32)).astype(BF16)
            to_down = (to_down.astype(F32) + down.astype(F32)).astype(BF16)
        up = lax.ppermute(to_up, "tensor", [(i, i + 1) for i in range(s)])
        down = lax.ppermute(to_down, "tensor", [(i, i - 1) for i in range(size - s, size)])
    return block(0).astype(F32) + up.astype(F32) + down.astype(F32)


def turn(values, cosine, low_sine, high_sine, sign):
    half = ROT // 2
    lanes = cosine.shape[-1]
    head = values[:, :lanes]
    turned = (
        head * cosine
        - sign * pltpu.roll(head, lanes - half, 1) * low_sine
        + sign * pltpu.roll(head, half, 1) * high_sine
    )
    return jnp.concatenate([turned, values[:, lanes:]], axis=1)


def contract(a, b, dims):
    return lax.dot_general(a, b, (dims, ((), ())), preferred_element_type=F32)


def masked(scores, column_starts, row_starts, query_block, block):
    keys = scores.shape[1]
    query = lax.broadcasted_iota(jnp.int32, scores.shape, 0) + query_block * block
    key = lax.broadcasted_iota(jnp.int32, scores.shape, 1)
    allowed = (column_starts == row_starts[:, :keys]) & (key <= query)
    return allowed, jnp.where(allowed, scores, -1e30)


def spots(me_ref, size, block):
    def spot(b):
        return pl.ds(pl.multiple_of(lax.rem(b - me_ref[0] + size, size) * block, block), block)

    return spot


def forward_block(q_out, k_out, v_out, att_ref, log_ref, col_ref, row_ref, spot, b, block):
    scale = q_out.shape[-1] ** (-0.5)
    here = slice(b * block, (b + 1) * block)
    query = q_out[spot(b), :]
    scores = jnp.concatenate(
        [contract(query, k_out[spot(c), :], ((1,), (1,))) for c in range(b + 1)], axis=1
    ) * scale
    _, scores = masked(scores, col_ref[here, :1], row_ref[:1, :], b, block)
    top = jnp.max(scores, axis=1, keepdims=True)
    powers = jnp.exp(scores - top)
    total = jnp.sum(powers, axis=1, keepdims=True)
    weights = (powers / total).astype(BF16)
    attended = contract(weights[:, :block], v_out[spot(0), :], ((1,), (0,)))
    for c in range(1, b + 1):
        attended = attended + contract(
            weights[:, c * block : (c + 1) * block], v_out[spot(c), :], ((1,), (0,))
        )
    att_ref[spot(b), :] = attended.astype(BF16)
    log_ref[0, here, :] = jnp.broadcast_to(top + jnp.log(total), (block, log_ref.shape[2]))


def forward_kernel(
    me_ref, q_ref, k_ref, v_ref, cos_ref, low_ref, high_ref, col_ref, row_ref,
    q_out, k_out, v_out, att_ref, log_ref, *, size, block,
):
    spot = spots(me_ref, size, block)
    for b in range(size):
        here = slice(b * block, (b + 1) * block)
        at = spot(b)
        tables = cos_ref[here, :], low_ref[here, :], high_ref[here, :]
        q_out[at, :] = turn(q_ref[at, :], *tables, 1.0).astype(BF16)
        k_out[at, :] = turn(k_ref[at, :], *tables, 1.0).astype(BF16)
        v_out[at, :] = v_ref[at, :].astype(BF16)
    for b in range(size):
        forward_block(q_out, k_out, v_out, att_ref, log_ref, col_ref, row_ref, spot, b, block)


def joined_forward_kernel(
    me_ref, rows_ref, qa_ref, ka_ref, va_ref, qb_ref, kb_ref, vb_ref, q_bias, k_bias, v_bias,
    cos_ref, low_ref, high_ref, col_ref, row_ref,
    q_out, k_out, v_out, att_ref, log_ref, *, size, block,
):
    spot = spots(me_ref, size, block)
    middle = qa_ref.shape[0]
    for b in range(size):
        here = slice(b * block, (b + 1) * block)
        at = spot(b)
        tables = cos_ref[here, :], low_ref[here, :], high_ref[here, :]
        top, low = rows_ref[at, :middle], rows_ref[at, middle:]

        def project(one, two, bias):
            return contract(top, one[:, :], ((1,), (0,))) + contract(low, two[:, :], ((1,), (0,))) + bias[:, :]

        q_out[at, :] = turn(project(qa_ref, qb_ref, q_bias), *tables, 1.0).astype(BF16)
        k_out[at, :] = turn(project(ka_ref, kb_ref, k_bias), *tables, 1.0).astype(BF16)
        v_out[at, :] = project(va_ref, vb_ref, v_bias).astype(BF16)
        forward_block(q_out, k_out, v_out, att_ref, log_ref, col_ref, row_ref, spot, b, block)


def backward_pass(
    q_ref, k_ref, v_ref, g_ref, log_ref, cos_ref, low_ref, high_ref, col_ref, row_ref,
    put, k_acc, v_acc, spot, size, block,
):
    scale = q_ref.shape[-1] ** (-0.5)
    for b in range(size):
        here = slice(b * block, (b + 1) * block)
        query, grad = q_ref[spot(b), :], g_ref[spot(b), :]
        scores = jnp.concatenate(
            [contract(query, k_ref[spot(c), :], ((1,), (1,))) for c in range(b + 1)], axis=1
        ) * scale
        allowed, scores = masked(scores, col_ref[here, :1], row_ref[:1, :], b, block)
        probs = jnp.where(allowed, jnp.exp(scores - log_ref[0, here, :1]), 0.0)
        grad_probs = jnp.concatenate(
            [contract(grad, v_ref[spot(c), :], ((1,), (1,))) for c in range(b + 1)], axis=1
        )
        inner = jnp.sum(probs * grad_probs, axis=1, keepdims=True)
        weights = probs.astype(BF16)
        grad_scores = (probs * (grad_probs - inner)).astype(BF16)
        back = None
        for c in range(b + 1):
            part = slice(c * block, (c + 1) * block)
            key_term = contract(grad_scores[:, part], query, ((0,), (0,)))
            value_term = contract(weights[:, part], grad, ((0,), (0,)))
            query_term = contract(grad_scores[:, part], k_ref[spot(c), :], ((1,), (0,)))
            back = query_term if c == 0 else back + query_term
            if c == b:
                k_acc[part, :] = key_term
                v_acc[part, :] = value_term
            else:
                k_acc[part, :] += key_term
                v_acc[part, :] += value_term
        tables = cos_ref[here, :], low_ref[here, :], high_ref[here, :]
        put(0, spot(b), turn(back * scale, *tables, -1.0).astype(BF16))
    for b in range(size):
        here = slice(b * block, (b + 1) * block)
        tables = cos_ref[here, :], low_ref[here, :], high_ref[here, :]
        put(1, spot(b), turn(k_acc[here, :] * scale, *tables, -1.0).astype(BF16))
        put(2, spot(b), v_acc[here, :].astype(BF16))


def backward_kernel(
    me_ref, q_ref, k_ref, v_ref, g_ref, log_ref, cos_ref, low_ref, high_ref, col_ref, row_ref,
    dq_ref, dk_ref, dv_ref, k_acc, v_acc, *, size, block,
):
    outs = (dq_ref, dk_ref, dv_ref)

    def put(k, at, value):
        outs[k][at, :] = value

    backward_pass(
        q_ref, k_ref, v_ref, g_ref, log_ref, cos_ref, low_ref, high_ref, col_ref, row_ref,
        put, k_acc, v_acc, spots(me_ref, size, block), size, block,
    )


def mixed_backward_kernel(
    me_ref, q_ref, k_ref, v_ref, g_ref, a_ref, b_ref, log_ref, cos_ref, low_ref, high_ref, col_ref, row_ref,
    d_ref, k_acc, v_acc, g_acc, *, size, block, heads,
):
    middle = a_ref.shape[0]
    head = q_ref.shape[1]
    for b in range(size):
        here = slice(b * block, (b + 1) * block)
        g_acc[here, :] = (
            contract(g_ref[here, :middle], a_ref[:, :], ((1,), (0,)))
            + contract(g_ref[here, middle:], b_ref[:, :], ((1,), (0,)))
        ).astype(BF16)
    h = pl.program_id(0)

    def put(k, at, value):
        d_ref[at, pl.ds(pl.multiple_of((k * heads + h) * head, head), head)] = value

    backward_pass(
        q_ref, k_ref, v_ref, g_acc, log_ref, cos_ref, low_ref, high_ref, col_ref, row_ref,
        put, k_acc, v_acc, spots(me_ref, size, block), size, block,
    )


def hidden_kernel(rows_ref, a_ref, b_ref, bias_ref, act_ref, slope_ref, *, step):
    middle = a_ref.shape[0]
    for i in range(rows_ref.shape[0] // step):
        here = slice(i * step, (i + 1) * step)
        hidden = contract(rows_ref[here, :middle], a_ref[:, :], ((1,), (0,)))
        hidden = hidden + contract(rows_ref[here, middle:], b_ref[:, :], ((1,), (0,))) + bias_ref[:, :]
        bell = lax.erf(hidden * (0.5**0.5))
        act_ref[here, :] = (0.5 * hidden * (1.0 + bell)).astype(BF16)
        slope = 0.5 * (1.0 + bell) + hidden * jnp.exp(-0.5 * hidden * hidden) * 0.3989422804014327
        slope_ref[here, :] = slope.astype(BF16)


def hidden_half(rows, top, low, bias):
    count, width = rows.shape
    out = top.shape[1]
    tile = 512
    half = pl.BlockSpec((width // 2, tile), lambda j: (0, j))
    made = pl.BlockSpec((count, tile), lambda j: (0, j))
    return pl.pallas_call(
        functools.partial(hidden_kernel, step=256),
        out_shape=(jax.ShapeDtypeStruct((count, out), BF16),) * 2,
        grid=(out // tile,),
        in_specs=[
            pl.BlockSpec((count, width), lambda j: (0, 0)), half, half, pl.BlockSpec((1, tile), lambda j: (0, j))
        ],
        out_specs=(made, made),
        cost_estimate=SMALL,
        name="hidden",
    )(rows, top, low, bias.reshape(1, -1))


def slope_kernel(rows_ref, a_ref, b_ref, slope_ref, out_ref, sum_ref, *, step):
    middle = a_ref.shape[0]
    total = 0.0
    for i in range(rows_ref.shape[0] // step):
        here = slice(i * step, (i + 1) * step)
        active = contract(rows_ref[here, :middle], a_ref[:, :], ((1,), (0,)))
        active = active + contract(rows_ref[here, middle:], b_ref[:, :], ((1,), (0,)))
        made = (active * slope_ref[here, :].astype(F32)).astype(BF16)
        out_ref[here, :] = made
        total = total + jnp.sum(made.astype(F32), axis=0, keepdims=True)
    sum_ref[:, :] = total


def hidden_back(rows, top, low, slope):
    count, width = rows.shape
    out = top.shape[1]
    tile = 512
    half = pl.BlockSpec((top.shape[0], tile), lambda j: (0, j))
    made = pl.BlockSpec((count, tile), lambda j: (0, j))
    return pl.pallas_call(
        functools.partial(slope_kernel, step=256),
        out_shape=(jax.ShapeDtypeStruct((count, out), BF16), jax.ShapeDtypeStruct((1, out), F32)),
        grid=(out // tile,),
        in_specs=[pl.BlockSpec((count, width), lambda j: (0, 0)), half, half, made],
        out_specs=(made, pl.BlockSpec((1, tile), lambda j: (0, j))),
        cost_estimate=SMALL,
        name="hidden_back",
    )(rows, top, low, slope)


def branch_kernel(att_ref, mix_ref, act_ref, down_ref, out_ref, *, step):
    for i in range(att_ref.shape[0] // step):
        here = slice(i * step, (i + 1) * step)
        total = contract(att_ref[here, :], mix_ref[:, :], ((1,), (1,)))
        total = total + contract(act_ref[here, :], down_ref[:, :], ((1,), (1,)))
        out_ref[here, :] = total.astype(BF16)


def branch_half(attended, mixed, activated, down):
    count, inner = attended.shape
    units = activated.shape[1]
    width = down.shape[0]
    tile = 256
    spot = mixed.shape[1] // inner - 1
    return pl.pallas_call(
        functools.partial(branch_kernel, step=256),
        out_shape=jax.ShapeDtypeStruct((count, width), BF16),
        grid=(width // tile,),
        in_specs=[
            pl.BlockSpec((count, inner), lambda j: (0, 0)),
            pl.BlockSpec((tile, inner), lambda j: (j + width // tile, spot)),
            pl.BlockSpec((count, units), lambda j: (0, 0)),
            pl.BlockSpec((tile, units), lambda j: (j, 0)),
        ],
        out_specs=pl.BlockSpec((count, tile), lambda j: (0, j)),
        cost_estimate=SMALL,
        name="branches",
    )(attended, mixed, activated, down)


def back_kernel(
    hid_ref, proj_ref, up_1, up_2, join_1, join_2, tok_ref, mean_ref, scale_ref, gain_ref, back_ref, sum_ref,
    *, step, tiles,
):
    def work(up_ref, join_ref):
        sums = [0.0] * 4
        for i in range(hid_ref.shape[0] // step):
            here = slice(i * step, (i + 1) * step)
            two = contract(hid_ref[here, :], up_ref[:, :], ((1,), (1,)))
            one = contract(proj_ref[here, :], join_ref[:, :], ((1,), (1,)))
            back_ref[here, :] = (one * gain_ref[:1, :] + two * gain_ref[1:2, :]).astype(BF16)
            xhat = (tok_ref[here, :].astype(F32) - mean_ref[here, :1]) * scale_ref[here, :1]
            for k, term in enumerate((one * xhat, two * xhat, one, two)):
                sums[k] = sums[k] + jnp.sum(term, axis=0, keepdims=True)
        for k in range(4):
            sum_ref[k : k + 1, :] = sums[k]

    @pl.when(pl.program_id(0) < tiles)
    def _():
        work(up_1, join_1)

    @pl.when(pl.program_id(0) >= tiles)
    def _():
        work(up_2, join_2)


def back_whole(grad_hidden, grad_projected, both_1, both_2, token_rows, mean, scale, gains):
    count, units = grad_hidden.shape
    joined = grad_projected.shape[1]
    width = both_1.shape[0] // 2
    tile = 256
    tiles = width // tile
    whole = lambda j: (0, 0)

    def of(columns, block):
        low = pl.BlockSpec((tile, columns), lambda j: (block + jnp.minimum(j, tiles - 1), 0))
        high = pl.BlockSpec((tile, columns), lambda j: (block + jnp.maximum(j - tiles, 0), 0))
        return [low, high]

    return pl.pallas_call(
        functools.partial(back_kernel, step=256, tiles=tiles),
        out_shape=(jax.ShapeDtypeStruct((count, 2 * width), BF16), jax.ShapeDtypeStruct((8, 2 * width), F32)),
        grid=(2 * tiles,),
        in_specs=[pl.BlockSpec((count, units), whole), pl.BlockSpec((count, joined), whole)]
        + of(units, 0) + of(joined, tiles)
        + [
            pl.BlockSpec((count, tile), lambda j: (0, j)),
            pl.BlockSpec((count, 128), whole),
            pl.BlockSpec((count, 128), whole),
            pl.BlockSpec((2, tile), lambda j: (0, j)),
        ],
        out_specs=(pl.BlockSpec((count, tile), lambda j: (0, j)), pl.BlockSpec((8, tile), lambda j: (0, j))),
        cost_estimate=SMALL,
        name="back",
    )(grad_hidden, grad_projected, both_1, both_2, both_1, both_2, token_rows, mean, scale, gains)


def lay_kernel(*refs):
    *ins, out_ref = refs
    rows = ins[0].shape[0]
    half = rows // 2
    for w in range(len(ins) // 3):
        own, from_x, from_y = ins[3 * w : 3 * w + 3]
        base = 4 * w * rows
        out_ref[base : base + rows, :] = own[:, :]
        out_ref[base + 2 * rows : base + 3 * rows, :] = jnp.zeros(own.shape, BF16)
        for piece, at in ((from_x, base + rows), (from_y, base + 3 * rows)):
            out_ref[at : at + half, :] = piece[half:, :]
            out_ref[at + half : at + rows, :] = piece[:half, :]


def lay(*pieces):
    rows, width = pieces[0].shape
    weights = len(pieces) // 3
    tile = width // 4
    return pl.pallas_call(
        lay_kernel,
        out_shape=jax.ShapeDtypeStruct((4 * rows * weights, width), BF16),
        grid=(4,),
        in_specs=[pl.BlockSpec((rows, tile), lambda j: (0, j))] * len(pieces),
        out_specs=pl.BlockSpec((4 * rows * weights, tile), lambda j: (0, j)),
        cost_estimate=SMALL,
        name="lay",
    )(*pieces)


def pair_sums_kernel(kept_x, came_x, kept_y, came_y, to_x, to_y):
    to_x[:, :] = (kept_x[:, :].astype(F32) + came_x[:, :].astype(F32)).astype(BF16)
    to_y[:, :] = (kept_y[:, :].astype(F32) + came_y[:, :].astype(F32)).astype(BF16)


def pair_sums(kept, came, half):
    width = kept.shape[1]
    of_x = pl.BlockSpec((half, width), lambda i: (3 + i, 0))
    of_y = pl.BlockSpec((half, width), lambda i: (5 + i, 0))
    out = pl.BlockSpec((half, width), lambda i: (i, 0))
    return pl.pallas_call(
        pair_sums_kernel,
        out_shape=(jax.ShapeDtypeStruct((2 * half, width), BF16),) * 2,
        grid=(2,),
        in_specs=[of_x, of_x, of_y, of_y],
        out_specs=(out, out),
        cost_estimate=SMALL,
        name="pair_sums",
    )(kept, came, kept, came)


def own_sums_kernel(kept, came, a, b, c, d, out):
    half = a.shape[0]
    top, low = slice(0, half), slice(half, 2 * half)
    for part, one, two in ((top, a, b), (low, c, d)):
        total = kept[part, :].astype(F32) + came[part, :].astype(F32)
        out[part, :] = total + one[:, :].astype(F32) + two[:, :].astype(F32)


def own_sums(kept, came, half, *came_in):
    width = kept.shape[1]
    tile = width // 4
    rows = pl.BlockSpec((2 * half, tile), lambda j: (0, j))
    return pl.pallas_call(
        own_sums_kernel,
        out_shape=jax.ShapeDtypeStruct((2 * half, width), F32),
        grid=(4,),
        in_specs=[rows, rows] + [pl.BlockSpec((half, tile), lambda j, k=k: (k, j)) for _, k in came_in],
        out_specs=rows,
        cost_estimate=SMALL,
        name="own_sums",
    )(kept, came, *(v for v, _ in came_in))


def terms_kernel(*refs):
    *ins, to_up, to_down = refs
    up = jnp.concatenate([ins[0][:, :], ins[1][:, :]], axis=1)
    down = jnp.concatenate([ins[2][:, :], ins[3][:, :]], axis=1)
    if len(ins) > 4:
        up = (up.astype(F32) + ins[4][:, :].astype(F32)).astype(BF16)
        down = (down.astype(F32) + ins[5][:, :].astype(F32)).astype(BF16)
    to_up[:, :] = up
    to_down[:, :] = down


def step_terms(halves, up_block, down_block, rows, width, *came):
    tiles = 2
    tile = rows // tiles

    def of(block):
        return [pl.BlockSpec((tile, width), lambda i, k=k: (block * tiles + i, k)) for _, k in halves]

    full = pl.BlockSpec((tile, 2 * width), lambda i: (i, 0))
    arrays = [v for v, _ in halves]
    return pl.pallas_call(
        terms_kernel,
        out_shape=(jax.ShapeDtypeStruct((rows, 2 * width), BF16),) * 2,
        grid=(tiles,),
        in_specs=of(up_block) + of(down_block) + [full] * len(came),
        out_specs=(full, full),
        cost_estimate=SMALL,
        name="terms",
    )(*arrays, *arrays, *came)


def input_grad_kernel(index_ref, own_ref, up_ref, down_ref, tok_ref, grad_ref, out_ref):
    back = own_ref[:, :].astype(F32) + up_ref[:, :].astype(F32) + down_ref[:, :].astype(F32)
    xhat, scale = standardize(tok_ref[:, :])
    back = back - jnp.mean(back, axis=-1, keepdims=True) - xhat * jnp.mean(back * xhat, axis=-1, keepdims=True)
    total = grad_ref[:, :].astype(F32) + back * scale
    count = index_ref.shape[0]
    step = total.shape[1] // count
    for j in range(count):
        out_ref[:, pl.ds(pl.multiple_of(index_ref[j] * step, step), step)] = total[:, j * step : (j + 1) * step]


def input_grad_rows(own, up, down, tokens, grads):
    rows, width = tokens.shape
    tile = rows // 4
    full = pl.BlockSpec((tile, width), lambda i, s: (i, 0))
    return pl.pallas_call(
        input_grad_kernel,
        out_shape=jax.ShapeDtypeStruct((rows, width), F32),
        grid_spec=pltpu.PrefetchScalarGridSpec(
            num_scalar_prefetch=1,
            grid=(rows // tile,),
            in_specs=[full] * 5,
            out_specs=full,
        ),
        cost_estimate=SMALL,
        name="input_grad",
    )(frame_index(), own, up, down, tokens, grads)


def joined_forward(rows, top, low, bias, tables, me, heads, head, size):
    count, width = rows.shape
    block = count // size
    whole = lambda h, s: (0, 0)
    table_specs = [pl.BlockSpec((count, 128), whole)] * 4 + [pl.BlockSpec((8, count), whole)]
    by_head = pl.BlockSpec((count, head), lambda h, s: (0, h))
    wide = jax.ShapeDtypeStruct((count, heads * head), BF16)

    def thirds(n, spot):
        return [pl.BlockSpec((n, head), lambda h, s, k=k: (spot, k * heads + h)) for k in range(3)]

    return pl.pallas_call(
        functools.partial(joined_forward_kernel, size=size, block=block),
        out_shape=(wide, wide, wide, wide, jax.ShapeDtypeStruct((heads, count, 128), F32)),
        grid_spec=pltpu.PrefetchScalarGridSpec(
            num_scalar_prefetch=1,
            grid=(heads,),
            in_specs=[pl.BlockSpec((count, width), whole)]
            + thirds(width // 2, 1) + thirds(width // 2, 1) + thirds(1, 0) + table_specs,
            out_specs=(by_head,) * 4 + (pl.BlockSpec((1, count, 128), lambda h, s: (h, 0, 0)),),
        ),
        cost_estimate=SMALL,
        name="joined_forward",
    )(me, rows, top, top, top, low, low, low, bias, bias, bias, *tables)


def mixed_backward(queries, keys, values, grads, top, low, log_total, tables, me, heads, size):
    count = queries.shape[0]
    head = queries.shape[1] // heads
    block = count // size
    whole = lambda h, s: (0, 0)
    table_specs = [pl.BlockSpec((count, 128), whole)] * 4 + [pl.BlockSpec((8, count), whole)]
    by_head = pl.BlockSpec((count, head), lambda h, s: (0, h))
    mix = pl.BlockSpec((grads.shape[1] // 2, head), lambda h, s: (1, 3 * heads + h))
    return pl.pallas_call(
        functools.partial(mixed_backward_kernel, size=size, block=block, heads=heads),
        out_shape=jax.ShapeDtypeStruct((count, 3 * heads * head), BF16),
        grid_spec=pltpu.PrefetchScalarGridSpec(
            num_scalar_prefetch=1,
            grid=(heads,),
            in_specs=[by_head] * 3
            + [pl.BlockSpec((count, grads.shape[1]), whole), mix, mix]
            + [pl.BlockSpec((1, count, 128), lambda h, s: (h, 0, 0))]
            + table_specs,
            out_specs=pl.BlockSpec((count, 3 * heads * head), whole),
            scratch_shapes=[pltpu.VMEM((count, head), F32)] * 2 + [pltpu.VMEM((count, head), BF16)],
        ),
        cost_estimate=SMALL,
        name="mixed_backward",
    )(me, queries, keys, values, grads, top, low, log_total, *tables)


def attention_tables(positions, starts):
    half = ROT // 2
    frequency = ROTARY_BASE ** (-(jnp.arange(half, dtype=F32) * 2.0) / ROT)
    angles = positions.astype(F32)[:, None] * frequency[None, :]
    cosine, sine = jnp.cos(angles), jnp.sin(angles)
    rows = positions.shape[0]
    cosines = jnp.concatenate([cosine, cosine, jnp.ones((rows, 128 - ROT), F32)], axis=1)
    low = jnp.concatenate([sine, jnp.zeros((rows, 128 - half), F32)], axis=1)
    high = jnp.concatenate([jnp.zeros((rows, half), F32), sine, jnp.zeros((rows, 128 - ROT), F32)], axis=1)
    columns = jnp.broadcast_to(starts[:, None], (rows, 128))
    across = jnp.broadcast_to(starts[None, :], (8, rows))
    return cosines, low, high, columns, across


def attention_forward(projected, tables, me, heads, size):
    rows = projected.shape[0]
    head = projected.shape[1] // (3 * heads)
    block = rows // size
    whole = lambda h, s: (0, 0)
    table_specs = [pl.BlockSpec((rows, 128), whole)] * 4 + [pl.BlockSpec((8, rows), whole)]
    by_head = pl.BlockSpec((rows, head), lambda h, s: (0, h))
    wide = jax.ShapeDtypeStruct((rows, heads * head), BF16)
    return pl.pallas_call(
        functools.partial(forward_kernel, size=size, block=block),
        out_shape=(wide, wide, wide, wide, jax.ShapeDtypeStruct((heads, rows, 128), F32)),
        grid_spec=pltpu.PrefetchScalarGridSpec(
            num_scalar_prefetch=1,
            grid=(heads,),
            in_specs=[
                pl.BlockSpec((rows, head), lambda h, s, k=k: (0, k * heads + h)) for k in range(3)
            ]
            + table_specs,
            out_specs=(by_head,) * 4 + (pl.BlockSpec((1, rows, 128), lambda h, s: (h, 0, 0)),),
        ),
        cost_estimate=pl.CostEstimate(
            flops=heads * rows * rows * head * 40, bytes_accessed=rows * head * heads * 24,
            transcendentals=heads * rows * rows // 2,
        ),
        name="attention_forward",
    )(me, projected, projected, projected, *tables)


def attention_backward(queries, keys, values, grads, log_total, tables, me, heads, size):
    rows = queries.shape[0]
    head = queries.shape[1] // heads
    block = rows // size
    whole = lambda h, s: (0, 0)
    table_specs = [pl.BlockSpec((rows, 128), whole)] * 4 + [pl.BlockSpec((8, rows), whole)]
    by_head = pl.BlockSpec((rows, head), lambda h, s: (0, h))
    wide = jax.ShapeDtypeStruct((rows, heads * head), BF16)
    return pl.pallas_call(
        functools.partial(backward_kernel, size=size, block=block),
        out_shape=(wide, wide, wide),
        grid_spec=pltpu.PrefetchScalarGridSpec(
            num_scalar_prefetch=1,
            grid=(heads,),
            in_specs=[by_head] * 4
            + [pl.BlockSpec((1, rows, 128), lambda h, s: (h, 0, 0))]
            + table_specs,
            out_specs=(by_head,) * 3,
            scratch_shapes=[pltpu.VMEM((rows, head), F32)] * 2,
        ),
        cost_estimate=pl.CostEstimate(
            flops=heads * rows * rows * head * 60, bytes_accessed=rows * head * heads * 24,
            transcendentals=heads * rows * rows // 2,
        ),
        name="attention_backward",
    )(me, queries, keys, values, grads, log_total, *tables)


def standardize(values):
    values = values.astype(F32)
    centered = values - jnp.mean(values, axis=-1, keepdims=True)
    spread = jnp.mean(centered * centered, axis=-1, keepdims=True)
    scale = lax.rsqrt(spread + EPSILON)
    return centered * scale, scale


def norm_rows(token_rows, gain_rows, shift_rows):
    xhat, _ = standardize(token_rows)
    first_rows = (xhat * gain_rows[0] + shift_rows[0]).astype(BF16)
    second_rows = (xhat * gain_rows[1] + shift_rows[1]).astype(BF16)
    return first_rows, second_rows


def hidden_units(second_rows, up_rows, hidden_bias):
    hidden = jnp.dot(second_rows, up_rows, preferred_element_type=F32) + hidden_bias
    bell = lax.erf(hidden * (0.5**0.5))
    activated = (0.5 * hidden * (1.0 + bell)).astype(BF16)
    slope = 0.5 * (1.0 + bell) + hidden * jnp.exp(-0.5 * hidden * hidden) * 0.3989422804014327
    return activated, slope.astype(BF16)


def branch_rows(attended, mix_rows, activated, down_rows):
    return (
        jnp.einsum("ne,de->nd", attended, mix_rows, preferred_element_type=F32)
        + jnp.einsum("nf,df->nd", activated, down_rows, preferred_element_type=F32)
    ).astype(BF16)


def hidden_grads(grad_rows, down_rows, slope):
    grad_active = jnp.einsum("nd,df->nf", grad_rows, down_rows, preferred_element_type=F32)
    return (grad_active * slope.astype(F32)).astype(BF16)


def attended_grads(grad_rows, mix_rows):
    return jnp.einsum("nd,de->ne", grad_rows, mix_rows, preferred_element_type=F32).astype(BF16)


def back_rows(grads, weight_rows):
    return jnp.einsum("nf,df->nd", grads, weight_rows, preferred_element_type=F32)


def grad_half(rows, columns, part):
    width = rows.shape[1] // 2
    chosen = rows[:, part * width : (part + 1) * width]
    return jnp.einsum("nd,nf->df", chosen, columns, preferred_element_type=F32).astype(BF16)


def plus(*terms):
    return functools.reduce(lambda a, b: a + b, [t.astype(F32) for t in terms])


def width_sums(grad_first, grad_second, xhat, grad_local):
    return jnp.stack(
        [
            jnp.sum(grad_first * xhat, axis=0),
            jnp.sum(grad_second * xhat, axis=0),
            jnp.sum(grad_first, axis=0),
            jnp.sum(grad_second, axis=0),
            jnp.sum(grad_local.astype(F32), axis=0),
        ],
        axis=0,
    )


def shards(
    tokens,
    seq_start,
    proj_weight,
    proj_bias,
    out_weight,
    up_weight,
    up_bias,
    down_weight,
    norm_gains,
    biases,
    cotangent,
):
    local_rows, width = tokens.shape
    n_dp, n_tensor = lax.axis_size("dp"), lax.axis_size("tensor")
    dp_index, tensor_index = lax.axis_index("dp"), lax.axis_index("tensor")
    row_count = local_rows * n_tensor
    hidden_width = up_weight.shape[1]
    heads_here = proj_bias.shape[1]
    head_size = proj_bias.shape[2] * n_dp
    local_width = heads_here * head_size
    joined_width = 3 * local_width
    columns = norm_gains.shape[1]

    vectors = jnp.concatenate(
        [norm_gains.reshape(1, -1), biases.reshape(1, -1), proj_bias.reshape(1, -1), up_bias.reshape(1, -1)],
        axis=1,
    )
    table = jnp.zeros((n_dp * n_tensor, vectors.shape[1]), BF16)
    table = lax.dynamic_update_slice(table, vectors, (dp_index * n_tensor + tensor_index, 0))
    local_tokens, local_grads = to_frame(tokens), to_frame(cotangent)
    positions = dp_index * row_count + jnp.arange(row_count, dtype=jnp.int32) - seq_start
    tables = attention_tables(positions, seq_start)
    me = tensor_index.astype(jnp.int32).reshape(1)
    flat_proj = proj_weight.reshape(-1, joined_width)

    def small_parameters(table):
        six_rows = table[:, : 6 * columns].reshape(n_dp * n_tensor, 6, columns).transpose(1, 0, 2)
        six_rows = to_frame(six_rows.reshape(6, width).astype(F32))
        of_tensor = lax.dynamic_index_in_dim(
            table[:, 6 * columns :].reshape(n_dp, n_tensor, -1), tensor_index, 1, keepdims=False
        ).astype(F32)
        joined_bias = (
            of_tensor[:, : proj_bias.size]
            .reshape(n_dp, 3, heads_here, -1)
            .transpose(1, 2, 0, 3)
            .reshape(joined_width)
        )
        hidden_bias = of_tensor[:, proj_bias.size :].reshape(hidden_width)
        return six_rows[:2], six_rows[2:], joined_bias, hidden_bias

    def attend(first_rows, joined_rows, joined_bias):
        projected = jnp.dot(first_rows, joined_rows, preferred_element_type=F32) + joined_bias
        return attention_forward(projected, tables, me, heads_here, n_tensor)

    def attend_back(kept, grad_attended):
        queries, keys, values, log_total = kept
        backs = attention_backward(
            queries, keys, values, grad_attended, log_total, tables, me, heads_here, n_tensor
        )
        return jnp.concatenate(backs, axis=1)

    def finish_output(branches, shift_rows):
        output = local_tokens.astype(F32) + branches + shift_rows[2] + shift_rows[3]
        return from_frame(output.astype(BF16))

    def finish_input_grad(back):
        xhat_local, scale_local = standardize(local_tokens)
        grad_norm_in = (
            back
            - jnp.mean(back, axis=-1, keepdims=True)
            - xhat_local * jnp.mean(back * xhat_local, axis=-1, keepdims=True)
        ) * scale_local
        return from_frame(local_grads.astype(F32) + grad_norm_in)

    def small_shares(five, joined_bias_sums, up_bias_sums):
        five = five.reshape(5, width)
        mine = lax.dynamic_slice_in_dim(
            five, (dp_index * n_tensor + tensor_index) * columns, columns, 1
        )
        biases_grad = jnp.concatenate([mine[2:], mine[4:]], axis=0)
        joined_bias_sum = lax.dynamic_slice_in_dim(
            joined_bias_sums.reshape(3, heads_here, head_size),
            dp_index * proj_bias.shape[2],
            proj_bias.shape[2],
            2,
        )
        up_bias_sum = lax.dynamic_slice_in_dim(
            up_bias_sums.reshape(1, -1), dp_index * up_bias.shape[1], up_bias.shape[1], 1
        )
        return mine[:2], biases_grad, joined_bias_sum, up_bias_sum

    def small_grads(five, joined_bias_term, up_bias_term):
        five = from_frame(five).reshape(1, -1)
        terms = jnp.concatenate([five, joined_bias_term[None], up_bias_term[None]], axis=1)
        terms = butterfly(terms, "dp")
        five = butterfly(terms[:, : 5 * width], "tensor")
        return small_shares(
            five, terms[0, 5 * width : 5 * width + joined_width], terms[:, 5 * width + joined_width :]
        )

    def plain():
        token_rows, grad_rows = line_gather(local_tokens), line_gather(local_grads)
        up_rows, down_rows = dp_gather(up_weight), dp_gather(down_weight.T)
        joined_rows, mix_rows = dp_gather(flat_proj), dp_gather(out_weight.T)
        up_rows, down_rows, joined_rows, mix_rows = (
            join(w, 0, None) for w in (up_rows, down_rows, joined_rows, mix_rows)
        )
        gain_rows, shift_rows, joined_bias, hidden_bias = small_parameters(
            butterfly(butterfly(table, "dp"), "tensor")
        )
        first_rows, second_rows = norm_rows(token_rows, gain_rows, shift_rows)
        activated, slope = cut(*hidden_units(second_rows, up_rows, hidden_bias))
        *kept, attended, log_total = attend(first_rows, joined_rows, joined_bias)
        branches = line_scatter(branch_rows(attended, mix_rows, activated, down_rows))
        output = finish_output(branches, shift_rows)
        grad_hidden = hidden_grads(grad_rows, down_rows, slope)
        down_sum = weight_grad(grad_rows, activated)
        up_sum = weight_grad(second_rows, grad_hidden)
        grad_second = back_rows(grad_hidden, up_rows)
        grad_attended = attended_grads(grad_rows, mix_rows)
        mix_sum = weight_grad(grad_rows, attended)
        grad_projected = attend_back((*kept, log_total), grad_attended)
        joined_sum = weight_grad(first_rows, grad_projected)
        grad_first = back_rows(grad_projected, joined_rows)
        back = grad_first * gain_rows[0] + grad_second * gain_rows[1]
        input_grad = finish_input_grad(line_scatter(back.astype(BF16)))
        five = width_sums(grad_first, grad_second, standardize(token_rows)[0], local_grads)
        small = small_grads(
            five, jnp.sum(grad_projected, axis=0, dtype=F32), jnp.sum(grad_hidden, axis=0, dtype=F32)
        )
        return output, input_grad, joined_sum, mix_sum.T, up_sum, down_sum.T, small

    def staged():
        half = local_rows // 2
        first, second = slice(0, half), slice(half, 2 * half)

        def x(values):
            return xor_shift(values, "dp", 2)

        def y(values):
            return xor_shift(values, "dp", 4)

        def core(values):
            return xor_shift(values, "dp", 1)

        def gather_step(up, down, s):
            up = lax.ppermute(up, "tensor", [(i, i + 1) for i in range(s, 3)])
            down = lax.ppermute(down, "tensor", [(i + 1, i) for i in range(3 - s)])
            return up, down

        def scatter_terms(halves, up, down, s):
            came = () if s == 1 else (up, down)
            return step_terms(halves, 4 - s, s, local_rows, width // 2, *came)

        def scatter_step(to_up, to_down, s):
            up = lax.ppermute(to_up, "tensor", [(i, i + 1) for i in range(s)])
            down = lax.ppermute(to_down, "tensor", [(i, i - 1) for i in range(4 - s, 4)])
            return up, down

        def in_turn(block, ups, downs):
            blocks = [block] + [
                jnp.where(tensor_index + r < 4, downs[r - 1], ups[3 - r]) for r in range(1, 4)
            ]
            return jnp.concatenate(blocks, axis=0)

        def pair(top, low):
            return jnp.concatenate([top, low], axis=0)

        def place(base, piece, part):
            return lax.dynamic_update_slice(base, piece, ((4 * part + 2) * local_rows, 0))

        def at(keep, came, start, stop):
            return plus(keep[start * half : stop * half], came[start * half : stop * half])

        def joined_half(first_rows, grad_projected, grad_rows, attended, part):
            return jnp.concatenate(
                [grad_half(first_rows, grad_projected, part), grad_half(grad_rows, attended, part)], axis=1
            )

        wa = up_weight
        wb = jnp.concatenate([flat_proj, out_weight.T], axis=1)
        wc = down_weight.T

        ax, ay = x(wa), y(wa)
        tu1, td1 = gather_step(local_tokens, local_tokens, 0)
        table1 = table + core(table)
        table1, ax, ay = cut(table1, ax, ay)
        table1 = table1 + x(table1) + y(table1) + xor_shift(table1, "dp", 6)
        tu1, td1, ax, ay, table1, wb, wc, tables1 = cut(tu1, td1, ax, ay, table1, wb, wc, tables)
        tu2, td2 = gather_step(tu1, td1, 1)
        bx, by = x(wb), y(wb)
        table2 = table1 + xor_shift(table1, "tensor", 1)
        tu2, td2, bx, by, table2, local_grads1 = cut(tu2, td2, bx, by, table2, local_grads)
        tu3, td3 = gather_step(tu2, td2, 2)
        fa, fb = x(ay), y(bx)
        table3 = table2 + xor_shift(table2, "tensor", 2)
        both = lay(wa, ax, ay, wb, bx, by)
        tu3, td3, fa, fb, table3, both = cut(tu3, td3, fa, fb, table3, both)
        both_1 = place(place(both, fa, 0), fb, 1)
        both_1, wc, local_grads1 = cut(both_1, wc, local_grads1)
        cu1, cd1 = gather_step(local_grads1, local_grads1, 0)
        cx, cy = x(wc), y(wc)
        both_2 = core(both_1)
        gain_rows, shift_rows, joined_bias, hidden_bias = small_parameters(table3)
        token_rows = in_turn(local_tokens, (tu1, tu2, tu3), (td1, td2, td3))
        first_rows, second_rows = norm_rows(token_rows, gain_rows, shift_rows)
        mean = jnp.mean(token_rows.astype(F32), axis=-1, keepdims=True)
        _, scale = standardize(token_rows)
        mean, scale = (jnp.broadcast_to(v, (row_count, 128)) for v in (mean, scale))
        activated, slope = hidden_half(second_rows, both_1, both_2, hidden_bias)
        cu1, cd1, cx, cy, both_1, both_2, first_rows, activated, slope = cut(
            cu1, cd1, cx, cy, both_1, both_2, first_rows, activated, slope
        )
        cu2, cd2 = gather_step(cu1, cd1, 1)
        fc = x(cy)
        down_0 = lay(wc, cx, cy)
        *kept, attended, log_total = joined_forward(
            first_rows, both_1, both_2, joined_bias.reshape(1, -1), tables1, me, heads_here, head_size, n_tensor
        )
        cu2, cd2, fc, attended, down_0, mean, scale = cut(cu2, cd2, fc, attended, down_0, mean, scale)
        cu3, cd3 = gather_step(cu2, cd2, 2)
        down_1 = place(down_0, fc, 0)
        down_2 = core(down_1)
        branch_1 = branch_half(attended, both_1, activated, down_1)
        branch_2 = branch_half(attended, both_2, activated, down_2)
        cu3, cd3, branch_1, branch_2, activated = cut(cu3, cd3, branch_1, branch_2, activated)
        branches = ((branch_1, 0), (branch_2, 0))
        zu, zd, activated, cu3, cd3 = cut(*scatter_terms(branches, None, None, 1), activated, cu3, cd3)
        bu, bd = scatter_step(zu, zd, 1)
        grad_rows = in_turn(local_grads1, (cu1, cu2, cu3), (cd1, cd2, cd3))
        came_d = core(grad_half(grad_rows, activated, 1))
        keep_d = grad_half(grad_rows, activated, 0)
        grad_hidden, up_bias_term = hidden_back(grad_rows, down_1, down_2, slope)
        bu, bd, came_d, keep_d, grad_hidden, grad_rows = cut(
            bu, bd, came_d, keep_d, grad_hidden, grad_rows
        )
        zu, zd, sx, sy, second_rows, grad_hidden, grad_rows = cut(
            *scatter_terms(branches, bu, bd, 2),
            *pair_sums(keep_d, came_d, half),
            second_rows, grad_hidden, grad_rows,
        )
        bu, bd = scatter_step(zu, zd, 2)
        d1x, d1y = x(sx), y(sy)
        came_u = core(grad_half(second_rows, grad_hidden, 1))
        keep_u = grad_half(second_rows, grad_hidden, 0)
        grad_projected = mixed_backward(
            *kept, grad_rows, both_1, both_2, log_total, tables1, me, heads_here, n_tensor
        )
        bu, bd, d1x, d1y, came_u, keep_u, grad_projected, grad_hidden = cut(
            bu, bd, d1x, d1y, came_u, keep_u, grad_projected, grad_hidden
        )
        d2x = plus(at(keep_d, came_d, 2, 3), d1y[first]).astype(BF16)
        d2y = plus(at(keep_d, came_d, 7, 8), d1x[second]).astype(BF16)
        zu, zd, sx, sy, grad_hidden, grad_projected = cut(
            *scatter_terms(branches, bu, bd, 3),
            pair(d2x, at(keep_u, came_u, 4, 5).astype(BF16)),
            pair(d2y, at(keep_u, came_u, 5, 6).astype(BF16)),
            grad_hidden, grad_projected,
        )
        bu, bd = scatter_step(zu, zd, 3)
        s9x, s9y = x(sx), y(sy)
        came_j = core(joined_half(first_rows, grad_projected, grad_rows, attended, 1))
        back, sums = back_whole(
            grad_hidden, grad_projected, both_1, both_2, token_rows, mean, scale, gain_rows
        )
        bu, bd, s9x, s9y, came_j, back, sums, grad_projected, attended = cut(
            bu, bd, s9x, s9y, came_j, back, sums, grad_projected, attended
        )
        backs = ((back, 0), (back, 1))
        none = jnp.zeros((half, s9x.shape[1]), BF16)
        zu, zd, sx, sy, first_rows, grad_rows, bu, bd, sums = cut(
            *scatter_terms(backs, None, None, 1),
            plus(at(keep_u, came_u, 2, 4), pair(s9y[second], none)).astype(BF16),
            plus(at(keep_u, came_u, 6, 8), pair(none, s9x[second])).astype(BF16),
            first_rows, grad_rows, bu, bd, sums,
        )
        eu, ed = scatter_step(zu, zd, 1)
        s10x, s10y = x(sx), y(sy)
        keep_j = joined_half(first_rows, grad_projected, grad_rows, attended, 0)
        five = jnp.concatenate(
            [
                sums[:4],
                jnp.sum(local_grads.astype(F32), axis=0, keepdims=True),
            ],
            axis=0,
        )
        sx, sy = pair_sums(keep_j, came_j, half)
        five = five.reshape(1, -1)
        five = five + xor_shift(five, "tensor", 1)
        five = from_frame(five.reshape(5, width)).reshape(1, -1)
        eu, ed, s10x, s10y, keep_j, five, bu, bd, sx, sy = cut(
            eu, ed, s10x, s10y, keep_j, five, bu, bd, sx, sy
        )
        zu, zd, sx, sy, s10x, s10y, five = cut(
            *scatter_terms(backs, eu, ed, 2), sx, sy, s10x, s10y, five
        )
        eu, ed = scatter_step(zu, zd, 2)
        j1x, j1y = x(sx), y(sy)
        five = five + xor_shift(five, "tensor", 2)
        down_sum = own_sums(keep_d, came_d, half, (d1x, 0), (s9y, 0), (d1y, 1), (s9x, 0)).T
        up_sum = own_sums(keep_u, came_u, half, (s10x, 1), (s10y, 1), (s10x, 0), (s10y, 0))
        terms = jnp.concatenate(
            [
                jnp.sum(grad_projected, axis=0, dtype=F32, keepdims=True),
                up_bias_term,
            ],
            axis=1,
        )
        eu, ed, j1x, j1y, five, terms, down_sum, up_sum, bu, bd = cut(
            eu, ed, j1x, j1y, five, terms, down_sum, up_sum, bu, bd
        )
        zu, zd, sx, sy, five, bu, bd = cut(
            *scatter_terms(backs, eu, ed, 3),
            plus(at(keep_j, came_j, 2, 3), j1y[first]).astype(BF16),
            plus(at(keep_j, came_j, 7, 8), j1x[second]).astype(BF16),
            five, bu, bd,
        )
        eu, ed = scatter_step(zu, zd, 3)
        j2x, j2y = x(sx), y(sy)
        own = jnp.concatenate([branch_1[:local_rows], branch_2[:local_rows]], axis=1)
        output = finish_output(plus(own, bu, bd), shift_rows)
        terms = jnp.concatenate([five, terms], axis=1)
        terms = terms + core(terms)
        terms = terms + x(terms)
        terms, j2x, j2y = cut(terms, j2x, j2y)
        terms = terms + y(terms)
        small = small_shares(
            terms[:, : 5 * width], terms[0, 5 * width : 5 * width + joined_width],
            terms[:, 5 * width + joined_width :],
        )
        joined_mix = own_sums(keep_j, came_j, half, (j1x, 0), (j2y, 0), (j1y, 1), (j2x, 0))
        joined_sum = joined_mix[:, :joined_width].reshape(proj_weight.shape)
        eu, ed, joined_sum, mix_sum = cut(eu, ed, joined_sum, joined_mix[:, joined_width:].T)
        input_grad = input_grad_rows(back, eu, ed, local_tokens, local_grads)
        return output, input_grad, joined_sum, mix_sum, up_sum, down_sum, small

    parts = staged() if fast_dp() and n_tensor == 4 else plain()
    output, input_grad, joined_sum, mix_sum, up_sum, down_sum, small = parts
    gains_grad, biases_grad, joined_bias_sum, up_bias_sum = small
    return (
        output,
        input_grad,
        joined_sum.reshape(proj_weight.shape),
        joined_bias_sum,
        mix_sum,
        up_sum,
        up_bias_sum,
        down_sum,
        gains_grad,
        biases_grad,
    )


def solution(mesh):
    in_specs = (
        P(("dp", "tensor"), None),
        P("dp"),
        P("dp", None, "tensor"),
        P(None, "tensor", "dp"),
        P("tensor", "dp"),
        P("dp", "tensor"),
        P("tensor", "dp"),
        P("tensor", "dp"),
        P(None, ("dp", "tensor")),
        P(None, ("dp", "tensor")),
        P(("dp", "tensor"), None),
    )
    out_specs = (
        P(("dp", "tensor"), None),
        P(("dp", "tensor"), None),
        P("dp", None, "tensor"),
        P(None, "tensor", "dp"),
        P("tensor", "dp"),
        P("dp", "tensor"),
        P("tensor", "dp"),
        P("tensor", "dp"),
        P(None, ("dp", "tensor")),
        P(None, ("dp", "tensor")),
    )
    return jax.shard_map(shards, mesh=mesh, in_specs=in_specs, out_specs=out_specs, check_vma=False)
```

```python
import functools

import jax
import jax.numpy as jnp
from jax import lax
from jax.experimental import pallas as pl
from jax.experimental.pallas import tpu as pltpu
from jax.sharding import PartitionSpec as P

ROT = 64
EPSILON = 1e-05
ROTARY_BASE = 10000.0
F32 = jnp.float32
BF16 = jnp.bfloat16
HALVES = [(0, 0), (0, 1), (2, 1), (2, 0), (6, 0), (6, 1), (4, 1), (4, 0)]
ORDER = HALVES + [(p ^ 1, h) for p, h in HALVES]


SMALL = pl.CostEstimate(flops=1000, bytes_accessed=1000, transcendentals=0)


def cut(*values):
    return lax.optimization_barrier(values)


def is_power(n):
    return n & (n - 1) == 0


def fast_dp():
    return lax.axis_size("dp") == 8


def xor_shift(values, axis, bit):
    size = lax.axis_size(axis)
    return lax.ppermute(values, axis, [(i, i ^ bit) for i in range(size)])


def butterfly(values, axis):
    size = lax.axis_size(axis)
    if not is_power(size):
        return lax.psum(values, axis)
    bit = 1
    while bit < size:
        values = values + xor_shift(values, axis, bit)
        bit *= 2
    return values


def columns_kernel(index_ref, x_ref, o_ref, *, count, step):
    for j in range(count):
        at = pl.multiple_of(index_ref[j] * step, step)
        o_ref[:, j * step : (j + 1) * step] = x_ref[:, pl.ds(at, step)]


def take_columns(values, index):
    rows, width = values.shape
    count = index.shape[0]
    tile = rows // 2 if rows % 64 == 0 else rows
    return pl.pallas_call(
        functools.partial(columns_kernel, count=count, step=width // count),
        out_shape=jax.ShapeDtypeStruct(values.shape, values.dtype),
        grid_spec=pltpu.PrefetchScalarGridSpec(
            num_scalar_prefetch=1,
            grid=(rows // tile,),
            in_specs=[pl.BlockSpec((tile, width), lambda i, s: (i, 0))],
            out_specs=pl.BlockSpec((tile, width), lambda i, s: (i, 0)),
        ),
        cost_estimate=SMALL,
        name="columns",
    )(index, values)


FRAME = [[(me ^ p) * 2 + h for p, h in ORDER] for me in range(8)]
PLAIN = [[row.index(k) for k in range(16)] for row in FRAME]


def frame_index():
    return lax.dynamic_index_in_dim(jnp.array(FRAME, jnp.int32), lax.axis_index("dp"), 0, keepdims=False)


def plain_index():
    return lax.dynamic_index_in_dim(jnp.array(PLAIN, jnp.int32), lax.axis_index("dp"), 0, keepdims=False)


def to_frame(values):
    return take_columns(values, frame_index()) if fast_dp() else values


def from_frame(values):
    return take_columns(values, plain_index()) if fast_dp() else values


def dp_gather(shard):
    if not fast_dp():
        return [lax.all_gather(shard, "dp", axis=0, tiled=True)]
    half = shard.shape[0] // 2
    from_x = xor_shift(shard, "dp", 2)
    from_y = xor_shift(shard, "dp", 4)
    far_1 = xor_shift(from_y[:half], "dp", 2)
    far_2 = xor_shift(from_x[half:], "dp", 4)
    far = jnp.concatenate([far_1, far_2], axis=0)
    near = xor_shift(shard, "dp", 1)
    near_x = xor_shift(from_x, "dp", 1)
    near_y = xor_shift(from_y, "dp", 1)
    near_far = xor_shift(far, "dp", 1)
    out = []
    for own, x, f, y in ((shard, from_x, far, from_y), (near, near_x, near_far, near_y)):
        out += [own, x[half:], x[:half], f, y[half:], y[:half]]
    return out


def join(pieces, start, stop):
    return jnp.concatenate([p[:, start:stop] for p in pieces], axis=0)


def dp_scatter(make):
    away = make(1)
    came = xor_shift(away, "dp", 1)
    kept = make(0)
    rows = kept.shape[0] // 4
    half = rows // 2

    def summed(start, stop):
        return kept[start:stop].astype(F32) + came[start:stop].astype(F32)

    first_x = xor_shift(summed(rows + half, 2 * rows + half).astype(BF16), "dp", 2)
    first_y = xor_shift(summed(2 * rows + half, 3 * rows + half).astype(BF16), "dp", 4)
    last_x = summed(rows, rows + half) + first_y[:half].astype(F32)
    last_y = summed(3 * rows + half, 4 * rows) + first_x[half:].astype(F32)
    last_x = xor_shift(last_x.astype(BF16), "dp", 2)
    last_y = xor_shift(last_y.astype(BF16), "dp", 4)
    top = summed(0, half) + first_x[:half].astype(F32) + last_y.astype(F32)
    low = summed(half, rows) + first_y[half:].astype(F32) + last_x.astype(F32)
    return jnp.concatenate([top, low], axis=0)


def weight_grad(rows, columns):
    def make(part):
        width = rows.shape[1] // 2
        chosen = rows[:, part * width : (part + 1) * width]
        return jnp.einsum("nd,nf->df", chosen, columns, preferred_element_type=F32).astype(BF16)

    if fast_dp():
        return dp_scatter(make)
    whole = jnp.einsum("nd,nf->df", rows, columns, preferred_element_type=F32).astype(BF16)
    return lax.psum_scatter(whole, "dp", scatter_dimension=0, tiled=True).astype(F32)


def line_gather(block):
    size = lax.axis_size("tensor")
    me = lax.axis_index("tensor")
    up = down = block
    ups, downs = [block], [block]
    for s in range(size - 1):
        up = lax.ppermute(up, "tensor", [(i, i + 1) for i in range(s, size - 1)])
        down = lax.ppermute(down, "tensor", [(i + 1, i) for i in range(size - 1 - s)])
        ups.append(up)
        downs.append(down)
    blocks = [block]
    for r in range(1, size):
        blocks.append(jnp.where(me + r < size, downs[r], ups[size - r]))
    return jnp.concatenate(blocks, axis=0)


def line_scatter(terms):
    size = lax.axis_size("tensor")
    rows = terms.shape[0] // size

    def block(r):
        return terms[r * rows : (r + 1) * rows]

    up = down = None
    for s in range(1, size):
        to_up, to_down = block(size - s), block(s)
        if s > 1:
            to_up = (to_up.astype(F32) + up.astype(F32)).astype(BF16)
            to_down = (to_down.astype(F32) + down.astype(F32)).astype(BF16)
        up = lax.ppermute(to_up, "tensor", [(i, i + 1) for i in range(s)])
        down = lax.ppermute(to_down, "tensor", [(i, i - 1) for i in range(size - s, size)])
    return block(0).astype(F32) + up.astype(F32) + down.astype(F32)


def turn(values, cosine, low_sine, high_sine, sign):
    half = ROT // 2
    lanes = cosine.shape[-1]
    head = values[:, :lanes]
    turned = (
        head * cosine
        - sign * pltpu.roll(head, lanes - half, 1) * low_sine
        + sign * pltpu.roll(head, half, 1) * high_sine
    )
    return jnp.concatenate([turned, values[:, lanes:]], axis=1)


def contract(a, b, dims):
    return lax.dot_general(a, b, (dims, ((), ())), preferred_element_type=F32)


def masked(scores, column_starts, row_starts, query_block, block):
    keys = scores.shape[1]
    query = lax.broadcasted_iota(jnp.int32, scores.shape, 0) + query_block * block
    key = lax.broadcasted_iota(jnp.int32, scores.shape, 1)
    allowed = (column_starts == row_starts[:, :keys]) & (key <= query)
    return allowed, jnp.where(allowed, scores, -1e30)


def spots(me_ref, size, block):
    def spot(b):
        return pl.ds(pl.multiple_of(lax.rem(b - me_ref[0] + size, size) * block, block), block)

    return spot


def forward_block(q_out, k_out, v_out, att_ref, log_ref, col_ref, row_ref, spot, b, block):
    scale = q_out.shape[-1] ** (-0.5)
    here = slice(b * block, (b + 1) * block)
    query = q_out[spot(b), :]
    scores = jnp.concatenate(
        [contract(query, k_out[spot(c), :], ((1,), (1,))) for c in range(b + 1)], axis=1
    ) * scale
    _, scores = masked(scores, col_ref[here, :1], row_ref[:1, :], b, block)
    top = jnp.max(scores, axis=1, keepdims=True)
    powers = jnp.exp(scores - top)
    total = jnp.sum(powers, axis=1, keepdims=True)
    weights = (powers / total).astype(BF16)
    attended = contract(weights[:, :block], v_out[spot(0), :], ((1,), (0,)))
    for c in range(1, b + 1):
        attended = attended + contract(
            weights[:, c * block : (c + 1) * block], v_out[spot(c), :], ((1,), (0,))
        )
    att_ref[spot(b), :] = attended.astype(BF16)
    log_ref[0, here, :] = jnp.broadcast_to(top + jnp.log(total), (block, log_ref.shape[2]))


def forward_kernel(
    me_ref, q_ref, k_ref, v_ref, cos_ref, low_ref, high_ref, col_ref, row_ref,
    q_out, k_out, v_out, att_ref, log_ref, *, size, block,
):
    spot = spots(me_ref, size, block)
    for b in range(size):
        here = slice(b * block, (b + 1) * block)
        at = spot(b)
        tables = cos_ref[here, :], low_ref[here, :], high_ref[here, :]
        q_out[at, :] = turn(q_ref[at, :], *tables, 1.0).astype(BF16)
        k_out[at, :] = turn(k_ref[at, :], *tables, 1.0).astype(BF16)
        v_out[at, :] = v_ref[at, :].astype(BF16)
    for b in range(size):
        forward_block(q_out, k_out, v_out, att_ref, log_ref, col_ref, row_ref, spot, b, block)


def joined_forward_kernel(
    me_ref, rows_ref, qa_ref, ka_ref, va_ref, qb_ref, kb_ref, vb_ref, q_bias, k_bias, v_bias,
    cos_ref, low_ref, high_ref, col_ref, row_ref,
    q_out, k_out, v_out, att_ref, log_ref, *, size, block,
):
    spot = spots(me_ref, size, block)
    middle = qa_ref.shape[0]
    for b in range(size):
        here = slice(b * block, (b + 1) * block)
        at = spot(b)
        tables = cos_ref[here, :], low_ref[here, :], high_ref[here, :]
        top, low = rows_ref[at, :middle], rows_ref[at, middle:]

        def project(one, two, bias):
            return contract(top, one[:, :], ((1,), (0,))) + contract(low, two[:, :], ((1,), (0,))) + bias[:, :]

        q_out[at, :] = turn(project(qa_ref, qb_ref, q_bias), *tables, 1.0).astype(BF16)
        k_out[at, :] = turn(project(ka_ref, kb_ref, k_bias), *tables, 1.0).astype(BF16)
        v_out[at, :] = project(va_ref, vb_ref, v_bias).astype(BF16)
        forward_block(q_out, k_out, v_out, att_ref, log_ref, col_ref, row_ref, spot, b, block)


def backward_pass(
    q_ref, k_ref, v_ref, g_ref, log_ref, cos_ref, low_ref, high_ref, col_ref, row_ref,
    put, k_acc, v_acc, spot, size, block,
):
    scale = q_ref.shape[-1] ** (-0.5)
    for b in range(size):
        here = slice(b * block, (b + 1) * block)
        query, grad = q_ref[spot(b), :], g_ref[spot(b), :]
        scores = jnp.concatenate(
            [contract(query, k_ref[spot(c), :], ((1,), (1,))) for c in range(b + 1)], axis=1
        ) * scale
        allowed, scores = masked(scores, col_ref[here, :1], row_ref[:1, :], b, block)
        probs = jnp.where(allowed, jnp.exp(scores - log_ref[0, here, :1]), 0.0)
        grad_probs = jnp.concatenate(
            [contract(grad, v_ref[spot(c), :], ((1,), (1,))) for c in range(b + 1)], axis=1
        )
        inner = jnp.sum(probs * grad_probs, axis=1, keepdims=True)
        weights = probs.astype(BF16)
        grad_scores = (probs * (grad_probs - inner)).astype(BF16)
        back = None
        for c in range(b + 1):
            part = slice(c * block, (c + 1) * block)
            key_term = contract(grad_scores[:, part], query, ((0,), (0,)))
            value_term = contract(weights[:, part], grad, ((0,), (0,)))
            query_term = contract(grad_scores[:, part], k_ref[spot(c), :], ((1,), (0,)))
            back = query_term if c == 0 else back + query_term
            if c == b:
                k_acc[part, :] = key_term
                v_acc[part, :] = value_term
            else:
                k_acc[part, :] += key_term
                v_acc[part, :] += value_term
        tables = cos_ref[here, :], low_ref[here, :], high_ref[here, :]
        put(0, spot(b), turn(back * scale, *tables, -1.0).astype(BF16))
    for b in range(size):
        here = slice(b * block, (b + 1) * block)
        tables = cos_ref[here, :], low_ref[here, :], high_ref[here, :]
        put(1, spot(b), turn(k_acc[here, :] * scale, *tables, -1.0).astype(BF16))
        put(2, spot(b), v_acc[here, :].astype(BF16))


def backward_kernel(
    me_ref, q_ref, k_ref, v_ref, g_ref, log_ref, cos_ref, low_ref, high_ref, col_ref, row_ref,
    dq_ref, dk_ref, dv_ref, k_acc, v_acc, *, size, block,
):
    outs = (dq_ref, dk_ref, dv_ref)

    def put(k, at, value):
        outs[k][at, :] = value

    backward_pass(
        q_ref, k_ref, v_ref, g_ref, log_ref, cos_ref, low_ref, high_ref, col_ref, row_ref,
        put, k_acc, v_acc, spots(me_ref, size, block), size, block,
    )


def mixed_backward_kernel(
    me_ref, q_ref, k_ref, v_ref, g_ref, a_ref, b_ref, log_ref, cos_ref, low_ref, high_ref, col_ref, row_ref,
    d_ref, k_acc, v_acc, g_acc, *, size, block, heads,
):
    middle = a_ref.shape[0]
    head = q_ref.shape[1]
    for b in range(size):
        here = slice(b * block, (b + 1) * block)
        g_acc[here, :] = (
            contract(g_ref[here, :middle], a_ref[:, :], ((1,), (0,)))
            + contract(g_ref[here, middle:], b_ref[:, :], ((1,), (0,)))
        ).astype(BF16)
    h = pl.program_id(0)

    def put(k, at, value):
        d_ref[at, pl.ds(pl.multiple_of((k * heads + h) * head, head), head)] = value

    backward_pass(
        q_ref, k_ref, v_ref, g_acc, log_ref, cos_ref, low_ref, high_ref, col_ref, row_ref,
        put, k_acc, v_acc, spots(me_ref, size, block), size, block,
    )


def hidden_kernel(rows_ref, a_ref, b_ref, bias_ref, act_ref, slope_ref, *, step):
    middle = a_ref.shape[0]
    for i in range(rows_ref.shape[0] // step):
        here = slice(i * step, (i + 1) * step)
        hidden = contract(rows_ref[here, :middle], a_ref[:, :], ((1,), (0,)))
        hidden = hidden + contract(rows_ref[here, middle:], b_ref[:, :], ((1,), (0,))) + bias_ref[:, :]
        bell = lax.erf(hidden * (0.5**0.5))
        act_ref[here, :] = (0.5 * hidden * (1.0 + bell)).astype(BF16)
        slope = 0.5 * (1.0 + bell) + hidden * jnp.exp(-0.5 * hidden * hidden) * 0.3989422804014327
        slope_ref[here, :] = slope.astype(BF16)


def hidden_half(rows, top, low, bias):
    count, width = rows.shape
    out = top.shape[1]
    tile = 512
    half = pl.BlockSpec((width // 2, tile), lambda j: (0, j))
    made = pl.BlockSpec((count, tile), lambda j: (0, j))
    return pl.pallas_call(
        functools.partial(hidden_kernel, step=512),
        out_shape=(jax.ShapeDtypeStruct((count, out), BF16),) * 2,
        grid=(out // tile,),
        in_specs=[
            pl.BlockSpec((count, width), lambda j: (0, 0)), half, half, pl.BlockSpec((1, tile), lambda j: (0, j))
        ],
        out_specs=(made, made),
        cost_estimate=SMALL,
        name="hidden",
    )(rows, top, low, bias.reshape(1, -1))


def slope_kernel(rows_ref, a_ref, b_ref, slope_ref, out_ref, sum_ref, *, step):
    middle = a_ref.shape[0]
    total = 0.0
    for i in range(rows_ref.shape[0] // step):
        here = slice(i * step, (i + 1) * step)
        active = contract(rows_ref[here, :middle], a_ref[:, :], ((1,), (0,)))
        active = active + contract(rows_ref[here, middle:], b_ref[:, :], ((1,), (0,)))
        made = (active * slope_ref[here, :].astype(F32)).astype(BF16)
        out_ref[here, :] = made
        total = total + jnp.sum(made.astype(F32), axis=0, keepdims=True)
    sum_ref[:, :] = total


def hidden_back(rows, top, low, slope):
    count, width = rows.shape
    out = top.shape[1]
    tile = 512
    half = pl.BlockSpec((top.shape[0], tile), lambda j: (0, j))
    made = pl.BlockSpec((count, tile), lambda j: (0, j))
    return pl.pallas_call(
        functools.partial(slope_kernel, step=512),
        out_shape=(jax.ShapeDtypeStruct((count, out), BF16), jax.ShapeDtypeStruct((1, out), F32)),
        grid=(out // tile,),
        in_specs=[pl.BlockSpec((count, width), lambda j: (0, 0)), half, half, made],
        out_specs=(made, pl.BlockSpec((1, tile), lambda j: (0, j))),
        cost_estimate=SMALL,
        name="hidden_back",
    )(rows, top, low, slope)


def branch_kernel(att_ref, mix_ref, act_ref, down_ref, out_ref, *, step):
    for i in range(att_ref.shape[0] // step):
        here = slice(i * step, (i + 1) * step)
        total = contract(att_ref[here, :], mix_ref[:, :], ((1,), (1,)))
        total = total + contract(act_ref[here, :], down_ref[:, :], ((1,), (1,)))
        out_ref[here, :] = total.astype(BF16)


def branch_half(attended, mixed, activated, down):
    count, inner = attended.shape
    units = activated.shape[1]
    width = down.shape[0]
    tile = 256
    spot = mixed.shape[1] // inner - 1
    return pl.pallas_call(
        functools.partial(branch_kernel, step=512),
        out_shape=jax.ShapeDtypeStruct((count, width), BF16),
        grid=(width // tile,),
        in_specs=[
            pl.BlockSpec((count, inner), lambda j: (0, 0)),
            pl.BlockSpec((tile, inner), lambda j: (j + width // tile, spot)),
            pl.BlockSpec((count, units), lambda j: (0, 0)),
            pl.BlockSpec((tile, units), lambda j: (j, 0)),
        ],
        out_specs=pl.BlockSpec((count, tile), lambda j: (0, j)),
        cost_estimate=SMALL,
        name="branches",
    )(attended, mixed, activated, down)


def back_kernel(
    hid_ref, proj_ref, up_1, up_2, join_1, join_2, tok_ref, mean_ref, scale_ref, gain_ref, back_ref, sum_ref,
    *, step, tiles,
):
    def work(up_ref, join_ref):
        sums = [0.0] * 4
        for i in range(hid_ref.shape[0] // step):
            here = slice(i * step, (i + 1) * step)
            two = contract(hid_ref[here, :], up_ref[:, :], ((1,), (1,)))
            one = contract(proj_ref[here, :], join_ref[:, :], ((1,), (1,)))
            back_ref[here, :] = (one * gain_ref[:1, :] + two * gain_ref[1:2, :]).astype(BF16)
            xhat = (tok_ref[here, :].astype(F32) - mean_ref[here, :1]) * scale_ref[here, :1]
            for k, term in enumerate((one * xhat, two * xhat, one, two)):
                sums[k] = sums[k] + jnp.sum(term, axis=0, keepdims=True)
        for k in range(4):
            sum_ref[k : k + 1, :] = sums[k]

    @pl.when(pl.program_id(0) < tiles)
    def _():
        work(up_1, join_1)

    @pl.when(pl.program_id(0) >= tiles)
    def _():
        work(up_2, join_2)


def back_whole(grad_hidden, grad_projected, both_1, both_2, token_rows, mean, scale, gains):
    count, units = grad_hidden.shape
    joined = grad_projected.shape[1]
    width = both_1.shape[0] // 2
    tile = 256
    tiles = width // tile
    whole = lambda j: (0, 0)

    def of(columns, block):
        low = pl.BlockSpec((tile, columns), lambda j: (block + jnp.minimum(j, tiles - 1), 0))
        high = pl.BlockSpec((tile, columns), lambda j: (block + jnp.maximum(j - tiles, 0), 0))
        return [low, high]

    return pl.pallas_call(
        functools.partial(back_kernel, step=512, tiles=tiles),
        out_shape=(jax.ShapeDtypeStruct((count, 2 * width), BF16), jax.ShapeDtypeStruct((8, 2 * width), F32)),
        grid=(2 * tiles,),
        in_specs=[pl.BlockSpec((count, units), whole), pl.BlockSpec((count, joined), whole)]
        + of(units, 0) + of(joined, tiles)
        + [
            pl.BlockSpec((count, tile), lambda j: (0, j)),
            pl.BlockSpec((count, 128), whole),
            pl.BlockSpec((count, 128), whole),
            pl.BlockSpec((2, tile), lambda j: (0, j)),
        ],
        out_specs=(pl.BlockSpec((count, tile), lambda j: (0, j)), pl.BlockSpec((8, tile), lambda j: (0, j))),
        cost_estimate=SMALL,
        name="back",
    )(grad_hidden, grad_projected, both_1, both_2, both_1, both_2, token_rows, mean, scale, gains)


def lay_kernel(*refs):
    *ins, out_ref = refs
    rows = ins[0].shape[0]
    half = rows // 2
    for w in range(len(ins) // 3):
        own, from_x, from_y = ins[3 * w : 3 * w + 3]
        base = 4 * w * rows
        out_ref[base : base + rows, :] = own[:, :]
        out_ref[base + 2 * rows : base + 3 * rows, :] = jnp.zeros(own.shape, BF16)
        for piece, at in ((from_x, base + rows), (from_y, base + 3 * rows)):
            out_ref[at : at + half, :] = piece[half:, :]
            out_ref[at + half : at + rows, :] = piece[:half, :]


def lay(*pieces):
    rows, width = pieces[0].shape
    weights = len(pieces) // 3
    tile = width // 4
    return pl.pallas_call(
        lay_kernel,
        out_shape=jax.ShapeDtypeStruct((4 * rows * weights, width), BF16),
        grid=(4,),
        in_specs=[pl.BlockSpec((rows, tile), lambda j: (0, j))] * len(pieces),
        out_specs=pl.BlockSpec((4 * rows * weights, tile), lambda j: (0, j)),
        cost_estimate=SMALL,
        name="lay",
    )(*pieces)


def pair_sums_kernel(kept_x, came_x, kept_y, came_y, to_x, to_y):
    to_x[:, :] = (kept_x[:, :].astype(F32) + came_x[:, :].astype(F32)).astype(BF16)
    to_y[:, :] = (kept_y[:, :].astype(F32) + came_y[:, :].astype(F32)).astype(BF16)


def pair_sums(kept, came, half):
    width = kept.shape[1]
    of_x = pl.BlockSpec((half, width), lambda i: (3 + i, 0))
    of_y = pl.BlockSpec((half, width), lambda i: (5 + i, 0))
    out = pl.BlockSpec((half, width), lambda i: (i, 0))
    return pl.pallas_call(
        pair_sums_kernel,
        out_shape=(jax.ShapeDtypeStruct((2 * half, width), BF16),) * 2,
        grid=(2,),
        in_specs=[of_x, of_x, of_y, of_y],
        out_specs=(out, out),
        cost_estimate=SMALL,
        name="pair_sums",
    )(kept, came, kept, came)


def own_sums_kernel(kept, came, a, b, c, d, out):
    half = a.shape[0]
    top, low = slice(0, half), slice(half, 2 * half)
    for part, one, two in ((top, a, b), (low, c, d)):
        total = kept[part, :].astype(F32) + came[part, :].astype(F32)
        out[part, :] = total + one[:, :].astype(F32) + two[:, :].astype(F32)


def own_sums(kept, came, half, *came_in):
    width = kept.shape[1]
    tile = width // 4
    rows = pl.BlockSpec((2 * half, tile), lambda j: (0, j))
    return pl.pallas_call(
        own_sums_kernel,
        out_shape=jax.ShapeDtypeStruct((2 * half, width), F32),
        grid=(4,),
        in_specs=[rows, rows] + [pl.BlockSpec((half, tile), lambda j, k=k: (k, j)) for _, k in came_in],
        out_specs=rows,
        cost_estimate=SMALL,
        name="own_sums",
    )(kept, came, *(v for v, _ in came_in))


def terms_kernel(*refs):
    *ins, to_up, to_down = refs
    up = jnp.concatenate([ins[0][:, :], ins[1][:, :]], axis=1)
    down = jnp.concatenate([ins[2][:, :], ins[3][:, :]], axis=1)
    if len(ins) > 4:
        up = (up.astype(F32) + ins[4][:, :].astype(F32)).astype(BF16)
        down = (down.astype(F32) + ins[5][:, :].astype(F32)).astype(BF16)
    to_up[:, :] = up
    to_down[:, :] = down


def step_terms(halves, up_block, down_block, rows, width, *came):
    tiles = 2
    tile = rows // tiles

    def of(block):
        return [pl.BlockSpec((tile, width), lambda i, k=k: (block * tiles + i, k)) for _, k in halves]

    full = pl.BlockSpec((tile, 2 * width), lambda i: (i, 0))
    arrays = [v for v, _ in halves]
    return pl.pallas_call(
        terms_kernel,
        out_shape=(jax.ShapeDtypeStruct((rows, 2 * width), BF16),) * 2,
        grid=(tiles,),
        in_specs=of(up_block) + of(down_block) + [full] * len(came),
        out_specs=(full, full),
        cost_estimate=SMALL,
        name="terms",
    )(*arrays, *arrays, *came)


def input_grad_kernel(index_ref, own_ref, up_ref, down_ref, tok_ref, grad_ref, out_ref):
    back = own_ref[:, :].astype(F32) + up_ref[:, :].astype(F32) + down_ref[:, :].astype(F32)
    xhat, scale = standardize(tok_ref[:, :])
    back = back - jnp.mean(back, axis=-1, keepdims=True) - xhat * jnp.mean(back * xhat, axis=-1, keepdims=True)
    total = grad_ref[:, :].astype(F32) + back * scale
    count = index_ref.shape[0]
    step = total.shape[1] // count
    for j in range(count):
        out_ref[:, pl.ds(pl.multiple_of(index_ref[j] * step, step), step)] = total[:, j * step : (j + 1) * step]


def input_grad_rows(own, up, down, tokens, grads):
    rows, width = tokens.shape
    tile = rows // 4
    full = pl.BlockSpec((tile, width), lambda i, s: (i, 0))
    return pl.pallas_call(
        input_grad_kernel,
        out_shape=jax.ShapeDtypeStruct((rows, width), F32),
        grid_spec=pltpu.PrefetchScalarGridSpec(
            num_scalar_prefetch=1,
            grid=(rows // tile,),
            in_specs=[full] * 5,
            out_specs=full,
        ),
        cost_estimate=SMALL,
        name="input_grad",
    )(frame_index(), own, up, down, tokens, grads)


def joined_forward(rows, top, low, bias, tables, me, heads, head, size):
    count, width = rows.shape
    block = count // size
    whole = lambda h, s: (0, 0)
    table_specs = [pl.BlockSpec((count, 128), whole)] * 4 + [pl.BlockSpec((8, count), whole)]
    by_head = pl.BlockSpec((count, head), lambda h, s: (0, h))
    wide = jax.ShapeDtypeStruct((count, heads * head), BF16)

    def thirds(n, spot):
        return [pl.BlockSpec((n, head), lambda h, s, k=k: (spot, k * heads + h)) for k in range(3)]

    return pl.pallas_call(
        functools.partial(joined_forward_kernel, size=size, block=block),
        out_shape=(wide, wide, wide, wide, jax.ShapeDtypeStruct((heads, count, 128), F32)),
        grid_spec=pltpu.PrefetchScalarGridSpec(
            num_scalar_prefetch=1,
            grid=(heads,),
            in_specs=[pl.BlockSpec((count, width), whole)]
            + thirds(width // 2, 1) + thirds(width // 2, 1) + thirds(1, 0) + table_specs,
            out_specs=(by_head,) * 4 + (pl.BlockSpec((1, count, 128), lambda h, s: (h, 0, 0)),),
        ),
        cost_estimate=SMALL,
        name="joined_forward",
    )(me, rows, top, top, top, low, low, low, bias, bias, bias, *tables)


def mixed_backward(queries, keys, values, grads, top, low, log_total, tables, me, heads, size):
    count = queries.shape[0]
    head = queries.shape[1] // heads
    block = count // size
    whole = lambda h, s: (0, 0)
    table_specs = [pl.BlockSpec((count, 128), whole)] * 4 + [pl.BlockSpec((8, count), whole)]
    by_head = pl.BlockSpec((count, head), lambda h, s: (0, h))
    mix = pl.BlockSpec((grads.shape[1] // 2, head), lambda h, s: (1, 3 * heads + h))
    return pl.pallas_call(
        functools.partial(mixed_backward_kernel, size=size, block=block, heads=heads),
        out_shape=jax.ShapeDtypeStruct((count, 3 * heads * head), BF16),
        grid_spec=pltpu.PrefetchScalarGridSpec(
            num_scalar_prefetch=1,
            grid=(heads,),
            in_specs=[by_head] * 3
            + [pl.BlockSpec((count, grads.shape[1]), whole), mix, mix]
            + [pl.BlockSpec((1, count, 128), lambda h, s: (h, 0, 0))]
            + table_specs,
            out_specs=pl.BlockSpec((count, 3 * heads * head), whole),
            scratch_shapes=[pltpu.VMEM((count, head), F32)] * 2 + [pltpu.VMEM((count, head), BF16)],
        ),
        cost_estimate=SMALL,
        name="mixed_backward",
    )(me, queries, keys, values, grads, top, low, log_total, *tables)


def attention_tables(positions, starts):
    half = ROT // 2
    frequency = ROTARY_BASE ** (-(jnp.arange(half, dtype=F32) * 2.0) / ROT)
    angles = positions.astype(F32)[:, None] * frequency[None, :]
    cosine, sine = jnp.cos(angles), jnp.sin(angles)
    rows = positions.shape[0]
    cosines = jnp.concatenate([cosine, cosine, jnp.ones((rows, 128 - ROT), F32)], axis=1)
    low = jnp.concatenate([sine, jnp.zeros((rows, 128 - half), F32)], axis=1)
    high = jnp.concatenate([jnp.zeros((rows, half), F32), sine, jnp.zeros((rows, 128 - ROT), F32)], axis=1)
    columns = jnp.broadcast_to(starts[:, None], (rows, 128))
    across = jnp.broadcast_to(starts[None, :], (8, rows))
    return cosines, low, high, columns, across


def attention_forward(projected, tables, me, heads, size):
    rows = projected.shape[0]
    head = projected.shape[1] // (3 * heads)
    block = rows // size
    whole = lambda h, s: (0, 0)
    table_specs = [pl.BlockSpec((rows, 128), whole)] * 4 + [pl.BlockSpec((8, rows), whole)]
    by_head = pl.BlockSpec((rows, head), lambda h, s: (0, h))
    wide = jax.ShapeDtypeStruct((rows, heads * head), BF16)
    return pl.pallas_call(
        functools.partial(forward_kernel, size=size, block=block),
        out_shape=(wide, wide, wide, wide, jax.ShapeDtypeStruct((heads, rows, 128), F32)),
        grid_spec=pltpu.PrefetchScalarGridSpec(
            num_scalar_prefetch=1,
            grid=(heads,),
            in_specs=[
                pl.BlockSpec((rows, head), lambda h, s, k=k: (0, k * heads + h)) for k in range(3)
            ]
            + table_specs,
            out_specs=(by_head,) * 4 + (pl.BlockSpec((1, rows, 128), lambda h, s: (h, 0, 0)),),
        ),
        cost_estimate=pl.CostEstimate(
            flops=heads * rows * rows * head * 40, bytes_accessed=rows * head * heads * 24,
            transcendentals=heads * rows * rows // 2,
        ),
        name="attention_forward",
    )(me, projected, projected, projected, *tables)


def attention_backward(queries, keys, values, grads, log_total, tables, me, heads, size):
    rows = queries.shape[0]
    head = queries.shape[1] // heads
    block = rows // size
    whole = lambda h, s: (0, 0)
    table_specs = [pl.BlockSpec((rows, 128), whole)] * 4 + [pl.BlockSpec((8, rows), whole)]
    by_head = pl.BlockSpec((rows, head), lambda h, s: (0, h))
    wide = jax.ShapeDtypeStruct((rows, heads * head), BF16)
    return pl.pallas_call(
        functools.partial(backward_kernel, size=size, block=block),
        out_shape=(wide, wide, wide),
        grid_spec=pltpu.PrefetchScalarGridSpec(
            num_scalar_prefetch=1,
            grid=(heads,),
            in_specs=[by_head] * 4
            + [pl.BlockSpec((1, rows, 128), lambda h, s: (h, 0, 0))]
            + table_specs,
            out_specs=(by_head,) * 3,
            scratch_shapes=[pltpu.VMEM((rows, head), F32)] * 2,
        ),
        cost_estimate=pl.CostEstimate(
            flops=heads * rows * rows * head * 60, bytes_accessed=rows * head * heads * 24,
            transcendentals=heads * rows * rows // 2,
        ),
        name="attention_backward",
    )(me, queries, keys, values, grads, log_total, *tables)


def standardize(values):
    values = values.astype(F32)
    centered = values - jnp.mean(values, axis=-1, keepdims=True)
    spread = jnp.mean(centered * centered, axis=-1, keepdims=True)
    scale = lax.rsqrt(spread + EPSILON)
    return centered * scale, scale


def norm_rows(token_rows, gain_rows, shift_rows):
    xhat, _ = standardize(token_rows)
    first_rows = (xhat * gain_rows[0] + shift_rows[0]).astype(BF16)
    second_rows = (xhat * gain_rows[1] + shift_rows[1]).astype(BF16)
    return first_rows, second_rows


def hidden_units(second_rows, up_rows, hidden_bias):
    hidden = jnp.dot(second_rows, up_rows, preferred_element_type=F32) + hidden_bias
    bell = lax.erf(hidden * (0.5**0.5))
    activated = (0.5 * hidden * (1.0 + bell)).astype(BF16)
    slope = 0.5 * (1.0 + bell) + hidden * jnp.exp(-0.5 * hidden * hidden) * 0.3989422804014327
    return activated, slope.astype(BF16)


def branch_rows(attended, mix_rows, activated, down_rows):
    return (
        jnp.einsum("ne,de->nd", attended, mix_rows, preferred_element_type=F32)
        + jnp.einsum("nf,df->nd", activated, down_rows, preferred_element_type=F32)
    ).astype(BF16)


def hidden_grads(grad_rows, down_rows, slope):
    grad_active = jnp.einsum("nd,df->nf", grad_rows, down_rows, preferred_element_type=F32)
    return (grad_active * slope.astype(F32)).astype(BF16)


def attended_grads(grad_rows, mix_rows):
    return jnp.einsum("nd,de->ne", grad_rows, mix_rows, preferred_element_type=F32).astype(BF16)


def back_rows(grads, weight_rows):
    return jnp.einsum("nf,df->nd", grads, weight_rows, preferred_element_type=F32)


def grad_half(rows, columns, part):
    width = rows.shape[1] // 2
    chosen = rows[:, part * width : (part + 1) * width]
    return jnp.einsum("nd,nf->df", chosen, columns, preferred_element_type=F32).astype(BF16)


def plus(*terms):
    return functools.reduce(lambda a, b: a + b, [t.astype(F32) for t in terms])


def width_sums(grad_first, grad_second, xhat, grad_local):
    return jnp.stack(
        [
            jnp.sum(grad_first * xhat, axis=0),
            jnp.sum(grad_second * xhat, axis=0),
            jnp.sum(grad_first, axis=0),
            jnp.sum(grad_second, axis=0),
            jnp.sum(grad_local.astype(F32), axis=0),
        ],
        axis=0,
    )


def shards(
    tokens,
    seq_start,
    proj_weight,
    proj_bias,
    out_weight,
    up_weight,
    up_bias,
    down_weight,
    norm_gains,
    biases,
    cotangent,
):
    local_rows, width = tokens.shape
    n_dp, n_tensor = lax.axis_size("dp"), lax.axis_size("tensor")
    dp_index, tensor_index = lax.axis_index("dp"), lax.axis_index("tensor")
    row_count = local_rows * n_tensor
    hidden_width = up_weight.shape[1]
    heads_here = proj_bias.shape[1]
    head_size = proj_bias.shape[2] * n_dp
    local_width = heads_here * head_size
    joined_width = 3 * local_width
    columns = norm_gains.shape[1]

    vectors = jnp.concatenate(
        [norm_gains.reshape(1, -1), biases.reshape(1, -1), proj_bias.reshape(1, -1), up_bias.reshape(1, -1)],
        axis=1,
    )
    table = jnp.zeros((n_dp * n_tensor, vectors.shape[1]), BF16)
    table = lax.dynamic_update_slice(table, vectors, (dp_index * n_tensor + tensor_index, 0))
    local_tokens, local_grads = to_frame(tokens), to_frame(cotangent)
    positions = dp_index * row_count + jnp.arange(row_count, dtype=jnp.int32) - seq_start
    tables = attention_tables(positions, seq_start)
    me = tensor_index.astype(jnp.int32).reshape(1)
    flat_proj = proj_weight.reshape(-1, joined_width)

    def small_parameters(table):
        six_rows = table[:, : 6 * columns].reshape(n_dp * n_tensor, 6, columns).transpose(1, 0, 2)
        six_rows = to_frame(six_rows.reshape(6, width).astype(F32))
        of_tensor = lax.dynamic_index_in_dim(
            table[:, 6 * columns :].reshape(n_dp, n_tensor, -1), tensor_index, 1, keepdims=False
        ).astype(F32)
        joined_bias = (
            of_tensor[:, : proj_bias.size]
            .reshape(n_dp, 3, heads_here, -1)
            .transpose(1, 2, 0, 3)
            .reshape(joined_width)
        )
        hidden_bias = of_tensor[:, proj_bias.size :].reshape(hidden_width)
        return six_rows[:2], six_rows[2:], joined_bias, hidden_bias

    def attend(first_rows, joined_rows, joined_bias):
        projected = jnp.dot(first_rows, joined_rows, preferred_element_type=F32) + joined_bias
        return attention_forward(projected, tables, me, heads_here, n_tensor)

    def attend_back(kept, grad_attended):
        queries, keys, values, log_total = kept
        backs = attention_backward(
            queries, keys, values, grad_attended, log_total, tables, me, heads_here, n_tensor
        )
        return jnp.concatenate(backs, axis=1)

    def finish_output(branches, shift_rows):
        output = local_tokens.astype(F32) + branches + shift_rows[2] + shift_rows[3]
        return from_frame(output.astype(BF16))

    def finish_input_grad(back):
        xhat_local, scale_local = standardize(local_tokens)
        grad_norm_in = (
            back
            - jnp.mean(back, axis=-1, keepdims=True)
            - xhat_local * jnp.mean(back * xhat_local, axis=-1, keepdims=True)
        ) * scale_local
        return from_frame(local_grads.astype(F32) + grad_norm_in)

    def small_shares(five, joined_bias_sums, up_bias_sums):
        five = five.reshape(5, width)
        mine = lax.dynamic_slice_in_dim(
            five, (dp_index * n_tensor + tensor_index) * columns, columns, 1
        )
        biases_grad = jnp.concatenate([mine[2:], mine[4:]], axis=0)
        joined_bias_sum = lax.dynamic_slice_in_dim(
            joined_bias_sums.reshape(3, heads_here, head_size),
            dp_index * proj_bias.shape[2],
            proj_bias.shape[2],
            2,
        )
        up_bias_sum = lax.dynamic_slice_in_dim(
            up_bias_sums.reshape(1, -1), dp_index * up_bias.shape[1], up_bias.shape[1], 1
        )
        return mine[:2], biases_grad, joined_bias_sum, up_bias_sum

    def small_grads(five, joined_bias_term, up_bias_term):
        five = from_frame(five).reshape(1, -1)
        terms = jnp.concatenate([five, joined_bias_term[None], up_bias_term[None]], axis=1)
        terms = butterfly(terms, "dp")
        five = butterfly(terms[:, : 5 * width], "tensor")
        return small_shares(
            five, terms[0, 5 * width : 5 * width + joined_width], terms[:, 5 * width + joined_width :]
        )

    def plain():
        token_rows, grad_rows = line_gather(local_tokens), line_gather(local_grads)
        up_rows, down_rows = dp_gather(up_weight), dp_gather(down_weight.T)
        joined_rows, mix_rows = dp_gather(flat_proj), dp_gather(out_weight.T)
        up_rows, down_rows, joined_rows, mix_rows = (
            join(w, 0, None) for w in (up_rows, down_rows, joined_rows, mix_rows)
        )
        gain_rows, shift_rows, joined_bias, hidden_bias = small_parameters(
            butterfly(butterfly(table, "dp"), "tensor")
        )
        first_rows, second_rows = norm_rows(token_rows, gain_rows, shift_rows)
        activated, slope = cut(*hidden_units(second_rows, up_rows, hidden_bias))
        *kept, attended, log_total = attend(first_rows, joined_rows, joined_bias)
        branches = line_scatter(branch_rows(attended, mix_rows, activated, down_rows))
        output = finish_output(branches, shift_rows)
        grad_hidden = hidden_grads(grad_rows, down_rows, slope)
        down_sum = weight_grad(grad_rows, activated)
        up_sum = weight_grad(second_rows, grad_hidden)
        grad_second = back_rows(grad_hidden, up_rows)
        grad_attended = attended_grads(grad_rows, mix_rows)
        mix_sum = weight_grad(grad_rows, attended)
        grad_projected = attend_back((*kept, log_total), grad_attended)
        joined_sum = weight_grad(first_rows, grad_projected)
        grad_first = back_rows(grad_projected, joined_rows)
        back = grad_first * gain_rows[0] + grad_second * gain_rows[1]
        input_grad = finish_input_grad(line_scatter(back.astype(BF16)))
        five = width_sums(grad_first, grad_second, standardize(token_rows)[0], local_grads)
        small = small_grads(
            five, jnp.sum(grad_projected, axis=0, dtype=F32), jnp.sum(grad_hidden, axis=0, dtype=F32)
        )
        return output, input_grad, joined_sum, mix_sum.T, up_sum, down_sum.T, small

    def staged():
        half = local_rows // 2
        first, second = slice(0, half), slice(half, 2 * half)

        def x(values):
            return xor_shift(values, "dp", 2)

        def y(values):
            return xor_shift(values, "dp", 4)

        def core(values):
            return xor_shift(values, "dp", 1)

        def gather_step(up, down, s):
            up = lax.ppermute(up, "tensor", [(i, i + 1) for i in range(s, 3)])
            down = lax.ppermute(down, "tensor", [(i + 1, i) for i in range(3 - s)])
            return up, down

        def scatter_terms(halves, up, down, s):
            came = () if s == 1 else (up, down)
            return step_terms(halves, 4 - s, s, local_rows, width // 2, *came)

        def scatter_step(to_up, to_down, s):
            up = lax.ppermute(to_up, "tensor", [(i, i + 1) for i in range(s)])
            down = lax.ppermute(to_down, "tensor", [(i, i - 1) for i in range(4 - s, 4)])
            return up, down

        def in_turn(block, ups, downs):
            blocks = [block] + [
                jnp.where(tensor_index + r < 4, downs[r - 1], ups[3 - r]) for r in range(1, 4)
            ]
            return jnp.concatenate(blocks, axis=0)

        def pair(top, low):
            return jnp.concatenate([top, low], axis=0)

        def place(base, piece, part):
            return lax.dynamic_update_slice(base, piece, ((4 * part + 2) * local_rows, 0))

        def at(keep, came, start, stop):
            return plus(keep[start * half : stop * half], came[start * half : stop * half])

        def joined_half(first_rows, grad_projected, grad_rows, attended, part):
            return jnp.concatenate(
                [grad_half(first_rows, grad_projected, part), grad_half(grad_rows, attended, part)], axis=1
            )

        wa = up_weight
        wb = jnp.concatenate([flat_proj, out_weight.T], axis=1)
        wc = down_weight.T

        ax, ay = x(wa), y(wa)
        tu1, td1 = gather_step(local_tokens, local_tokens, 0)
        table1 = table + core(table)
        table1, ax, ay = cut(table1, ax, ay)
        table1 = table1 + x(table1) + y(table1) + xor_shift(table1, "dp", 6)
        tu1, td1, ax, ay, table1, wb, wc, tables1 = cut(tu1, td1, ax, ay, table1, wb, wc, tables)
        tu2, td2 = gather_step(tu1, td1, 1)
        bx, by = x(wb), y(wb)
        table2 = table1 + xor_shift(table1, "tensor", 1)
        tu2, td2, bx, by, table2, local_grads1 = cut(tu2, td2, bx, by, table2, local_grads)
        tu3, td3 = gather_step(tu2, td2, 2)
        fa, fb = x(ay), y(bx)
        table3 = table2 + xor_shift(table2, "tensor", 2)
        both = lay(wa, ax, ay, wb, bx, by)
        tu3, td3, fa, fb, table3, both = cut(tu3, td3, fa, fb, table3, both)
        both_1 = place(place(both, fa, 0), fb, 1)
        both_1, wc, local_grads1 = cut(both_1, wc, local_grads1)
        cu1, cd1 = gather_step(local_grads1, local_grads1, 0)
        cx, cy = x(wc), y(wc)
        both_2 = core(both_1)
        gain_rows, shift_rows, joined_bias, hidden_bias = small_parameters(table3)
        token_rows = in_turn(local_tokens, (tu1, tu2, tu3), (td1, td2, td3))
        first_rows, second_rows = norm_rows(token_rows, gain_rows, shift_rows)
        mean = jnp.mean(token_rows.astype(F32), axis=-1, keepdims=True)
        _, scale = standardize(token_rows)
        mean, scale = (jnp.broadcast_to(v, (row_count, 128)) for v in (mean, scale))
        activated, slope = hidden_half(second_rows, both_1, both_2, hidden_bias)
        cu1, cd1, cx, cy, both_1, both_2, first_rows, activated, slope = cut(
            cu1, cd1, cx, cy, both_1, both_2, first_rows, activated, slope
        )
        cu2, cd2 = gather_step(cu1, cd1, 1)
        fc = x(cy)
        down_0 = lay(wc, cx, cy)
        *kept, attended, log_total = joined_forward(
            first_rows, both_1, both_2, joined_bias.reshape(1, -1), tables1, me, heads_here, head_size, n_tensor
        )
        cu2, cd2, fc, attended, down_0, mean, scale = cut(cu2, cd2, fc, attended, down_0, mean, scale)
        cu3, cd3 = gather_step(cu2, cd2, 2)
        down_1 = place(down_0, fc, 0)
        down_2 = core(down_1)
        branch_1 = branch_half(attended, both_1, activated, down_1)
        branch_2 = branch_half(attended, both_2, activated, down_2)
        cu3, cd3, branch_1, branch_2, activated = cut(cu3, cd3, branch_1, branch_2, activated)
        branches = ((branch_1, 0), (branch_2, 0))
        zu, zd, activated, cu3, cd3 = cut(*scatter_terms(branches, None, None, 1), activated, cu3, cd3)
        bu, bd = scatter_step(zu, zd, 1)
        grad_rows = in_turn(local_grads1, (cu1, cu2, cu3), (cd1, cd2, cd3))
        came_d = core(grad_half(grad_rows, activated, 1))
        keep_d = grad_half(grad_rows, activated, 0)
        grad_hidden, up_bias_term = hidden_back(grad_rows, down_1, down_2, slope)
        bu, bd, came_d, keep_d, grad_hidden, grad_rows = cut(
            bu, bd, came_d, keep_d, grad_hidden, grad_rows
        )
        zu, zd, sx, sy, second_rows, grad_hidden, grad_rows = cut(
            *scatter_terms(branches, bu, bd, 2),
            *pair_sums(keep_d, came_d, half),
            second_rows, grad_hidden, grad_rows,
        )
        bu, bd = scatter_step(zu, zd, 2)
        d1x, d1y = x(sx), y(sy)
        came_u = core(grad_half(second_rows, grad_hidden, 1))
        keep_u = grad_half(second_rows, grad_hidden, 0)
        grad_projected = mixed_backward(
            *kept, grad_rows, both_1, both_2, log_total, tables1, me, heads_here, n_tensor
        )
        bu, bd, d1x, d1y, came_u, keep_u, grad_projected, grad_hidden = cut(
            bu, bd, d1x, d1y, came_u, keep_u, grad_projected, grad_hidden
        )
        d2x = plus(at(keep_d, came_d, 2, 3), d1y[first]).astype(BF16)
        d2y = plus(at(keep_d, came_d, 7, 8), d1x[second]).astype(BF16)
        zu, zd, sx, sy, grad_hidden, grad_projected = cut(
            *scatter_terms(branches, bu, bd, 3),
            pair(d2x, at(keep_u, came_u, 4, 5).astype(BF16)),
            pair(d2y, at(keep_u, came_u, 5, 6).astype(BF16)),
            grad_hidden, grad_projected,
        )
        bu, bd = scatter_step(zu, zd, 3)
        s9x, s9y = x(sx), y(sy)
        came_j = core(joined_half(first_rows, grad_projected, grad_rows, attended, 1))
        back, sums = back_whole(
            grad_hidden, grad_projected, both_1, both_2, token_rows, mean, scale, gain_rows
        )
        bu, bd, s9x, s9y, came_j, back, sums, grad_projected, attended = cut(
            bu, bd, s9x, s9y, came_j, back, sums, grad_projected, attended
        )
        backs = ((back, 0), (back, 1))
        none = jnp.zeros((half, s9x.shape[1]), BF16)
        zu, zd, sx, sy, first_rows, grad_rows, bu, bd, sums = cut(
            *scatter_terms(backs, None, None, 1),
            plus(at(keep_u, came_u, 2, 4), pair(s9y[second], none)).astype(BF16),
            plus(at(keep_u, came_u, 6, 8), pair(none, s9x[second])).astype(BF16),
            first_rows, grad_rows, bu, bd, sums,
        )
        eu, ed = scatter_step(zu, zd, 1)
        s10x, s10y = x(sx), y(sy)
        keep_j = joined_half(first_rows, grad_projected, grad_rows, attended, 0)
        five = jnp.concatenate(
            [
                sums[:4],
                jnp.sum(local_grads.astype(F32), axis=0, keepdims=True),
            ],
            axis=0,
        )
        sx, sy = pair_sums(keep_j, came_j, half)
        five = five.reshape(1, -1)
        five = five + xor_shift(five, "tensor", 1)
        five = from_frame(five.reshape(5, width)).reshape(1, -1)
        eu, ed, s10x, s10y, keep_j, five, bu, bd, sx, sy = cut(
            eu, ed, s10x, s10y, keep_j, five, bu, bd, sx, sy
        )
        zu, zd, sx, sy, s10x, s10y, five = cut(
            *scatter_terms(backs, eu, ed, 2), sx, sy, s10x, s10y, five
        )
        eu, ed = scatter_step(zu, zd, 2)
        j1x, j1y = x(sx), y(sy)
        five = five + xor_shift(five, "tensor", 2)
        down_sum = own_sums(keep_d, came_d, half, (d1x, 0), (s9y, 0), (d1y, 1), (s9x, 0)).T
        up_sum = own_sums(keep_u, came_u, half, (s10x, 1), (s10y, 1), (s10x, 0), (s10y, 0))
        terms = jnp.concatenate(
            [
                jnp.sum(grad_projected, axis=0, dtype=F32, keepdims=True),
                up_bias_term,
            ],
            axis=1,
        )
        eu, ed, j1x, j1y, five, terms, down_sum, up_sum, bu, bd = cut(
            eu, ed, j1x, j1y, five, terms, down_sum, up_sum, bu, bd
        )
        zu, zd, sx, sy, five, bu, bd = cut(
            *scatter_terms(backs, eu, ed, 3),
            plus(at(keep_j, came_j, 2, 3), j1y[first]).astype(BF16),
            plus(at(keep_j, came_j, 7, 8), j1x[second]).astype(BF16),
            five, bu, bd,
        )
        eu, ed = scatter_step(zu, zd, 3)
        j2x, j2y = x(sx), y(sy)
        own = jnp.concatenate([branch_1[:local_rows], branch_2[:local_rows]], axis=1)
        output = finish_output(plus(own, bu, bd), shift_rows)
        terms = jnp.concatenate([five, terms], axis=1)
        terms = terms + core(terms)
        terms = terms + x(terms)
        terms, j2x, j2y = cut(terms, j2x, j2y)
        terms = terms + y(terms)
        small = small_shares(
            terms[:, : 5 * width], terms[0, 5 * width : 5 * width + joined_width],
            terms[:, 5 * width + joined_width :],
        )
        joined_mix = own_sums(keep_j, came_j, half, (j1x, 0), (j2y, 0), (j1y, 1), (j2x, 0))
        joined_sum = joined_mix[:, :joined_width].reshape(proj_weight.shape)
        eu, ed, joined_sum, mix_sum = cut(eu, ed, joined_sum, joined_mix[:, joined_width:].T)
        input_grad = input_grad_rows(back, eu, ed, local_tokens, local_grads)
        return output, input_grad, joined_sum, mix_sum, up_sum, down_sum, small

    parts = staged() if fast_dp() and n_tensor == 4 else plain()
    output, input_grad, joined_sum, mix_sum, up_sum, down_sum, small = parts
    gains_grad, biases_grad, joined_bias_sum, up_bias_sum = small
    return (
        output,
        input_grad,
        joined_sum.reshape(proj_weight.shape),
        joined_bias_sum,
        mix_sum,
        up_sum,
        up_bias_sum,
        down_sum,
        gains_grad,
        biases_grad,
    )


def solution(mesh):
    in_specs = (
        P(("dp", "tensor"), None),
        P("dp"),
        P("dp", None, "tensor"),
        P(None, "tensor", "dp"),
        P("tensor", "dp"),
        P("dp", "tensor"),
        P("tensor", "dp"),
        P("tensor", "dp"),
        P(None, ("dp", "tensor")),
        P(None, ("dp", "tensor")),
        P(("dp", "tensor"), None),
    )
    out_specs = (
        P(("dp", "tensor"), None),
        P(("dp", "tensor"), None),
        P("dp", None, "tensor"),
        P(None, "tensor", "dp"),
        P("tensor", "dp"),
        P("dp", "tensor"),
        P("tensor", "dp"),
        P("tensor", "dp"),
        P(None, ("dp", "tensor")),
        P(None, ("dp", "tensor")),
    )
    return jax.shard_map(shards, mesh=mesh, in_specs=in_specs, out_specs=out_specs, check_vma=False)
```
